128 devices in a mesh: dp: 8 (over y_lo, x), zero: 16 (over z, y_hi, core).
Axes of the slice: x: 4, y: 4 (y_hi: 2, y_lo: 2; y = y_hi * 2 + y_lo), z: 4, core: 2. Of those that a mesh axis runs over, the one named last changes fastest.
Arguments:
- tokens: bfloat16 [16384, 1024], P(('dp', 'zero')), may hold values from -24 to 24
- cotangent: bfloat16 [16384, 1024], P(('dp', 'zero')), may hold values from -6 to 6
- segments: int32 [128, 128], P(('dp', 'zero')), may hold values from 0 to 3, never falling along the last dimension, each value on 1 to 64 neighbouring positions
- w_qkv: float32 [1024, 3072], P('zero'), may hold values from -0.1875 to 0.1875
- w_out: float32 [1024, 1024], P('zero'), may hold values from -0.75 to 0.75
- w_fc: float32 [1024, 4096], P('zero'), may hold values from -0.1875 to 0.1875
- w_proj: float32 [4096, 1024], P('zero'), may hold values from -0.09375 to 0.09375
- vectors: float32 [12, 1024], P(None, 'zero'), may hold values from -1.2 to 1.6, as said below
- mean_qkv: float32 [1024, 3072], P('zero'), may hold values from -0.6 to 0.6
- mean_out: float32 [1024, 1024], P('zero'), may hold values from -0.6 to 0.6
- mean_fc: float32 [1024, 4096], P('zero'), may hold values from -0.6 to 0.6
- mean_proj: float32 [4096, 1024], P('zero'), may hold values from -0.6 to 0.6
- mean_vectors: float32 [12, 1024], P(None, 'zero'), may hold values from -0.6 to 0.6
- square_qkv: float32 [1024, 3072], P('zero'), may hold values from 1e-05 to 0.001
- square_out: float32 [1024, 1024], P('zero'), may hold values from 1e-05 to 0.001
- square_fc: float32 [1024, 4096], P('zero'), may hold values from 1e-05 to 0.001
- square_proj: float32 [4096, 1024], P('zero'), may hold values from 1e-05 to 0.001
- square_vectors: float32 [12, 1024], P(None, 'zero'), may hold values from 1e-05 to 0.001
Outputs:
- block_out: bfloat16 [16384, 1024], P(('dp', 'zero'))
- input_grad: bfloat16 [16384, 1024], P(('dp', 'zero'))
- grad_qkv: float32 [1024, 3072], P('zero')
- grad_out: float32 [1024, 1024], P('zero')
- grad_fc: float32 [1024, 4096], P('zero')
- grad_proj: float32 [4096, 1024], P('zero')
- grad_vectors: float32 [12, 1024], P(None, 'zero')
- next_qkv: float32 [1024, 3072], P('zero')
- next_out: float32 [1024, 1024], P('zero')
- next_fc: float32 [1024, 4096], P('zero')
- next_proj: float32 [4096, 1024], P('zero')
- next_vectors: float32 [12, 1024], P(None, 'zero')
- next_mean_qkv: float32 [1024, 3072], P('zero')
- next_mean_out: float32 [1024, 1024], P('zero')
- next_mean_fc: float32 [1024, 4096], P('zero')
- next_mean_proj: float32 [4096, 1024], P('zero')
- next_mean_vectors: float32 [12, 1024], P(None, 'zero')
- next_square_qkv: float32 [1024, 3072], P('zero')
- next_square_out: float32 [1024, 1024], P('zero')
- next_square_fc: float32 [1024, 4096], P('zero')
- next_square_proj: float32 [4096, 1024], P('zero')
- next_square_vectors: float32 [12, 1024], P(None, 'zero')
The draws below stay inside these ranges and needn't reach their ends.
Inputs may be any that keep to these rules, and one draw needn't show every extreme that they name: `segments`: in each row of 128 tokens the segment numbers never fall; each of the 4 documents of a row has 1 to 64 tokens, and one has exactly 64. `vectors`: rows 0 and 5 lie within 0.4 to 1.6; the other rows within -1.2 to 1.2.
All inputs are finite; a program needn't handle non-finite values.
Results may differ from the reference program's by a relative error of at most 0.04.
Values may be sent and summed in bfloat16 or wider, within the bound.
A program may use at most 192 MiB of HBM per device.

```python
import math
from functools import partial
import jax
import jax.numpy as jnp
import numpy as np
from jax import lax

D = 1024
HEADS = 16
FF = 4096
SEQ = 128
SEGMENTS = 4
SEG_MOST = 64
ADAM_STEP = 3
NVEC = 12
TOKENS = 16384
ROWS = 128
N_DP = 8
N_ZERO = 16


def draw_vectors(key, part):
    row_index = jnp.arange(NVEC)[:, None]
    is_gain = jnp.logical_or(row_index == 0, row_index == 5)
    random_part = jnp.clip(jax.random.normal(key, (NVEC, D), jnp.float32), -4.0, 4.0)
    gain_rows = 1.0 + 0.15 * random_part
    biases = 0.3 * random_part
    return jnp.where(is_gain, gain_rows, biases).astype(jnp.float32)


def spiked(result, own_key, source, target, parts, factor):
    def block_of(position):
        return (jnp.arange(result.shape[position]) // (result.shape[position] // parts)).reshape((-1,) + (1,) * (result.ndim - 1 - position))

    first = jax.random.permutation(own_key, parts)[block_of(target)]
    second = (block_of(target) + parts // 2) % parts
    return jnp.where((block_of(source) == first) | (block_of(source) == second), factor * result, result)


def steps_of(key, extent, pieces, least, high):
    level = 1.0
    for axis_at, shards_of in pieces:
        steps = jax.random.uniform(jax.random.fold_in(jax.random.fold_in(key, 6), axis_at), (shards_of,), jnp.float32, least / len(pieces), high / len(pieces))
        level = level * jnp.repeat(jnp.exp(steps), extent[axis_at] // shards_of).reshape((-1,) + (1,) * (len(extent) - 1 - axis_at))
    return level


def profile(amount, total, limit, slope):
    portions = [(1 << 20) // math.isqrt(grade ** slope) + 1 for grade in range(2, amount + 1)]
    spare, counts = total - limit - (amount - 1), [1] * (amount - 1)
    while spare > 0:
        movable = [i for i in range(amount - 1) if counts[i] < limit]
        whole, budget = sum([portions[i] for i in movable]), spare
        for i in movable:
            more = min(limit - counts[i], max(1, budget * portions[i] // whole), spare)
            counts[i] = counts[i] + more
            spare = spare - more
    return np.array([limit] + counts)


def ragged(key, amount, total, limit, slope):
    if amount == 2:
        one = jax.random.randint(key, (), max(1, total - limit), min(limit, total - 1) + 1)
        return jnp.stack([one, total - one])
    tallies = jnp.asarray(profile(amount, total, limit, slope), jnp.int32)
    couples = (amount - 1) // 2
    donor, sink = tallies[1:1 + 2 * couples:2], tallies[2:2 + 2 * couples:2]
    margin = jnp.minimum(donor - 1, limit - sink)
    passed = jax.random.randint(jax.random.fold_in(key, 1), (couples,), 0, 1 << 20) % (margin + 1)
    tallies = tallies.at[1:1 + 2 * couples:2].set(donor - passed).at[2:2 + 2 * couples:2].set(sink + passed)
    return tallies[jax.random.permutation(jax.random.fold_in(key, 2), amount)]


def gaussian(rng, dims, scale, bound, split=(), kind=jnp.bfloat16):
    result = scale * jax.random.normal(rng, dims, jnp.float32)
    if split:
        result = result * steps_of(rng, dims, split, -0.22, 0.18)
    return jnp.clip(result, -bound, bound).astype(kind)


def noise_with(key, shape, deviation, most, split, heavy, kind=jnp.bfloat16):
    values = deviation * jax.random.normal(key, shape, jnp.float32)
    if split:
        values = values * steps_of(key, shape, split, -0.22, 0.18)
    return jnp.clip(spiked(values, jax.random.fold_in(key, 3), *heavy), -most, most).astype(kind)


def setup_inputs(seed: int = 0) -> dict:
    streams_of = jax.random.split(jax.random.key(seed), 19)
    tokens = noise_with(streams_of[0], (TOKENS, D), 1.0, 24.0, ((0, 128),), (0, 1, 128, 5.5))
    cotangent = gaussian(streams_of[1], (TOKENS, D), 1.0, 6.0, ((0, 128),))
    segments = jax.vmap(lambda own: jnp.searchsorted(jnp.cumsum(ragged(own, SEGMENTS, SEQ, SEG_MOST, 0)), jnp.arange(SEQ), side="right"))(jax.random.split(streams_of[2], ROWS)).reshape((ROWS, SEQ)).astype(jnp.int32)
    w_qkv = gaussian(streams_of[3], (D, 3 * D), D ** -0.5, 0.1875, ((0, 16),), jnp.float32)
    w_out = gaussian(streams_of[4], (D, D), (D // 16) ** -0.5, 0.75, ((0, 16),), jnp.float32)
    w_fc = gaussian(streams_of[5], (D, FF), D ** -0.5, 0.1875, ((0, 16),), jnp.float32)
    w_proj = gaussian(streams_of[6], (FF, D), FF ** -0.5, 0.09375, ((0, 16),), jnp.float32)
    vectors = draw_vectors(jax.random.fold_in(streams_of[18], 71), 0)
    mean_qkv = gaussian(streams_of[8], (D, 3 * D), 0.1, 0.6, ((0, 16),), jnp.float32)
    mean_out = gaussian(streams_of[9], (D, D), 0.1, 0.6, ((0, 16),), jnp.float32)
    mean_fc = gaussian(streams_of[10], (D, FF), 0.1, 0.6, ((0, 16),), jnp.float32)
    mean_proj = gaussian(streams_of[11], (FF, D), 0.1, 0.6, ((0, 16),), jnp.float32)
    mean_vectors = gaussian(streams_of[12], (NVEC, D), 0.1, 0.6, ((1, 16),), jnp.float32)
    square_qkv = jnp.clip(jnp.exp(math.log(0.001) - 4.6051703 * jax.random.uniform(streams_of[13], (D, 3 * D), jnp.float32) ** steps_of(streams_of[13], (D, 3 * D), ((0, 16),), -0.2, 0.2)), 9.999999747378752e-06, 0.001)
    square_out = jnp.clip(jnp.exp(math.log(0.001) - 4.6051703 * jax.random.uniform(streams_of[14], (D, D), jnp.float32) ** steps_of(streams_of[14], (D, D), ((0, 16),), -0.2, 0.2)), 9.999999747378752e-06, 0.001)
    square_fc = jnp.clip(jnp.exp(math.log(0.001) - 4.6051703 * jax.random.uniform(streams_of[15], (D, FF), jnp.float32) ** steps_of(streams_of[15], (D, FF), ((0, 16),), -0.2, 0.2)), 9.999999747378752e-06, 0.001)
    square_proj = jnp.clip(jnp.exp(math.log(0.001) - 4.6051703 * jax.random.uniform(streams_of[16], (FF, D), jnp.float32) ** steps_of(streams_of[16], (FF, D), ((0, 16),), -0.2, 0.2)), 9.999999747378752e-06, 0.001)
    square_vectors = jnp.clip(jnp.exp(math.log(0.001) - 4.6051703 * jax.random.uniform(streams_of[17], (NVEC, D), jnp.float32) ** steps_of(streams_of[17], (NVEC, D), ((1, 16),), -0.2, 0.2)), 9.999999747378752e-06, 0.001)
    return dict(tokens=tokens, cotangent=cotangent, segments=segments, w_qkv=w_qkv, w_out=w_out, w_fc=w_fc, w_proj=w_proj, vectors=vectors, mean_qkv=mean_qkv, mean_out=mean_out, mean_fc=mean_fc, mean_proj=mean_proj, mean_vectors=mean_vectors, square_qkv=square_qkv, square_out=square_out, square_fc=square_fc, square_proj=square_proj, square_vectors=square_vectors)


eps_norm = 1e-05
beta_first = 0.9
beta_second = 0.999
eps_adam = 1e-08
rate_matrix = 0.02
rate_vector = 0.15
decay_matrix = 0.1

def gelu_tanh(inputs):
    inner = 0.7978845608028654 * (inputs + 0.044715 * inputs * inputs * inputs)
    return 0.5 * inputs * (1.0 + jnp.tanh(inner))

def layer_norm(inputs, gain_row, bias_row):
    average = lax.optimization_barrier(jnp.mean(inputs, axis=-1, keepdims=True))
    centred = inputs - average
    variance = lax.optimization_barrier(jnp.mean(centred * centred, axis=-1, keepdims=True))
    return centred * lax.rsqrt(variance + eps_norm) * gain_row + bias_row

def allowed_mask(seg_rows):
    length = seg_rows.shape[1]
    places = jnp.arange(length, dtype=jnp.int32)
    causal = places[:, None] >= places[None, :]
    same_doc = seg_rows[:, :, None] == seg_rows[:, None, :]
    return jnp.logical_and(same_doc, causal[None])[:, None]

def attend_scores(queries, keys_in, seg_rows):
    scaling = queries.shape[-1] ** (-0.5)
    scores = jnp.einsum('rqhe,rkhe->rhqk', queries.astype(jnp.float32), keys_in.astype(jnp.float32)) * scaling
    return (scores, allowed_mask(seg_rows), scaling)

def attention_forward(queries, keys_in, values, seg_rows):
    scores, allowed, scaling = attend_scores(queries, keys_in, seg_rows)
    exponent = jnp.where(allowed, jnp.exp(scores), 0.0)
    log_total = jnp.log(lax.optimization_barrier(jnp.sum(exponent, axis=-1, keepdims=True)))
    attn_weights = jnp.where(allowed, jnp.exp(scores - log_total), 0.0).astype(jnp.bfloat16)
    attended = jnp.einsum('rhqk,rkhe->rqhe', attn_weights.astype(jnp.float32), values.astype(jnp.float32))
    return (attended.astype(jnp.bfloat16), log_total)

def attention_backward(queries, keys_in, values, seg_rows, log_total, grad_att):
    scores, allowed, scaling = attend_scores(queries, keys_in, seg_rows)
    weights_full = jnp.where(allowed, jnp.exp(scores - log_total), 0.0)
    weights_half = weights_full.astype(jnp.bfloat16)
    grad_values = jnp.einsum('rhqk,rqhe->rkhe', weights_half.astype(jnp.float32), grad_att.astype(jnp.float32))
    grad_weights = jnp.einsum('rqhe,rkhe->rhqk', grad_att.astype(jnp.float32), values.astype(jnp.float32))
    row_dot = lax.optimization_barrier(jnp.sum(weights_full * grad_weights, axis=-1, keepdims=True))
    grad_scores = (weights_full * (grad_weights - row_dot) * scaling).astype(jnp.bfloat16)
    grad_queries = jnp.einsum('rhqk,rkhe->rqhe', grad_scores.astype(jnp.float32), keys_in.astype(jnp.float32))
    grad_keys = jnp.einsum('rhqk,rqhe->rkhe', grad_scores.astype(jnp.float32), queries.astype(jnp.float32))
    return (grad_queries, grad_keys, grad_values)

def block_pass(tokens_in, cot_in, seg_rows, qkv_mat, out_mat, fc_mat, proj_mat, vec_rows):
    count_tok = tokens_in.shape[0]
    width = tokens_in.shape[1]
    head_width = width // HEADS
    row_count = count_tok // SEQ
    split_shape = (row_count, SEQ, HEADS, head_width)
    tokens32 = tokens_in.astype(jnp.float32)
    normed_one = layer_norm(tokens32, vec_rows[0], vec_rows[1]).astype(jnp.bfloat16)
    projected = jnp.dot(normed_one, qkv_mat, preferred_element_type=jnp.float32)
    queries = (projected[:, :width] + vec_rows[2]).astype(jnp.bfloat16).reshape(split_shape)
    keys_in = projected[:, width:2 * width].astype(jnp.bfloat16).reshape(split_shape)
    values = (projected[:, 2 * width:] + vec_rows[3]).astype(jnp.bfloat16).reshape(split_shape)
    attended, log_total = attention_forward(queries, keys_in, values, seg_rows)
    attended = attended.reshape(count_tok, width)
    middle = tokens32 + jnp.dot(attended, out_mat, preferred_element_type=jnp.float32) + vec_rows[4]
    normed_two = layer_norm(middle, vec_rows[5], vec_rows[6]).astype(jnp.bfloat16)
    fc_bias = vec_rows[8:].reshape(-1)
    hidden_pre = jnp.dot(normed_two, fc_mat, preferred_element_type=jnp.float32) + fc_bias
    hidden = gelu_tanh(hidden_pre).astype(jnp.bfloat16)
    block_out = (middle + jnp.dot(hidden, proj_mat, preferred_element_type=jnp.float32) + vec_rows[7]).astype(jnp.bfloat16)
    cot32 = cot_in.astype(jnp.float32)
    grad_proj = jnp.dot(hidden.T, cot_in, preferred_element_type=jnp.float32)
    grad_hidden = jnp.dot(cot_in, proj_mat.T, preferred_element_type=jnp.float32)
    gelu_back = jax.vjp(gelu_tanh, hidden_pre)[1]
    grad_pre = gelu_back(grad_hidden)[0]
    grad_pre_half = grad_pre.astype(jnp.bfloat16)
    grad_fc = jnp.dot(normed_two.T, grad_pre_half, preferred_element_type=jnp.float32)
    grad_normed_two = jnp.dot(grad_pre_half, fc_mat.T, preferred_element_type=jnp.float32)
    norm_two_back = jax.vjp(layer_norm, middle, vec_rows[5], vec_rows[6])[1]
    grad_mid_norm, grad_gain_two, grad_bias_two = norm_two_back(grad_normed_two)
    grad_middle = cot32 + grad_mid_norm
    grad_middle_half = grad_middle.astype(jnp.bfloat16)
    grad_out = jnp.dot(attended.T, grad_middle_half, preferred_element_type=jnp.float32)
    grad_attended = jnp.dot(grad_middle_half, out_mat.T, preferred_element_type=jnp.float32)
    grad_attended = grad_attended.astype(jnp.bfloat16).reshape(split_shape)
    grad_queries, grad_keys, grad_values = attention_backward(queries, keys_in, values, seg_rows, log_total, grad_attended)
    flat_queries = grad_queries.reshape(count_tok, width)
    flat_keys = grad_keys.reshape(count_tok, width)
    flat_values = grad_values.reshape(count_tok, width)
    grad_projected = jnp.concatenate([flat_queries, flat_keys, flat_values], axis=1).astype(jnp.bfloat16)
    grad_qkv = jnp.dot(normed_one.T, grad_projected, preferred_element_type=jnp.float32)
    grad_normed_one = jnp.dot(grad_projected, qkv_mat.T, preferred_element_type=jnp.float32)
    norm_one_back = jax.vjp(layer_norm, tokens32, vec_rows[0], vec_rows[1])[1]
    grad_tok_norm, grad_gain_one, grad_bias_one = norm_one_back(grad_normed_one)
    input_grad = (grad_middle + grad_tok_norm).astype(jnp.bfloat16)
    small_rows = jnp.stack([grad_gain_one, grad_bias_one, lax.optimization_barrier(jnp.sum(flat_queries, axis=0)), lax.optimization_barrier(jnp.sum(flat_values, axis=0)), lax.optimization_barrier(jnp.sum(grad_middle, axis=0)), grad_gain_two, grad_bias_two, lax.optimization_barrier(jnp.sum(cot32, axis=0))])
    grad_vec = jnp.concatenate([small_rows, lax.optimization_barrier(jnp.sum(grad_pre, axis=0)).reshape(-1, width)], axis=0)
    return (block_out, input_grad, (grad_qkv, grad_out, grad_fc, grad_proj, grad_vec))

def adam_step(weight, gradient, mean_old, square_old, rate, decay):
    mean_new = beta_first * mean_old + (1.0 - beta_first) * gradient
    square_new = beta_second * square_old + (1.0 - beta_second) * gradient * gradient
    mean_hat = mean_new / (1.0 - beta_first ** ADAM_STEP)
    square_hat = square_new / (1.0 - beta_second ** ADAM_STEP)
    weight_new = weight - rate * (mean_hat / (jnp.sqrt(square_hat) + eps_adam) + decay * weight)
    return (weight_new, mean_new, square_new)

def reference(tokens, cotangent, segments, w_qkv, w_out, w_fc, w_proj, vectors, mean_qkv, mean_out, mean_fc, mean_proj, mean_vectors, square_qkv, square_out, square_fc, square_proj, square_vectors):
    replicas = N_DP * N_ZERO
    qkv_mat = w_qkv.astype(jnp.bfloat16)
    out_mat = w_out.astype(jnp.bfloat16)
    fc_mat = w_fc.astype(jnp.bfloat16)
    proj_mat = w_proj.astype(jnp.bfloat16)
    vec_rows = lax.optimization_barrier(vectors.astype(jnp.bfloat16)).astype(jnp.float32)
    row_total = TOKENS // SEQ
    per_block = math.gcd(row_total, max(1, 4096 // SEQ))
    count_blocks = row_total // per_block
    tok_blocks = tokens.reshape(count_blocks, per_block * SEQ, D)
    cot_blocks = cotangent.reshape(count_blocks, per_block * SEQ, D)
    seg_blocks = segments.reshape(count_blocks, per_block, SEQ)
    start_sums = (jnp.zeros((D, 3 * D), jnp.float32), jnp.zeros((D, D), jnp.float32), jnp.zeros((D, FF), jnp.float32), jnp.zeros((FF, D), jnp.float32), jnp.zeros((NVEC, D), jnp.float32))

    def scan_step(carry, block_in):
        tok_blk, cot_blk, seg_blk = block_in
        out_blk, back_blk, grads_blk = block_pass(tok_blk, cot_blk, seg_blk, qkv_mat, out_mat, fc_mat, proj_mat, vec_rows)
        return (jax.tree.map(jnp.add, carry, grads_blk), (out_blk, back_blk))
    sums, stacked = lax.scan(scan_step, start_sums, (tok_blocks, cot_blocks, seg_blocks))
    block_out = stacked[0].reshape(TOKENS, D)
    input_grad = stacked[1].reshape(TOKENS, D)
    grads = jax.tree.map(partial(jnp.multiply, 1.0 / replicas), sums)
    first = adam_step(w_qkv, grads[0], mean_qkv, square_qkv, rate_matrix, decay_matrix)
    second = adam_step(w_out, grads[1], mean_out, square_out, rate_matrix, decay_matrix)
    third = adam_step(w_fc, grads[2], mean_fc, square_fc, rate_matrix, decay_matrix)
    fourth = adam_step(w_proj, grads[3], mean_proj, square_proj, rate_matrix, decay_matrix)
    fifth = adam_step(vectors, grads[4], mean_vectors, square_vectors, rate_vector, 0.0)
    return (block_out, input_grad, grads[0], grads[1], grads[2], grads[3], grads[4], first[0], second[0], third[0], fourth[0], fifth[0], first[1], second[1], third[1], fourth[1], fifth[1], first[2], second[2], third[2], fourth[2], fifth[2])
```

```python
from functools import partial

import jax
import jax.numpy as jnp
from jax import lax
from jax.sharding import PartitionSpec as P

HEADS = 16
SEQ = 128
ADAM_STEP = 3
LANE = 128


eps_norm = 1e-05
beta_first = 0.9
beta_second = 0.999
eps_adam = 1e-08
rate_matrix = 0.02
rate_vector = 0.15
decay_matrix = 0.1


def sent_together(arrays, axis, dim, along):
    widths = [a.shape[along] for a in arrays]
    both = jnp.concatenate(arrays, axis=along)
    result = lax.all_gather(both, axis, axis=dim, tiled=True)
    return tuple(jnp.split(result, [sum(widths[:k]) for k in range(1, len(widths))], axis=along))


def in_one_piece(arrays, axis, dim, along):
    ends, at = ([], 0)
    for a in arrays[:-1]:
        at += a.shape[along]
        ends.append(at)
    both = jnp.concatenate(arrays, axis=along)
    return tuple(
        jnp.split(lax.psum_scatter(both, axis, scatter_dimension=dim, tiled=True), ends, axis=along)
    )


def gelu_tanh(inputs):
    inner = 0.7978845608028654 * (inputs + 0.044715 * inputs * inputs * inputs)
    return 0.5 * inputs * (1.0 + jnp.tanh(inner))


def layer_norm(inputs, gain_row, bias_row):
    average = jnp.mean(inputs, axis=-1, keepdims=True)
    centred = inputs - average
    variance = jnp.mean(centred * centred, axis=-1, keepdims=True)
    return centred * lax.rsqrt(variance + eps_norm) * gain_row + bias_row


def allowed_mask(seg_rows):
    length = seg_rows.shape[1]
    places = lax.iota(jnp.int32, length)
    causal = places[:, None] >= places[None, :]
    same_doc = seg_rows[:, :, None] == seg_rows[:, None, :]
    return jnp.logical_and(same_doc, causal[None])[:, None]


def attend_scores(queries, keys_in, seg_rows):
    scaling = queries.shape[-1] ** (-0.5)
    scores = (
        jnp.einsum("rqhe,rkhe->rhqk", queries, keys_in, preferred_element_type=jnp.float32)
        * scaling
    )
    return (scores, allowed_mask(seg_rows), scaling)


def attention_forward(queries, keys_in, values, seg_rows):
    scores, allowed, scaling = attend_scores(queries, keys_in, seg_rows)
    exponent = jnp.where(allowed, jnp.exp(scores), 0.0)
    log_total = jnp.log(jnp.sum(exponent, axis=-1, keepdims=True))
    attn_weights = jnp.where(allowed, jnp.exp(scores - log_total), 0.0).astype(jnp.bfloat16)
    attended = jnp.einsum(
        "rhqk,rkhe->rqhe", attn_weights, values, preferred_element_type=jnp.float32
    )
    return (attended.astype(jnp.bfloat16), log_total)


def attention_backward(queries, keys_in, values, seg_rows, log_total, grad_att):
    scores, allowed, scaling = attend_scores(queries, keys_in, seg_rows)
    weights_full = jnp.where(allowed, jnp.exp(scores - log_total), 0.0)
    weights_half = weights_full.astype(jnp.bfloat16)
    grad_values = jnp.einsum(
        "rhqk,rqhe->rkhe", weights_half, grad_att, preferred_element_type=jnp.float32
    )
    grad_weights = jnp.einsum(
        "rqhe,rkhe->rhqk", grad_att, values, preferred_element_type=jnp.float32
    )
    row_dot = jnp.sum(weights_full * grad_weights, axis=-1, keepdims=True)
    grad_scores = (weights_full * (grad_weights - row_dot) * scaling).astype(jnp.bfloat16)
    grad_queries = jnp.einsum(
        "rhqk,rkhe->rqhe", grad_scores, keys_in, preferred_element_type=jnp.float32
    )
    grad_keys = jnp.einsum(
        "rhqk,rqhe->rkhe", grad_scores, queries, preferred_element_type=jnp.float32
    )
    return (grad_queries, grad_keys, grad_values)


def block_pass(tokens_in, cot_in, seg_rows, qkv_mat, out_mat, fc_mat, proj_mat, vec_rows):
    count_tok = tokens_in.shape[0]
    width = tokens_in.shape[1]
    head_width = width // HEADS
    row_count = count_tok // SEQ
    split_shape = (row_count, SEQ, HEADS, head_width)
    tokens32 = tokens_in.astype(jnp.float32)
    normed_one = layer_norm(tokens32, vec_rows[0], vec_rows[1]).astype(jnp.bfloat16)
    projected = jnp.dot(normed_one, qkv_mat, preferred_element_type=jnp.float32)
    queries = (projected[:, :width] + vec_rows[2]).astype(jnp.bfloat16).reshape(split_shape)
    keys_in = projected[:, width : 2 * width].astype(jnp.bfloat16).reshape(split_shape)
    values = (projected[:, 2 * width :] + vec_rows[3]).astype(jnp.bfloat16).reshape(split_shape)
    attended, log_total = attention_forward(queries, keys_in, values, seg_rows)
    attended = attended.reshape(count_tok, width)
    middle = tokens32 + jnp.dot(attended, out_mat, preferred_element_type=jnp.float32) + vec_rows[4]
    normed_two = layer_norm(middle, vec_rows[5], vec_rows[6]).astype(jnp.bfloat16)
    fc_bias = vec_rows[8:].reshape(-1)
    hidden_pre = jnp.dot(normed_two, fc_mat, preferred_element_type=jnp.float32) + fc_bias
    hidden = gelu_tanh(hidden_pre).astype(jnp.bfloat16)
    block_out = (
        middle + jnp.dot(hidden, proj_mat, preferred_element_type=jnp.float32) + vec_rows[7]
    ).astype(jnp.bfloat16)
    cot32 = cot_in.astype(jnp.float32)
    grad_proj = jnp.dot(hidden.T, cot_in, preferred_element_type=jnp.float32)
    grad_hidden = jnp.dot(cot_in, proj_mat.T, preferred_element_type=jnp.float32)
    gelu_back = jax.vjp(gelu_tanh, hidden_pre)[1]
    grad_pre = gelu_back(grad_hidden)[0]
    grad_pre_half = grad_pre.astype(jnp.bfloat16)
    grad_fc = jnp.dot(normed_two.T, grad_pre_half, preferred_element_type=jnp.float32)
    grad_normed_two = jnp.dot(grad_pre_half, fc_mat.T, preferred_element_type=jnp.float32)
    norm_two_back = jax.vjp(layer_norm, middle, vec_rows[5], vec_rows[6])[1]
    grad_mid_norm, grad_gain_two, grad_bias_two = norm_two_back(grad_normed_two)
    grad_middle = cot32 + grad_mid_norm
    grad_middle_half = grad_middle.astype(jnp.bfloat16)
    grad_out = jnp.dot(attended.T, grad_middle_half, preferred_element_type=jnp.float32)
    grad_attended = jnp.dot(grad_middle_half, out_mat.T, preferred_element_type=jnp.float32)
    grad_attended = grad_attended.astype(jnp.bfloat16).reshape(split_shape)
    grad_queries, grad_keys, grad_values = attention_backward(
        queries, keys_in, values, seg_rows, log_total, grad_attended
    )
    flat_queries = grad_queries.reshape(count_tok, width)
    flat_keys = grad_keys.reshape(count_tok, width)
    flat_values = grad_values.reshape(count_tok, width)
    grad_projected = jnp.concatenate([flat_queries, flat_keys, flat_values], axis=1).astype(
        jnp.bfloat16
    )
    grad_qkv = jnp.dot(normed_one.T, grad_projected, preferred_element_type=jnp.float32)
    grad_normed_one = jnp.dot(grad_projected, qkv_mat.T, preferred_element_type=jnp.float32)
    norm_one_back = jax.vjp(layer_norm, tokens32, vec_rows[0], vec_rows[1])[1]
    grad_tok_norm, grad_gain_one, grad_bias_one = norm_one_back(grad_normed_one)
    input_grad = (grad_middle + grad_tok_norm).astype(jnp.bfloat16)
    small_rows = jnp.stack(
        [
            grad_gain_one,
            grad_bias_one,
            jnp.sum(flat_queries, axis=0),
            jnp.sum(flat_values, axis=0),
            jnp.sum(grad_middle, axis=0),
            grad_gain_two,
            grad_bias_two,
            jnp.sum(cot32, axis=0),
        ]
    )
    grad_vec = jnp.concatenate([small_rows, jnp.sum(grad_pre, axis=0).reshape(-1, width)], axis=0)
    return (block_out, input_grad, (grad_qkv, grad_out, grad_fc, grad_proj, grad_vec))


def adam_step(weight, gradient, mean_old, square_old, rate, decay):
    mean_new = beta_first * mean_old + (1.0 - beta_first) * gradient
    square_new = beta_second * square_old + (1.0 - beta_second) * gradient * gradient
    mean_hat = mean_new / (1.0 - beta_first**ADAM_STEP)
    square_hat = square_new / (1.0 - beta_second**ADAM_STEP)
    weight_new = weight - rate * (mean_hat / (jnp.sqrt(square_hat) + eps_adam) + decay * weight)
    return (weight_new, mean_new, square_new)


def local(
    tokens,
    cotangent,
    segments,
    w_qkv,
    w_out,
    w_fc,
    w_proj,
    vectors,
    mean_qkv,
    mean_out,
    mean_fc,
    mean_proj,
    mean_vectors,
    square_qkv,
    square_out,
    square_fc,
    square_proj,
    square_vectors,
):
    dp_size = lax.axis_size("dp")
    zero_size = lax.axis_size("zero")
    replicas = dp_size * zero_size
    vec_cols = jnp.pad(vectors.astype(jnp.bfloat16).T, ((0, 0), (0, LANE - vectors.shape[0])))
    qkv_mat, out_mat, fc_mat, vec_cols_all = sent_together(
        (
            w_qkv.astype(jnp.bfloat16),
            w_out.astype(jnp.bfloat16),
            w_fc.astype(jnp.bfloat16),
            vec_cols,
        ),
        "zero",
        0,
        1,
    )
    proj_mat = lax.all_gather(w_proj.astype(jnp.bfloat16), "zero", axis=0, tiled=True)
    vec_rows = vec_cols_all[:, : vectors.shape[0]].T.astype(jnp.float32)
    block_out, input_grad, local_grads = block_pass(
        tokens, cotangent, segments, qkv_mat, out_mat, fc_mat, proj_mat, vec_rows
    )
    grad_vec_cols = jnp.pad(
        local_grads[4].astype(jnp.bfloat16).T, ((0, 0), (0, LANE - vectors.shape[0]))
    )
    joined = jnp.concatenate(
        (
            local_grads[0].astype(jnp.bfloat16),
            local_grads[1].astype(jnp.bfloat16),
            local_grads[2].astype(jnp.bfloat16),
            grad_vec_cols,
        ),
        axis=1,
    )
    scattered = lax.psum_scatter(joined, "zero", scatter_dimension=0, tiled=True)
    proj_scattered = lax.psum_scatter(
        local_grads[3].astype(jnp.bfloat16), "zero", scatter_dimension=0, tiled=True
    )
    summed_joined, summed_proj = lax.psum((scattered, proj_scattered), "dp")
    ends = [w_qkv.shape[1], w_qkv.shape[1] + w_out.shape[1], w_qkv.shape[1] + w_out.shape[1] + w_fc.shape[1]]
    g_qkv, g_out, g_fc, g_vec = jnp.split(summed_joined, ends, axis=1)
    summed = (
        g_qkv.astype(jnp.float32),
        g_out.astype(jnp.float32),
        g_fc.astype(jnp.float32),
        summed_proj.astype(jnp.float32),
        g_vec[:, : vectors.shape[0]].T.astype(jnp.float32),
    )
    grads = jax.tree.map(partial(jnp.multiply, 1.0 / replicas), summed)
    first = adam_step(w_qkv, grads[0], mean_qkv, square_qkv, rate_matrix, decay_matrix)
    second = adam_step(w_out, grads[1], mean_out, square_out, rate_matrix, decay_matrix)
    third = adam_step(w_fc, grads[2], mean_fc, square_fc, rate_matrix, decay_matrix)
    fourth = adam_step(w_proj, grads[3], mean_proj, square_proj, rate_matrix, decay_matrix)
    fifth = adam_step(vectors, grads[4], mean_vectors, square_vectors, rate_vector, 0.0)
    return (
        block_out,
        input_grad,
        grads[0],
        grads[1],
        grads[2],
        grads[3],
        grads[4],
        first[0],
        second[0],
        third[0],
        fourth[0],
        fifth[0],
        first[1],
        second[1],
        third[1],
        fourth[1],
        fifth[1],
        first[2],
        second[2],
        third[2],
        fourth[2],
        fifth[2],
    )


def solution(mesh):
    placed = (
        P(("dp", "zero"), None),
        P(("dp", "zero"), None),
        P(("dp", "zero"), None),
        P("zero", None),
        P("zero", None),
        P("zero", None),
        P("zero", None),
        P(None, "zero"),
        P("zero", None),
        P("zero", None),
        P("zero", None),
        P("zero", None),
        P(None, "zero"),
        P("zero", None),
        P("zero", None),
        P("zero", None),
        P("zero", None),
        P(None, "zero"),
    )
    return jax.shard_map(
        local,
        mesh=mesh,
        in_specs=placed,
        out_specs=(
            P(("dp", "zero"), None),
            P(("dp", "zero"), None),
            P("zero", None),
            P("zero", None),
            P("zero", None),
            P("zero", None),
            P(None, "zero"),
            P("zero", None),
            P("zero", None),
            P("zero", None),
            P("zero", None),
            P(None, "zero"),
            P("zero", None),
            P("zero", None),
            P("zero", None),
            P("zero", None),
            P(None, "zero"),
            P("zero", None),
            P("zero", None),
            P("zero", None),
            P("zero", None),
            P(None, "zero"),
        ),
        check_vma=False,
    )
```

```python
from functools import partial

import jax
import jax.numpy as jnp
from jax import lax
from jax.sharding import PartitionSpec as P

HEADS = 16
SEQ = 128
ADAM_STEP = 3
LANE = 128


eps_norm = 1e-05
beta_first = 0.9
beta_second = 0.999
eps_adam = 1e-08
rate_matrix = 0.02
rate_vector = 0.15
decay_matrix = 0.1


def sent_together(arrays, axis, dim, along):
    widths = [a.shape[along] for a in arrays]
    both = jnp.concatenate(arrays, axis=along)
    result = lax.all_gather(both, axis, axis=dim, tiled=True)
    return tuple(jnp.split(result, [sum(widths[:k]) for k in range(1, len(widths))], axis=along))


def in_one_piece(arrays, axis, dim, along):
    ends, at = ([], 0)
    for a in arrays[:-1]:
        at += a.shape[along]
        ends.append(at)
    both = jnp.concatenate(arrays, axis=along)
    return tuple(
        jnp.split(lax.psum_scatter(both, axis, scatter_dimension=dim, tiled=True), ends, axis=along)
    )


def gelu_tanh(inputs):
    inner = 0.7978845608028654 * (inputs + 0.044715 * inputs * inputs * inputs)
    return 0.5 * inputs * (1.0 + jnp.tanh(inner))


def layer_norm(inputs, gain_row, bias_row):
    average = jnp.mean(inputs, axis=-1, keepdims=True)
    centred = inputs - average
    variance = jnp.mean(centred * centred, axis=-1, keepdims=True)
    return centred * lax.rsqrt(variance + eps_norm) * gain_row + bias_row


def allowed_mask(seg_rows):
    length = seg_rows.shape[1]
    places = lax.iota(jnp.int32, length)
    causal = places[:, None] >= places[None, :]
    same_doc = seg_rows[:, :, None] == seg_rows[:, None, :]
    return jnp.logical_and(same_doc, causal[None])[:, None]


def attend_scores(queries, keys_in, seg_rows):
    scaling = queries.shape[-1] ** (-0.5)
    scores = (
        jnp.einsum("rqhe,rkhe->rhqk", queries, keys_in, preferred_element_type=jnp.float32)
        * scaling
    )
    return (scores, allowed_mask(seg_rows), scaling)


def attention_forward(queries, keys_in, values, seg_rows):
    scores, allowed, scaling = attend_scores(queries, keys_in, seg_rows)
    exponent = jnp.where(allowed, jnp.exp(scores), 0.0)
    log_total = jnp.log(jnp.sum(exponent, axis=-1, keepdims=True))
    attn_weights = jnp.where(allowed, jnp.exp(scores - log_total), 0.0).astype(jnp.bfloat16)
    attended = jnp.einsum(
        "rhqk,rkhe->rqhe", attn_weights, values, preferred_element_type=jnp.float32
    )
    return (attended.astype(jnp.bfloat16), log_total)


def attention_backward(queries, keys_in, values, seg_rows, log_total, grad_att):
    scores, allowed, scaling = attend_scores(queries, keys_in, seg_rows)
    weights_full = jnp.where(allowed, jnp.exp(scores - log_total), 0.0)
    weights_half = weights_full.astype(jnp.bfloat16)
    grad_values = jnp.einsum(
        "rhqk,rqhe->rkhe", weights_half, grad_att, preferred_element_type=jnp.float32
    )
    grad_weights = jnp.einsum(
        "rqhe,rkhe->rhqk", grad_att, values, preferred_element_type=jnp.float32
    )
    row_dot = jnp.sum(weights_full * grad_weights, axis=-1, keepdims=True)
    grad_scores = (weights_full * (grad_weights - row_dot) * scaling).astype(jnp.bfloat16)
    grad_queries = jnp.einsum(
        "rhqk,rkhe->rqhe", grad_scores, keys_in, preferred_element_type=jnp.float32
    )
    grad_keys = jnp.einsum(
        "rhqk,rqhe->rkhe", grad_scores, queries, preferred_element_type=jnp.float32
    )
    return (grad_queries, grad_keys, grad_values)


def block_pass(tokens_in, cot_in, seg_rows, qkv_mat, out_mat, fc_mat, proj_mat, vec_rows):
    count_tok = tokens_in.shape[0]
    width = tokens_in.shape[1]
    head_width = width // HEADS
    row_count = count_tok // SEQ
    split_shape = (row_count, SEQ, HEADS, head_width)
    tokens32 = tokens_in.astype(jnp.float32)
    normed_one = layer_norm(tokens32, vec_rows[0], vec_rows[1]).astype(jnp.bfloat16)
    projected = jnp.dot(normed_one, qkv_mat, preferred_element_type=jnp.float32)
    queries = (projected[:, :width] + vec_rows[2]).astype(jnp.bfloat16).reshape(split_shape)
    keys_in = projected[:, width : 2 * width].astype(jnp.bfloat16).reshape(split_shape)
    values = (projected[:, 2 * width :] + vec_rows[3]).astype(jnp.bfloat16).reshape(split_shape)
    attended, log_total = attention_forward(queries, keys_in, values, seg_rows)
    attended = attended.reshape(count_tok, width)
    middle = tokens32 + jnp.dot(attended, out_mat, preferred_element_type=jnp.float32) + vec_rows[4]
    normed_two = layer_norm(middle, vec_rows[5], vec_rows[6]).astype(jnp.bfloat16)
    fc_bias = vec_rows[8:].reshape(-1)
    hidden_pre = jnp.dot(normed_two, fc_mat, preferred_element_type=jnp.float32) + fc_bias
    hidden = gelu_tanh(hidden_pre).astype(jnp.bfloat16)
    block_out = (
        middle + jnp.dot(hidden, proj_mat, preferred_element_type=jnp.float32) + vec_rows[7]
    ).astype(jnp.bfloat16)
    cot32 = cot_in.astype(jnp.float32)
    grad_proj = jnp.dot(hidden.T, cot_in, preferred_element_type=jnp.float32)
    grad_hidden = jnp.dot(cot_in, proj_mat.T, preferred_element_type=jnp.float32)
    gelu_back = jax.vjp(gelu_tanh, hidden_pre)[1]
    grad_pre = gelu_back(grad_hidden)[0]
    grad_pre_half = grad_pre.astype(jnp.bfloat16)
    grad_fc = jnp.dot(normed_two.T, grad_pre_half, preferred_element_type=jnp.float32)
    grad_normed_two = jnp.dot(grad_pre_half, fc_mat.T, preferred_element_type=jnp.float32)
    norm_two_back = jax.vjp(layer_norm, middle, vec_rows[5], vec_rows[6])[1]
    grad_mid_norm, grad_gain_two, grad_bias_two = norm_two_back(grad_normed_two)
    grad_middle = cot32 + grad_mid_norm
    grad_middle_half = grad_middle.astype(jnp.bfloat16)
    grad_out = jnp.dot(attended.T, grad_middle_half, preferred_element_type=jnp.float32)
    grad_attended = jnp.dot(grad_middle_half, out_mat.T, preferred_element_type=jnp.float32)
    grad_attended = grad_attended.astype(jnp.bfloat16).reshape(split_shape)
    grad_queries, grad_keys, grad_values = attention_backward(
        queries, keys_in, values, seg_rows, log_total, grad_attended
    )
    flat_queries = grad_queries.reshape(count_tok, width)
    flat_keys = grad_keys.reshape(count_tok, width)
    flat_values = grad_values.reshape(count_tok, width)
    grad_projected = jnp.concatenate([flat_queries, flat_keys, flat_values], axis=1).astype(
        jnp.bfloat16
    )
    grad_qkv = jnp.dot(normed_one.T, grad_projected, preferred_element_type=jnp.float32)
    grad_normed_one = jnp.dot(grad_projected, qkv_mat.T, preferred_element_type=jnp.float32)
    norm_one_back = jax.vjp(layer_norm, tokens32, vec_rows[0], vec_rows[1])[1]
    grad_tok_norm, grad_gain_one, grad_bias_one = norm_one_back(grad_normed_one)
    input_grad = (grad_middle + grad_tok_norm).astype(jnp.bfloat16)
    small_rows = jnp.stack(
        [
            grad_gain_one,
            grad_bias_one,
            jnp.sum(flat_queries, axis=0),
            jnp.sum(flat_values, axis=0),
            jnp.sum(grad_middle, axis=0),
            grad_gain_two,
            grad_bias_two,
            jnp.sum(cot32, axis=0),
        ]
    )
    grad_vec = jnp.concatenate([small_rows, jnp.sum(grad_pre, axis=0).reshape(-1, width)], axis=0)
    return (block_out, input_grad, (grad_qkv, grad_out, grad_fc, grad_proj, grad_vec))


def adam_step(weight, gradient, mean_old, square_old, rate, decay):
    mean_new = beta_first * mean_old + (1.0 - beta_first) * gradient
    square_new = beta_second * square_old + (1.0 - beta_second) * gradient * gradient
    mean_hat = mean_new / (1.0 - beta_first**ADAM_STEP)
    square_hat = square_new / (1.0 - beta_second**ADAM_STEP)
    weight_new = weight - rate * (mean_hat / (jnp.sqrt(square_hat) + eps_adam) + decay * weight)
    return (weight_new, mean_new, square_new)


def local(
    tokens,
    cotangent,
    segments,
    w_qkv,
    w_out,
    w_fc,
    w_proj,
    vectors,
    mean_qkv,
    mean_out,
    mean_fc,
    mean_proj,
    mean_vectors,
    square_qkv,
    square_out,
    square_fc,
    square_proj,
    square_vectors,
):
    dp_size = lax.axis_size("dp")
    zero_size = lax.axis_size("zero")
    replicas = dp_size * zero_size
    vec_cols = jnp.pad(vectors.astype(jnp.bfloat16).T, ((0, 0), (0, LANE - vectors.shape[0])))
    qkv_mat, out_mat, fc_mat, vec_cols_all = sent_together(
        (
            w_qkv.astype(jnp.bfloat16),
            w_out.astype(jnp.bfloat16),
            w_fc.astype(jnp.bfloat16),
            vec_cols,
        ),
        "zero",
        0,
        1,
    )
    proj_mat = lax.all_gather(w_proj.astype(jnp.bfloat16), "zero", axis=0, tiled=True)
    vec_rows = vec_cols_all[:, : vectors.shape[0]].T.astype(jnp.float32)
    block_out, input_grad, local_grads = block_pass(
        tokens, cotangent, segments, qkv_mat, out_mat, fc_mat, proj_mat, vec_rows
    )
    grad_vec_cols = jnp.pad(
        local_grads[4].astype(jnp.bfloat16).T, ((0, 0), (0, LANE - vectors.shape[0]))
    )
    joined = jnp.concatenate(
        (
            local_grads[0].astype(jnp.bfloat16),
            local_grads[1].astype(jnp.bfloat16),
            local_grads[2].astype(jnp.bfloat16),
            grad_vec_cols,
        ),
        axis=1,
    )
    scattered = lax.psum_scatter(joined, "zero", scatter_dimension=0, tiled=True)
    proj_scattered = lax.psum_scatter(
        local_grads[3].astype(jnp.bfloat16), "zero", scatter_dimension=0, tiled=True
    )
    summed_joined, summed_proj = lax.psum((scattered, proj_scattered), "dp")
    ends = [w_qkv.shape[1], w_qkv.shape[1] + w_out.shape[1], w_qkv.shape[1] + w_out.shape[1] + w_fc.shape[1]]
    g_qkv, g_out, g_fc, g_vec = jnp.split(summed_joined, ends, axis=1)
    summed = (
        g_qkv.astype(jnp.float32),
        g_out.astype(jnp.float32),
        g_fc.astype(jnp.float32),
        summed_proj.astype(jnp.float32),
        lax.dot_general(
            g_vec[:, : vectors.shape[0]],
            jnp.eye(g_vec.shape[0], dtype=jnp.bfloat16),
            (((0,), (0,)), ((), ())),
            preferred_element_type=jnp.float32,
        ),
    )
    grads = jax.tree.map(partial(jnp.multiply, 1.0 / replicas), summed)
    first = adam_step(w_qkv, grads[0], mean_qkv, square_qkv, rate_matrix, decay_matrix)
    second = adam_step(w_out, grads[1], mean_out, square_out, rate_matrix, decay_matrix)
    third = adam_step(w_fc, grads[2], mean_fc, square_fc, rate_matrix, decay_matrix)
    fourth = adam_step(w_proj, grads[3], mean_proj, square_proj, rate_matrix, decay_matrix)
    fifth = adam_step(vectors, grads[4], mean_vectors, square_vectors, rate_vector, 0.0)
    return (
        block_out,
        input_grad,
        grads[0],
        grads[1],
        grads[2],
        grads[3],
        grads[4],
        first[0],
        second[0],
        third[0],
        fourth[0],
        fifth[0],
        first[1],
        second[1],
        third[1],
        fourth[1],
        fifth[1],
        first[2],
        second[2],
        third[2],
        fourth[2],
        fifth[2],
    )


def solution(mesh):
    placed = (
        P(("dp", "zero"), None),
        P(("dp", "zero"), None),
        P(("dp", "zero"), None),
        P("zero", None),
        P("zero", None),
        P("zero", None),
        P("zero", None),
        P(None, "zero"),
        P("zero", None),
        P("zero", None),
        P("zero", None),
        P("zero", None),
        P(None, "zero"),
        P("zero", None),
        P("zero", None),
        P("zero", None),
        P("zero", None),
        P(None, "zero"),
    )
    return jax.shard_map(
        local,
        mesh=mesh,
        in_specs=placed,
        out_specs=(
            P(("dp", "zero"), None),
            P(("dp", "zero"), None),
            P("zero", None),
            P("zero", None),
            P("zero", None),
            P("zero", None),
            P(None, "zero"),
            P("zero", None),
            P("zero", None),
            P("zero", None),
            P("zero", None),
            P(None, "zero"),
            P("zero", None),
            P("zero", None),
            P("zero", None),
            P("zero", None),
            P(None, "zero"),
            P("zero", None),
            P("zero", None),
            P("zero", None),
            P("zero", None),
            P(None, "zero"),
        ),
        check_vma=False,
    )
```

```python
from functools import partial

import jax
import jax.numpy as jnp
from jax import lax
from jax.sharding import PartitionSpec as P

HEADS = 16
SEQ = 128
ADAM_STEP = 3
LANE = 128


eps_norm = 1e-05
beta_first = 0.9
beta_second = 0.999
eps_adam = 1e-08
rate_matrix = 0.02
rate_vector = 0.15
decay_matrix = 0.1


def sent_together(arrays, axis, dim, along):
    widths = [a.shape[along] for a in arrays]
    both = jnp.concatenate(arrays, axis=along)
    result = lax.all_gather(both, axis, axis=dim, tiled=True)
    return tuple(jnp.split(result, [sum(widths[:k]) for k in range(1, len(widths))], axis=along))


def in_one_piece(arrays, axis, dim, along):
    ends, at = ([], 0)
    for a in arrays[:-1]:
        at += a.shape[along]
        ends.append(at)
    both = jnp.concatenate(arrays, axis=along)
    return tuple(
        jnp.split(lax.psum_scatter(both, axis, scatter_dimension=dim, tiled=True), ends, axis=along)
    )


def gather_rows(shard):
    chips = lax.all_gather(shard, "zc", axis=0, tiled=False)
    both = lax.all_gather(chips, "core", axis=1, tiled=False)
    return both.reshape((-1,) + shard.shape[1:])


def core_major(columns):
    chips = lax.axis_size("zc")
    cores = lax.axis_size("core")
    split = columns.reshape(columns.shape[0], chips, cores, -1)
    return split.transpose(0, 2, 1, 3).reshape(columns.shape)


def scatter_rows(whole):
    chips = lax.axis_size("zc")
    cores = lax.axis_size("core")
    grouped = whole.reshape((cores, chips, whole.shape[0] // (chips * cores)) + whole.shape[1:])
    on_chip = lax.psum_scatter(grouped, "core", scatter_dimension=0, tiled=False)
    return lax.psum_scatter(on_chip, "zc", scatter_dimension=0, tiled=False)


def gelu_tanh(inputs):
    inner = 0.7978845608028654 * (inputs + 0.044715 * inputs * inputs * inputs)
    return 0.5 * inputs * (1.0 + jnp.tanh(inner))


def layer_norm(inputs, gain_row, bias_row):
    average = jnp.mean(inputs, axis=-1, keepdims=True)
    centred = inputs - average
    variance = jnp.mean(centred * centred, axis=-1, keepdims=True)
    return centred * lax.rsqrt(variance + eps_norm) * gain_row + bias_row


def allowed_mask(seg_rows):
    length = seg_rows.shape[1]
    places = lax.iota(jnp.int32, length)
    causal = places[:, None] >= places[None, :]
    same_doc = seg_rows[:, :, None] == seg_rows[:, None, :]
    return jnp.logical_and(same_doc, causal[None])[:, None]


def attend_scores(queries, keys_in, seg_rows):
    scaling = queries.shape[-1] ** (-0.5)
    scores = (
        jnp.einsum("rqhe,rkhe->rhqk", queries, keys_in, preferred_element_type=jnp.float32)
        * scaling
    )
    return (scores, allowed_mask(seg_rows), scaling)


def attention_forward(queries, keys_in, values, seg_rows):
    scores, allowed, scaling = attend_scores(queries, keys_in, seg_rows)
    exponent = jnp.where(allowed, jnp.exp(scores), 0.0)
    log_total = jnp.log(jnp.sum(exponent, axis=-1, keepdims=True))
    attn_weights = jnp.where(allowed, jnp.exp(scores - log_total), 0.0).astype(jnp.bfloat16)
    attended = jnp.einsum(
        "rhqk,rkhe->rqhe", attn_weights, values, preferred_element_type=jnp.float32
    )
    return (attended.astype(jnp.bfloat16), log_total)


def attention_backward(queries, keys_in, values, seg_rows, log_total, grad_att):
    scores, allowed, scaling = attend_scores(queries, keys_in, seg_rows)
    weights_full = jnp.where(allowed, jnp.exp(scores - log_total), 0.0)
    weights_half = weights_full.astype(jnp.bfloat16)
    grad_values = jnp.einsum(
        "rhqk,rqhe->rkhe", weights_half, grad_att, preferred_element_type=jnp.float32
    )
    grad_weights = jnp.einsum(
        "rqhe,rkhe->rhqk", grad_att, values, preferred_element_type=jnp.float32
    )
    row_dot = jnp.sum(weights_full * grad_weights, axis=-1, keepdims=True)
    grad_scores = (weights_full * (grad_weights - row_dot) * scaling).astype(jnp.bfloat16)
    grad_queries = jnp.einsum(
        "rhqk,rkhe->rqhe", grad_scores, keys_in, preferred_element_type=jnp.float32
    )
    grad_keys = jnp.einsum(
        "rhqk,rqhe->rkhe", grad_scores, queries, preferred_element_type=jnp.float32
    )
    return (grad_queries, grad_keys, grad_values)


def block_pass(tokens_in, cot_in, seg_rows, qkv_mat, out_mat, fc_mat, proj_mat, vec_rows, order):
    count_tok = tokens_in.shape[0]
    width = tokens_in.shape[1]
    head_width = width // HEADS
    row_count = count_tok // SEQ
    split_shape = (row_count, SEQ, HEADS, head_width)
    tokens32 = tokens_in.astype(jnp.float32)
    normed_one = layer_norm(tokens32, vec_rows[0], vec_rows[1]).astype(jnp.bfloat16)
    projected = jnp.dot(normed_one, qkv_mat, preferred_element_type=jnp.float32)
    queries = (projected[:, :width] + vec_rows[2]).astype(jnp.bfloat16).reshape(split_shape)
    keys_in = projected[:, width : 2 * width].astype(jnp.bfloat16).reshape(split_shape)
    values = (projected[:, 2 * width :] + vec_rows[3]).astype(jnp.bfloat16).reshape(split_shape)
    attended, log_total = attention_forward(queries, keys_in, values, seg_rows)
    attended = attended.reshape(count_tok, width)
    middle = tokens32 + jnp.dot(attended, out_mat, preferred_element_type=jnp.float32) + vec_rows[4]
    normed_two = layer_norm(middle, vec_rows[5], vec_rows[6]).astype(jnp.bfloat16)
    fc_bias = vec_rows[8:].reshape(-1)
    hidden_pre = jnp.dot(normed_two, fc_mat, preferred_element_type=jnp.float32) + fc_bias
    hidden = gelu_tanh(hidden_pre).astype(jnp.bfloat16)
    block_out = (
        middle + jnp.dot(hidden, proj_mat, preferred_element_type=jnp.float32) + vec_rows[7]
    ).astype(jnp.bfloat16)
    cot32 = cot_in.astype(jnp.float32)
    grad_proj = jnp.dot(order(hidden).T, cot_in, preferred_element_type=jnp.float32)
    grad_hidden = jnp.dot(cot_in, proj_mat.T, preferred_element_type=jnp.float32)
    gelu_back = jax.vjp(gelu_tanh, hidden_pre)[1]
    grad_pre = gelu_back(grad_hidden)[0]
    grad_pre_half = grad_pre.astype(jnp.bfloat16)
    grad_fc = jnp.dot(order(normed_two).T, grad_pre_half, preferred_element_type=jnp.float32)
    grad_normed_two = jnp.dot(grad_pre_half, fc_mat.T, preferred_element_type=jnp.float32)
    norm_two_back = jax.vjp(layer_norm, middle, vec_rows[5], vec_rows[6])[1]
    grad_mid_norm, grad_gain_two, grad_bias_two = norm_two_back(grad_normed_two)
    grad_middle = cot32 + grad_mid_norm
    grad_middle_half = grad_middle.astype(jnp.bfloat16)
    grad_out = jnp.dot(order(attended).T, grad_middle_half, preferred_element_type=jnp.float32)
    grad_attended = jnp.dot(grad_middle_half, out_mat.T, preferred_element_type=jnp.float32)
    grad_attended = grad_attended.astype(jnp.bfloat16).reshape(split_shape)
    grad_queries, grad_keys, grad_values = attention_backward(
        queries, keys_in, values, seg_rows, log_total, grad_attended
    )
    flat_queries = grad_queries.reshape(count_tok, width)
    flat_keys = grad_keys.reshape(count_tok, width)
    flat_values = grad_values.reshape(count_tok, width)
    grad_projected = jnp.concatenate([flat_queries, flat_keys, flat_values], axis=1).astype(
        jnp.bfloat16
    )
    grad_qkv = jnp.dot(order(normed_one).T, grad_projected, preferred_element_type=jnp.float32)
    grad_normed_one = jnp.dot(grad_projected, qkv_mat.T, preferred_element_type=jnp.float32)
    norm_one_back = jax.vjp(layer_norm, tokens32, vec_rows[0], vec_rows[1])[1]
    grad_tok_norm, grad_gain_one, grad_bias_one = norm_one_back(grad_normed_one)
    input_grad = (grad_middle + grad_tok_norm).astype(jnp.bfloat16)
    small_rows = jnp.stack(
        [
            grad_gain_one,
            grad_bias_one,
            jnp.sum(flat_queries, axis=0),
            jnp.sum(flat_values, axis=0),
            jnp.sum(grad_middle, axis=0),
            grad_gain_two,
            grad_bias_two,
            jnp.sum(cot32, axis=0),
        ]
    )
    grad_vec = jnp.concatenate([small_rows, jnp.sum(grad_pre, axis=0).reshape(-1, width)], axis=0)
    return (block_out, input_grad, (grad_qkv, grad_out, grad_fc, grad_proj, grad_vec))


def adam_step(weight, gradient, mean_old, square_old, rate, decay):
    mean_new = beta_first * mean_old + (1.0 - beta_first) * gradient
    square_new = beta_second * square_old + (1.0 - beta_second) * gradient * gradient
    mean_hat = mean_new / (1.0 - beta_first**ADAM_STEP)
    square_hat = square_new / (1.0 - beta_second**ADAM_STEP)
    weight_new = weight - rate * (mean_hat / (jnp.sqrt(square_hat) + eps_adam) + decay * weight)
    return (weight_new, mean_new, square_new)


def local(
    tokens,
    cotangent,
    segments,
    w_qkv,
    w_out,
    w_fc,
    w_proj,
    vectors,
    mean_qkv,
    mean_out,
    mean_fc,
    mean_proj,
    mean_vectors,
    square_qkv,
    square_out,
    square_fc,
    square_proj,
    square_vectors,
):
    dp_size = lax.axis_size("dp")
    zero_size = lax.axis_size("zc") * lax.axis_size("core")
    replicas = dp_size * zero_size
    vec_cols = jnp.pad(vectors.astype(jnp.bfloat16).T, ((0, 0), (0, LANE - vectors.shape[0])))
    qkv_mat, out_mat, fc_mat, vec_cols_all = jnp.split(
        gather_rows(
            jnp.concatenate(
                (
                    w_qkv.astype(jnp.bfloat16),
                    w_out.astype(jnp.bfloat16),
                    w_fc.astype(jnp.bfloat16),
                    vec_cols,
                ),
                axis=1,
            )
        ),
        [w_qkv.shape[1], w_qkv.shape[1] + w_out.shape[1], w_qkv.shape[1] + w_out.shape[1] + w_fc.shape[1]],
        axis=1,
    )
    proj_mat = gather_rows(w_proj.astype(jnp.bfloat16))
    vec_rows = vec_cols_all[:, : vectors.shape[0]].T.astype(jnp.float32)
    block_out, input_grad, local_grads = block_pass(
        tokens, cotangent, segments, qkv_mat, out_mat, fc_mat, proj_mat, vec_rows, core_major
    )
    grad_vec_cols = jnp.pad(
        core_major(local_grads[4].astype(jnp.bfloat16)).T, ((0, 0), (0, LANE - vectors.shape[0]))
    )
    joined = jnp.concatenate(
        (
            local_grads[0].astype(jnp.bfloat16),
            local_grads[1].astype(jnp.bfloat16),
            local_grads[2].astype(jnp.bfloat16),
            grad_vec_cols,
        ),
        axis=1,
    )
    scattered = scatter_rows(joined)
    proj_scattered = scatter_rows(local_grads[3].astype(jnp.bfloat16))
    summed_joined, summed_proj = lax.psum((scattered, proj_scattered), "dp")
    ends = [w_qkv.shape[1], w_qkv.shape[1] + w_out.shape[1], w_qkv.shape[1] + w_out.shape[1] + w_fc.shape[1]]
    g_qkv, g_out, g_fc, g_vec = jnp.split(summed_joined, ends, axis=1)
    summed = (
        g_qkv.astype(jnp.float32),
        g_out.astype(jnp.float32),
        g_fc.astype(jnp.float32),
        summed_proj.astype(jnp.float32),
        lax.dot_general(
            g_vec[:, : vectors.shape[0]],
            jnp.eye(g_vec.shape[0], dtype=jnp.bfloat16),
            (((0,), (0,)), ((), ())),
            preferred_element_type=jnp.float32,
        ),
    )
    grads = jax.tree.map(partial(jnp.multiply, 1.0 / replicas), summed)
    first = adam_step(w_qkv, grads[0], mean_qkv, square_qkv, rate_matrix, decay_matrix)
    second = adam_step(w_out, grads[1], mean_out, square_out, rate_matrix, decay_matrix)
    third = adam_step(w_fc, grads[2], mean_fc, square_fc, rate_matrix, decay_matrix)
    fourth = adam_step(w_proj, grads[3], mean_proj, square_proj, rate_matrix, decay_matrix)
    fifth = adam_step(vectors, grads[4], mean_vectors, square_vectors, rate_vector, 0.0)
    return (
        block_out,
        input_grad,
        grads[0],
        grads[1],
        grads[2],
        grads[3],
        grads[4],
        first[0],
        second[0],
        third[0],
        fourth[0],
        fifth[0],
        first[1],
        second[1],
        third[1],
        fourth[1],
        fifth[1],
        first[2],
        second[2],
        third[2],
        fourth[2],
        fifth[2],
    )


def solution(mesh):
    cores = 2
    split_mesh = jax.sharding.Mesh(
        mesh.devices.reshape(mesh.shape["dp"], mesh.shape["zero"] // cores, cores),
        ("dp", "zc", "core"),
    )
    placed = (
        P(("dp", "zc", "core"), None),
        P(("dp", "zc", "core"), None),
        P(("dp", "zc", "core"), None),
        P(("zc", "core"), None),
        P(("zc", "core"), None),
        P(("zc", "core"), None),
        P(("zc", "core"), None),
        P(None, ("zc", "core")),
        P(("zc", "core"), None),
        P(("zc", "core"), None),
        P(("zc", "core"), None),
        P(("zc", "core"), None),
        P(None, ("zc", "core")),
        P(("zc", "core"), None),
        P(("zc", "core"), None),
        P(("zc", "core"), None),
        P(("zc", "core"), None),
        P(None, ("zc", "core")),
    )
    return jax.shard_map(
        local,
        mesh=split_mesh,
        in_specs=placed,
        out_specs=(
            P(("dp", "zc", "core"), None),
            P(("dp", "zc", "core"), None),
            P(("zc", "core"), None),
            P(("zc", "core"), None),
            P(("zc", "core"), None),
            P(("zc", "core"), None),
            P(None, ("zc", "core")),
            P(("zc", "core"), None),
            P(("zc", "core"), None),
            P(("zc", "core"), None),
            P(("zc", "core"), None),
            P(None, ("zc", "core")),
            P(("zc", "core"), None),
            P(("zc", "core"), None),
            P(("zc", "core"), None),
            P(("zc", "core"), None),
            P(None, ("zc", "core")),
            P(("zc", "core"), None),
            P(("zc", "core"), None),
            P(("zc", "core"), None),
            P(("zc", "core"), None),
            P(None, ("zc", "core")),
        ),
        check_vma=False,
    )
```

```python
from functools import partial

import jax
import jax.numpy as jnp
from jax import lax
from jax.sharding import PartitionSpec as P

HEADS = 16
SEQ = 128
ADAM_STEP = 3
LANE = 128


eps_norm = 1e-05
beta_first = 0.9
beta_second = 0.999
eps_adam = 1e-08
rate_matrix = 0.02
rate_vector = 0.15
decay_matrix = 0.1


def sent_together(arrays, axis, dim, along):
    widths = [a.shape[along] for a in arrays]
    both = jnp.concatenate(arrays, axis=along)
    result = lax.all_gather(both, axis, axis=dim, tiled=True)
    return tuple(jnp.split(result, [sum(widths[:k]) for k in range(1, len(widths))], axis=along))


def in_one_piece(arrays, axis, dim, along):
    ends, at = ([], 0)
    for a in arrays[:-1]:
        at += a.shape[along]
        ends.append(at)
    both = jnp.concatenate(arrays, axis=along)
    return tuple(
        jnp.split(lax.psum_scatter(both, axis, scatter_dimension=dim, tiled=True), ends, axis=along)
    )


def gelu_tanh(inputs):
    inner = 0.7978845608028654 * (inputs + 0.044715 * inputs * inputs * inputs)
    return 0.5 * inputs * (1.0 + jnp.tanh(inner))


def layer_norm(inputs, gain_row, bias_row):
    average = jnp.mean(inputs, axis=-1, keepdims=True)
    centred = inputs - average
    variance = jnp.mean(centred * centred, axis=-1, keepdims=True)
    return centred * lax.rsqrt(variance + eps_norm) * gain_row + bias_row


def allowed_mask(seg_rows):
    length = seg_rows.shape[1]
    places = lax.iota(jnp.int32, length)
    causal = places[:, None] >= places[None, :]
    same_doc = seg_rows[:, :, None] == seg_rows[:, None, :]
    return jnp.logical_and(same_doc, causal[None])[:, None]


def attend_scores(queries, keys_in, seg_rows):
    scaling = queries.shape[-1] ** (-0.5)
    scores = (
        jnp.einsum("rqhe,rkhe->rhqk", queries, keys_in, preferred_element_type=jnp.float32)
        * scaling
    )
    return (scores, allowed_mask(seg_rows), scaling)


def attention_forward(queries, keys_in, values, seg_rows):
    scores, allowed, scaling = attend_scores(queries, keys_in, seg_rows)
    exponent = jnp.where(allowed, jnp.exp(scores), 0.0)
    log_total = jnp.log(jnp.sum(exponent, axis=-1, keepdims=True))
    attn_weights = jnp.where(allowed, jnp.exp(scores - log_total), 0.0).astype(jnp.bfloat16)
    attended = jnp.einsum(
        "rhqk,rkhe->rqhe", attn_weights, values, preferred_element_type=jnp.float32
    )
    return (attended.astype(jnp.bfloat16), log_total)


def attention_backward(queries, keys_in, values, seg_rows, log_total, grad_att):
    scores, allowed, scaling = attend_scores(queries, keys_in, seg_rows)
    weights_full = jnp.where(allowed, jnp.exp(scores - log_total), 0.0)
    weights_half = weights_full.astype(jnp.bfloat16)
    grad_values = jnp.einsum(
        "rhqk,rqhe->rkhe", weights_half, grad_att, preferred_element_type=jnp.float32
    )
    grad_weights = jnp.einsum(
        "rqhe,rkhe->rhqk", grad_att, values, preferred_element_type=jnp.float32
    )
    row_dot = jnp.sum(weights_full * grad_weights, axis=-1, keepdims=True)
    grad_scores = (weights_full * (grad_weights - row_dot) * scaling).astype(jnp.bfloat16)
    grad_queries = jnp.einsum(
        "rhqk,rkhe->rqhe", grad_scores, keys_in, preferred_element_type=jnp.float32
    )
    grad_keys = jnp.einsum(
        "rhqk,rqhe->rkhe", grad_scores, queries, preferred_element_type=jnp.float32
    )
    return (grad_queries, grad_keys, grad_values)


def block_pass(tokens_in, cot_in, seg_rows, qkv_mat, out_mat, fc_mat, proj_mat, vec_rows):
    count_tok = tokens_in.shape[0]
    width = tokens_in.shape[1]
    head_width = width // HEADS
    row_count = count_tok // SEQ
    split_shape = (row_count, SEQ, HEADS, head_width)
    tokens32 = tokens_in.astype(jnp.float32)
    normed_one = layer_norm(tokens32, vec_rows[0], vec_rows[1]).astype(jnp.bfloat16)
    projected = jnp.dot(normed_one, qkv_mat, preferred_element_type=jnp.float32)
    queries = (projected[:, :width] + vec_rows[2]).astype(jnp.bfloat16).reshape(split_shape)
    keys_in = projected[:, width : 2 * width].astype(jnp.bfloat16).reshape(split_shape)
    values = (projected[:, 2 * width :] + vec_rows[3]).astype(jnp.bfloat16).reshape(split_shape)
    attended, log_total = attention_forward(queries, keys_in, values, seg_rows)
    attended = attended.reshape(count_tok, width)
    middle = tokens32 + jnp.dot(attended, out_mat, preferred_element_type=jnp.float32) + vec_rows[4]
    normed_two = layer_norm(middle, vec_rows[5], vec_rows[6]).astype(jnp.bfloat16)
    fc_bias = vec_rows[8:].reshape(-1)
    hidden_pre = jnp.dot(normed_two, fc_mat, preferred_element_type=jnp.float32) + fc_bias
    hidden = gelu_tanh(hidden_pre).astype(jnp.bfloat16)
    block_out = (
        middle + jnp.dot(hidden, proj_mat, preferred_element_type=jnp.float32) + vec_rows[7]
    ).astype(jnp.bfloat16)
    cot32 = cot_in.astype(jnp.float32)
    grad_proj = jnp.dot(hidden.T, cot_in, preferred_element_type=jnp.float32).astype(jnp.bfloat16)
    grad_proj, cot_in, hidden_pre, middle = lax.optimization_barrier(
        (grad_proj, cot_in, hidden_pre, middle)
    )
    grad_hidden = jnp.dot(cot_in, proj_mat.T, preferred_element_type=jnp.float32)
    gelu_back = jax.vjp(gelu_tanh, hidden_pre)[1]
    grad_pre = gelu_back(grad_hidden)[0]
    grad_pre_half = grad_pre.astype(jnp.bfloat16)
    grad_fc = jnp.dot(normed_two.T, grad_pre_half, preferred_element_type=jnp.float32)
    grad_normed_two = jnp.dot(grad_pre_half, fc_mat.T, preferred_element_type=jnp.float32)
    norm_two_back = jax.vjp(layer_norm, middle, vec_rows[5], vec_rows[6])[1]
    grad_mid_norm, grad_gain_two, grad_bias_two = norm_two_back(grad_normed_two)
    grad_middle = cot32 + grad_mid_norm
    grad_middle_half = grad_middle.astype(jnp.bfloat16)
    grad_out = jnp.dot(attended.T, grad_middle_half, preferred_element_type=jnp.float32)
    grad_attended = jnp.dot(grad_middle_half, out_mat.T, preferred_element_type=jnp.float32)
    grad_attended = grad_attended.astype(jnp.bfloat16).reshape(split_shape)
    grad_queries, grad_keys, grad_values = attention_backward(
        queries, keys_in, values, seg_rows, log_total, grad_attended
    )
    flat_queries = grad_queries.reshape(count_tok, width)
    flat_keys = grad_keys.reshape(count_tok, width)
    flat_values = grad_values.reshape(count_tok, width)
    grad_projected = jnp.concatenate([flat_queries, flat_keys, flat_values], axis=1).astype(
        jnp.bfloat16
    )
    grad_qkv = jnp.dot(normed_one.T, grad_projected, preferred_element_type=jnp.float32)
    grad_normed_one = jnp.dot(grad_projected, qkv_mat.T, preferred_element_type=jnp.float32)
    norm_one_back = jax.vjp(layer_norm, tokens32, vec_rows[0], vec_rows[1])[1]
    grad_tok_norm, grad_gain_one, grad_bias_one = norm_one_back(grad_normed_one)
    input_grad = (grad_middle + grad_tok_norm).astype(jnp.bfloat16)
    small_rows = jnp.stack(
        [
            grad_gain_one,
            grad_bias_one,
            jnp.sum(flat_queries, axis=0),
            jnp.sum(flat_values, axis=0),
            jnp.sum(grad_middle, axis=0),
            grad_gain_two,
            grad_bias_two,
            jnp.sum(cot32, axis=0),
        ]
    )
    grad_vec = jnp.concatenate([small_rows, jnp.sum(grad_pre, axis=0).reshape(-1, width)], axis=0)
    return (block_out, input_grad, (grad_qkv, grad_out, grad_fc, grad_proj, grad_vec))


def adam_step(weight, gradient, mean_old, square_old, rate, decay):
    mean_new = beta_first * mean_old + (1.0 - beta_first) * gradient
    square_new = beta_second * square_old + (1.0 - beta_second) * gradient * gradient
    mean_hat = mean_new / (1.0 - beta_first**ADAM_STEP)
    square_hat = square_new / (1.0 - beta_second**ADAM_STEP)
    weight_new = weight - rate * (mean_hat / (jnp.sqrt(square_hat) + eps_adam) + decay * weight)
    return (weight_new, mean_new, square_new)


def local(
    tokens,
    cotangent,
    segments,
    w_qkv,
    w_out,
    w_fc,
    w_proj,
    vectors,
    mean_qkv,
    mean_out,
    mean_fc,
    mean_proj,
    mean_vectors,
    square_qkv,
    square_out,
    square_fc,
    square_proj,
    square_vectors,
):
    dp_size = lax.axis_size("dp")
    zero_size = lax.axis_size("zero")
    replicas = dp_size * zero_size
    vec_cols = jnp.pad(vectors.astype(jnp.bfloat16).T, ((0, 0), (0, LANE - vectors.shape[0])))
    first_mats = (w_qkv.astype(jnp.bfloat16), w_out.astype(jnp.bfloat16), w_fc.astype(jnp.bfloat16), vec_cols)
    first_all = lax.all_gather(jnp.concatenate(first_mats, axis=1), "zero", axis=0, tiled=True)
    first_all, proj_shard = lax.optimization_barrier((first_all, w_proj.astype(jnp.bfloat16)))
    proj_mat = lax.all_gather(proj_shard, "zero", axis=0, tiled=True)
    widths = [m.shape[1] for m in first_mats]
    qkv_mat, out_mat, fc_mat, vec_cols_all = jnp.split(
        first_all, [sum(widths[:k]) for k in range(1, len(widths))], axis=1
    )
    vec_rows = vec_cols_all[:, : vectors.shape[0]].T.astype(jnp.float32)
    block_out, input_grad, local_grads = block_pass(
        tokens, cotangent, segments, qkv_mat, out_mat, fc_mat, proj_mat, vec_rows
    )
    grad_vec_cols = jnp.pad(
        local_grads[4].astype(jnp.bfloat16).T, ((0, 0), (0, LANE - vectors.shape[0]))
    )
    joined = jnp.concatenate(
        (
            local_grads[0].astype(jnp.bfloat16),
            local_grads[1].astype(jnp.bfloat16),
            local_grads[2].astype(jnp.bfloat16),
            grad_vec_cols,
        ),
        axis=1,
    )
    scattered = lax.psum_scatter(joined, "zero", scatter_dimension=0, tiled=True)
    proj_scattered = lax.psum_scatter(
        local_grads[3].astype(jnp.bfloat16), "zero", scatter_dimension=0, tiled=True
    )
    summed_joined, summed_proj = lax.psum((scattered, proj_scattered), "dp")
    ends = [w_qkv.shape[1], w_qkv.shape[1] + w_out.shape[1], w_qkv.shape[1] + w_out.shape[1] + w_fc.shape[1]]
    g_qkv, g_out, g_fc, g_vec = jnp.split(summed_joined, ends, axis=1)
    summed = (
        g_qkv.astype(jnp.float32),
        g_out.astype(jnp.float32),
        g_fc.astype(jnp.float32),
        summed_proj.astype(jnp.float32),
        lax.dot_general(
            g_vec[:, : vectors.shape[0]],
            jnp.eye(g_vec.shape[0], dtype=jnp.bfloat16),
            (((0,), (0,)), ((), ())),
            preferred_element_type=jnp.float32,
        ),
    )
    grads = jax.tree.map(partial(jnp.multiply, 1.0 / replicas), summed)
    first = adam_step(w_qkv, grads[0], mean_qkv, square_qkv, rate_matrix, decay_matrix)
    second = adam_step(w_out, grads[1], mean_out, square_out, rate_matrix, decay_matrix)
    third = adam_step(w_fc, grads[2], mean_fc, square_fc, rate_matrix, decay_matrix)
    fourth = adam_step(w_proj, grads[3], mean_proj, square_proj, rate_matrix, decay_matrix)
    fifth = adam_step(vectors, grads[4], mean_vectors, square_vectors, rate_vector, 0.0)
    return (
        block_out,
        input_grad,
        grads[0],
        grads[1],
        grads[2],
        grads[3],
        grads[4],
        first[0],
        second[0],
        third[0],
        fourth[0],
        fifth[0],
        first[1],
        second[1],
        third[1],
        fourth[1],
        fifth[1],
        first[2],
        second[2],
        third[2],
        fourth[2],
        fifth[2],
    )


def solution(mesh):
    placed = (
        P(("dp", "zero"), None),
        P(("dp", "zero"), None),
        P(("dp", "zero"), None),
        P("zero", None),
        P("zero", None),
        P("zero", None),
        P("zero", None),
        P(None, "zero"),
        P("zero", None),
        P("zero", None),
        P("zero", None),
        P("zero", None),
        P(None, "zero"),
        P("zero", None),
        P("zero", None),
        P("zero", None),
        P("zero", None),
        P(None, "zero"),
    )
    return jax.shard_map(
        local,
        mesh=mesh,
        in_specs=placed,
        out_specs=(
            P(("dp", "zero"), None),
            P(("dp", "zero"), None),
            P("zero", None),
            P("zero", None),
            P("zero", None),
            P("zero", None),
            P(None, "zero"),
            P("zero", None),
            P("zero", None),
            P("zero", None),
            P("zero", None),
            P(None, "zero"),
            P("zero", None),
            P("zero", None),
            P("zero", None),
            P("zero", None),
            P(None, "zero"),
            P("zero", None),
            P("zero", None),
            P("zero", None),
            P("zero", None),
            P(None, "zero"),
        ),
        check_vma=False,
    )
```

```python
from functools import partial

import jax
import jax.numpy as jnp
from jax import lax
from jax.experimental import pallas as pl
from jax.experimental.pallas import tpu as pltpu
from jax.sharding import PartitionSpec as P

HEADS = 16
SEQ = 128
ADAM_STEP = 3
LANE = 128


eps_norm = 1e-05
beta_first = 0.9
beta_second = 0.999
eps_adam = 1e-08
rate_matrix = 0.02
rate_vector = 0.15
decay_matrix = 0.1


def sent_together(arrays, axis, dim, along):
    widths = [a.shape[along] for a in arrays]
    both = jnp.concatenate(arrays, axis=along)
    result = lax.all_gather(both, axis, axis=dim, tiled=True)
    return tuple(jnp.split(result, [sum(widths[:k]) for k in range(1, len(widths))], axis=along))


def in_one_piece(arrays, axis, dim, along):
    ends, at = ([], 0)
    for a in arrays[:-1]:
        at += a.shape[along]
        ends.append(at)
    both = jnp.concatenate(arrays, axis=along)
    return tuple(
        jnp.split(lax.psum_scatter(both, axis, scatter_dimension=dim, tiled=True), ends, axis=along)
    )


def dp_sum_kernel(parts, x_ref, out_ref, recv_one, recv_two, mine, send_one, got_one, send_two, got_two):
    me = lax.axis_index("dp")
    shard = lax.axis_index("zero")
    rows = recv_one.shape[1]
    barrier = pltpu.get_barrier_semaphore()
    for k in range(1, parts):
        pl.semaphore_signal(
            barrier, inc=1, device_id=(lax.rem(me + k, parts), shard),
            device_id_type=pl.DeviceIdType.MESH,
        )
    pl.semaphore_wait(barrier, parts - 1)
    first = []
    for k in range(1, parts):
        peer = lax.rem(me + k, parts)
        copy = pltpu.make_async_remote_copy(
            src_ref=x_ref.at[pl.ds(pl.multiple_of(peer * rows, rows), rows)],
            dst_ref=recv_one.at[k],
            send_sem=send_one.at[k],
            recv_sem=got_one.at[k],
            device_id=(peer, shard),
            device_id_type=pl.DeviceIdType.MESH,
        )
        copy.start()
        first.append(copy)
    total = x_ref[pl.ds(pl.multiple_of(me * rows, rows), rows), :].astype(jnp.float32)
    for k, copy in enumerate(first, start=1):
        copy.wait_recv()
        total = total + recv_one[k].astype(jnp.float32)
    mine[...] = total.astype(mine.dtype)
    out_ref[pl.ds(pl.multiple_of(me * rows, rows), rows), :] = mine[...]
    second = []
    for k in range(1, parts):
        peer = lax.rem(me + k, parts)
        copy = pltpu.make_async_remote_copy(
            src_ref=mine,
            dst_ref=recv_two.at[k],
            send_sem=send_two.at[k],
            recv_sem=got_two.at[k],
            device_id=(peer, shard),
            device_id_type=pl.DeviceIdType.MESH,
        )
        copy.start()
        second.append(copy)
    for copy in first:
        copy.wait_send()
    for k, copy in enumerate(second, start=1):
        copy.wait_recv()
        source = lax.rem(me + parts - k, parts)
        out_ref[pl.ds(pl.multiple_of(source * rows, rows), rows), :] = recv_two[k]
    for copy in second:
        copy.wait_send()


def dp_sum(packed, parts):
    rows = packed.shape[0] // parts
    return pl.pallas_call(
        partial(dp_sum_kernel, parts),
        out_shape=jax.ShapeDtypeStruct(packed.shape, packed.dtype),
        in_specs=[pl.BlockSpec(memory_space=pltpu.VMEM)],
        out_specs=pl.BlockSpec(memory_space=pltpu.VMEM),
        scratch_shapes=[
            pltpu.VMEM((parts, rows, packed.shape[1]), packed.dtype),
            pltpu.VMEM((parts, rows, packed.shape[1]), packed.dtype),
            pltpu.VMEM((rows, packed.shape[1]), packed.dtype),
            pltpu.SemaphoreType.DMA((parts,)),
            pltpu.SemaphoreType.DMA((parts,)),
            pltpu.SemaphoreType.DMA((parts,)),
            pltpu.SemaphoreType.DMA((parts,)),
        ],
        compiler_params=pltpu.CompilerParams(collective_id=0, has_side_effects=True),
    )(packed)


def summed_over_dp(arrays):
    parts = lax.axis_size("dp")
    flat = [a.reshape(-1, LANE) for a in arrays]
    count = sum(f.shape[0] for f in flat)
    step = parts * 16
    padded = -(-count // step) * step
    packed = jnp.concatenate(flat + [jnp.zeros((padded - count, LANE), arrays[0].dtype)], axis=0)
    result = dp_sum(packed, parts)
    outs, at = [], 0
    for a, f in zip(arrays, flat):
        outs.append(result[at : at + f.shape[0]].reshape(a.shape))
        at += f.shape[0]
    return outs


def gelu_tanh(inputs):
    inner = 0.7978845608028654 * (inputs + 0.044715 * inputs * inputs * inputs)
    return 0.5 * inputs * (1.0 + jnp.tanh(inner))


def layer_norm(inputs, gain_row, bias_row):
    average = jnp.mean(inputs, axis=-1, keepdims=True)
    centred = inputs - average
    variance = jnp.mean(centred * centred, axis=-1, keepdims=True)
    return centred * lax.rsqrt(variance + eps_norm) * gain_row + bias_row


def allowed_mask(seg_rows):
    length = seg_rows.shape[1]
    places = lax.iota(jnp.int32, length)
    causal = places[:, None] >= places[None, :]
    same_doc = seg_rows[:, :, None] == seg_rows[:, None, :]
    return jnp.logical_and(same_doc, causal[None])[:, None]


def attend_scores(queries, keys_in, seg_rows):
    scaling = queries.shape[-1] ** (-0.5)
    scores = (
        jnp.einsum("rqhe,rkhe->rhqk", queries, keys_in, preferred_element_type=jnp.float32)
        * scaling
    )
    return (scores, allowed_mask(seg_rows), scaling)


def attention_forward(queries, keys_in, values, seg_rows):
    scores, allowed, scaling = attend_scores(queries, keys_in, seg_rows)
    exponent = jnp.where(allowed, jnp.exp(scores), 0.0)
    log_total = jnp.log(jnp.sum(exponent, axis=-1, keepdims=True))
    attn_weights = jnp.where(allowed, jnp.exp(scores - log_total), 0.0).astype(jnp.bfloat16)
    attended = jnp.einsum(
        "rhqk,rkhe->rqhe", attn_weights, values, preferred_element_type=jnp.float32
    )
    return (attended.astype(jnp.bfloat16), log_total)


def attention_backward(queries, keys_in, values, seg_rows, log_total, grad_att):
    scores, allowed, scaling = attend_scores(queries, keys_in, seg_rows)
    weights_full = jnp.where(allowed, jnp.exp(scores - log_total), 0.0)
    weights_half = weights_full.astype(jnp.bfloat16)
    grad_values = jnp.einsum(
        "rhqk,rqhe->rkhe", weights_half, grad_att, preferred_element_type=jnp.float32
    )
    grad_weights = jnp.einsum(
        "rqhe,rkhe->rhqk", grad_att, values, preferred_element_type=jnp.float32
    )
    row_dot = jnp.sum(weights_full * grad_weights, axis=-1, keepdims=True)
    grad_scores = (weights_full * (grad_weights - row_dot) * scaling).astype(jnp.bfloat16)
    grad_queries = jnp.einsum(
        "rhqk,rkhe->rqhe", grad_scores, keys_in, preferred_element_type=jnp.float32
    )
    grad_keys = jnp.einsum(
        "rhqk,rqhe->rkhe", grad_scores, queries, preferred_element_type=jnp.float32
    )
    return (grad_queries, grad_keys, grad_values)


def block_pass(tokens_in, cot_in, seg_rows, qkv_mat, out_mat, fc_mat, proj_mat, vec_rows):
    count_tok = tokens_in.shape[0]
    width = tokens_in.shape[1]
    head_width = width // HEADS
    row_count = count_tok // SEQ
    split_shape = (row_count, SEQ, HEADS, head_width)
    tokens32 = tokens_in.astype(jnp.float32)
    normed_one = layer_norm(tokens32, vec_rows[0], vec_rows[1]).astype(jnp.bfloat16)
    projected = jnp.dot(normed_one, qkv_mat, preferred_element_type=jnp.float32)
    queries = (projected[:, :width] + vec_rows[2]).astype(jnp.bfloat16).reshape(split_shape)
    keys_in = projected[:, width : 2 * width].astype(jnp.bfloat16).reshape(split_shape)
    values = (projected[:, 2 * width :] + vec_rows[3]).astype(jnp.bfloat16).reshape(split_shape)
    attended, log_total = attention_forward(queries, keys_in, values, seg_rows)
    attended = attended.reshape(count_tok, width)
    middle = tokens32 + jnp.dot(attended, out_mat, preferred_element_type=jnp.float32) + vec_rows[4]
    normed_two = layer_norm(middle, vec_rows[5], vec_rows[6]).astype(jnp.bfloat16)
    fc_bias = vec_rows[8:].reshape(-1)
    hidden_pre = jnp.dot(normed_two, fc_mat, preferred_element_type=jnp.float32) + fc_bias
    hidden = gelu_tanh(hidden_pre).astype(jnp.bfloat16)
    block_out = (
        middle + jnp.dot(hidden, proj_mat, preferred_element_type=jnp.float32) + vec_rows[7]
    ).astype(jnp.bfloat16)
    cot32 = cot_in.astype(jnp.float32)
    grad_proj = jnp.dot(hidden.T, cot_in, preferred_element_type=jnp.float32).astype(jnp.bfloat16)
    grad_proj, cot_in, hidden_pre, middle = lax.optimization_barrier(
        (grad_proj, cot_in, hidden_pre, middle)
    )
    grad_hidden = jnp.dot(cot_in, proj_mat.T, preferred_element_type=jnp.float32)
    gelu_back = jax.vjp(gelu_tanh, hidden_pre)[1]
    grad_pre = gelu_back(grad_hidden)[0]
    grad_pre_half = grad_pre.astype(jnp.bfloat16)
    grad_fc = jnp.dot(normed_two.T, grad_pre_half, preferred_element_type=jnp.float32)
    grad_normed_two = jnp.dot(grad_pre_half, fc_mat.T, preferred_element_type=jnp.float32)
    norm_two_back = jax.vjp(layer_norm, middle, vec_rows[5], vec_rows[6])[1]
    grad_mid_norm, grad_gain_two, grad_bias_two = norm_two_back(grad_normed_two)
    grad_middle = cot32 + grad_mid_norm
    grad_middle_half = grad_middle.astype(jnp.bfloat16)
    grad_out = jnp.dot(attended.T, grad_middle_half, preferred_element_type=jnp.float32)
    grad_attended = jnp.dot(grad_middle_half, out_mat.T, preferred_element_type=jnp.float32)
    grad_attended = grad_attended.astype(jnp.bfloat16).reshape(split_shape)
    grad_queries, grad_keys, grad_values = attention_backward(
        queries, keys_in, values, seg_rows, log_total, grad_attended
    )
    flat_queries = grad_queries.reshape(count_tok, width)
    flat_keys = grad_keys.reshape(count_tok, width)
    flat_values = grad_values.reshape(count_tok, width)
    grad_projected = jnp.concatenate([flat_queries, flat_keys, flat_values], axis=1).astype(
        jnp.bfloat16
    )
    grad_qkv = jnp.dot(normed_one.T, grad_projected, preferred_element_type=jnp.float32)
    grad_normed_one = jnp.dot(grad_projected, qkv_mat.T, preferred_element_type=jnp.float32)
    norm_one_back = jax.vjp(layer_norm, tokens32, vec_rows[0], vec_rows[1])[1]
    grad_tok_norm, grad_gain_one, grad_bias_one = norm_one_back(grad_normed_one)
    input_grad = (grad_middle + grad_tok_norm).astype(jnp.bfloat16)
    small_rows = jnp.stack(
        [
            grad_gain_one,
            grad_bias_one,
            jnp.sum(flat_queries, axis=0),
            jnp.sum(flat_values, axis=0),
            jnp.sum(grad_middle, axis=0),
            grad_gain_two,
            grad_bias_two,
            jnp.sum(cot32, axis=0),
        ]
    )
    grad_vec = jnp.concatenate([small_rows, jnp.sum(grad_pre, axis=0).reshape(-1, width)], axis=0)
    return (block_out, input_grad, (grad_qkv, grad_out, grad_fc, grad_proj, grad_vec))


def adam_step(weight, gradient, mean_old, square_old, rate, decay):
    mean_new = beta_first * mean_old + (1.0 - beta_first) * gradient
    square_new = beta_second * square_old + (1.0 - beta_second) * gradient * gradient
    mean_hat = mean_new / (1.0 - beta_first**ADAM_STEP)
    square_hat = square_new / (1.0 - beta_second**ADAM_STEP)
    weight_new = weight - rate * (mean_hat / (jnp.sqrt(square_hat) + eps_adam) + decay * weight)
    return (weight_new, mean_new, square_new)


def local(
    tokens,
    cotangent,
    segments,
    w_qkv,
    w_out,
    w_fc,
    w_proj,
    vectors,
    mean_qkv,
    mean_out,
    mean_fc,
    mean_proj,
    mean_vectors,
    square_qkv,
    square_out,
    square_fc,
    square_proj,
    square_vectors,
):
    dp_size = lax.axis_size("dp")
    zero_size = lax.axis_size("zero")
    replicas = dp_size * zero_size
    vec_cols = jnp.pad(vectors.astype(jnp.bfloat16).T, ((0, 0), (0, LANE - vectors.shape[0])))
    first_mats = (w_qkv.astype(jnp.bfloat16), w_out.astype(jnp.bfloat16), w_fc.astype(jnp.bfloat16), vec_cols)
    first_all = lax.all_gather(jnp.concatenate(first_mats, axis=1), "zero", axis=0, tiled=True)
    first_all, proj_shard = lax.optimization_barrier((first_all, w_proj.astype(jnp.bfloat16)))
    proj_mat = lax.all_gather(proj_shard, "zero", axis=0, tiled=True)
    widths = [m.shape[1] for m in first_mats]
    qkv_mat, out_mat, fc_mat, vec_cols_all = jnp.split(
        first_all, [sum(widths[:k]) for k in range(1, len(widths))], axis=1
    )
    vec_rows = vec_cols_all[:, : vectors.shape[0]].T.astype(jnp.float32)
    block_out, input_grad, local_grads = block_pass(
        tokens, cotangent, segments, qkv_mat, out_mat, fc_mat, proj_mat, vec_rows
    )
    grad_vec_cols = jnp.pad(
        local_grads[4].astype(jnp.bfloat16).T, ((0, 0), (0, LANE - vectors.shape[0]))
    )
    joined = jnp.concatenate(
        (
            local_grads[0].astype(jnp.bfloat16),
            local_grads[1].astype(jnp.bfloat16),
            local_grads[2].astype(jnp.bfloat16),
            grad_vec_cols,
        ),
        axis=1,
    )
    scattered = lax.psum_scatter(joined, "zero", scatter_dimension=0, tiled=True)
    proj_scattered = lax.psum_scatter(
        local_grads[3].astype(jnp.bfloat16), "zero", scatter_dimension=0, tiled=True
    )
    summed_joined, summed_proj = summed_over_dp((scattered, proj_scattered))
    ends = [w_qkv.shape[1], w_qkv.shape[1] + w_out.shape[1], w_qkv.shape[1] + w_out.shape[1] + w_fc.shape[1]]
    g_qkv, g_out, g_fc, g_vec = jnp.split(summed_joined, ends, axis=1)
    summed = (
        g_qkv.astype(jnp.float32),
        g_out.astype(jnp.float32),
        g_fc.astype(jnp.float32),
        summed_proj.astype(jnp.float32),
        lax.dot_general(
            g_vec[:, : vectors.shape[0]],
            jnp.eye(g_vec.shape[0], dtype=jnp.bfloat16),
            (((0,), (0,)), ((), ())),
            preferred_element_type=jnp.float32,
        ),
    )
    grads = jax.tree.map(partial(jnp.multiply, 1.0 / replicas), summed)
    first = adam_step(w_qkv, grads[0], mean_qkv, square_qkv, rate_matrix, decay_matrix)
    second = adam_step(w_out, grads[1], mean_out, square_out, rate_matrix, decay_matrix)
    third = adam_step(w_fc, grads[2], mean_fc, square_fc, rate_matrix, decay_matrix)
    fourth = adam_step(w_proj, grads[3], mean_proj, square_proj, rate_matrix, decay_matrix)
    fifth = adam_step(vectors, grads[4], mean_vectors, square_vectors, rate_vector, 0.0)
    return (
        block_out,
        input_grad,
        grads[0],
        grads[1],
        grads[2],
        grads[3],
        grads[4],
        first[0],
        second[0],
        third[0],
        fourth[0],
        fifth[0],
        first[1],
        second[1],
        third[1],
        fourth[1],
        fifth[1],
        first[2],
        second[2],
        third[2],
        fourth[2],
        fifth[2],
    )


def solution(mesh):
    placed = (
        P(("dp", "zero"), None),
        P(("dp", "zero"), None),
        P(("dp", "zero"), None),
        P("zero", None),
        P("zero", None),
        P("zero", None),
        P("zero", None),
        P(None, "zero"),
        P("zero", None),
        P("zero", None),
        P("zero", None),
        P("zero", None),
        P(None, "zero"),
        P("zero", None),
        P("zero", None),
        P("zero", None),
        P("zero", None),
        P(None, "zero"),
    )
    return jax.shard_map(
        local,
        mesh=mesh,
        in_specs=placed,
        out_specs=(
            P(("dp", "zero"), None),
            P(("dp", "zero"), None),
            P("zero", None),
            P("zero", None),
            P("zero", None),
            P("zero", None),
            P(None, "zero"),
            P("zero", None),
            P("zero", None),
            P("zero", None),
            P("zero", None),
            P(None, "zero"),
            P("zero", None),
            P("zero", None),
            P("zero", None),
            P("zero", None),
            P(None, "zero"),
            P("zero", None),
            P("zero", None),
            P("zero", None),
            P("zero", None),
            P(None, "zero"),
        ),
        check_vma=False,
    )
```

```python
from functools import partial

import jax
import jax.numpy as jnp
from jax import lax
from jax.experimental import pallas as pl
from jax.experimental.pallas import tpu as pltpu
from jax.sharding import PartitionSpec as P

HEADS = 16
SEQ = 128
ADAM_STEP = 3
LANE = 128


eps_norm = 1e-05
beta_first = 0.9
beta_second = 0.999
eps_adam = 1e-08
rate_matrix = 0.02
rate_vector = 0.15
decay_matrix = 0.1


def sent_together(arrays, axis, dim, along):
    widths = [a.shape[along] for a in arrays]
    both = jnp.concatenate(arrays, axis=along)
    result = lax.all_gather(both, axis, axis=dim, tiled=True)
    return tuple(jnp.split(result, [sum(widths[:k]) for k in range(1, len(widths))], axis=along))


def in_one_piece(arrays, axis, dim, along):
    ends, at = ([], 0)
    for a in arrays[:-1]:
        at += a.shape[along]
        ends.append(at)
    both = jnp.concatenate(arrays, axis=along)
    return tuple(
        jnp.split(lax.psum_scatter(both, axis, scatter_dimension=dim, tiled=True), ends, axis=along)
    )


def dp_sum_kernel(parts, count, *refs):
    x_refs, out_refs = refs[:count], refs[count : 2 * count]
    recv_one, recv_two = refs[2 * count : 3 * count], refs[3 * count : 4 * count]
    mine = refs[4 * count : 5 * count]
    send_one, got_one, send_two, got_two = refs[5 * count :]
    me = lax.axis_index("dp")
    shard = lax.axis_index("zero")
    barrier = pltpu.get_barrier_semaphore()
    for k in range(1, parts):
        pl.semaphore_signal(
            barrier, inc=1, device_id=(lax.rem(me + k, parts), shard),
            device_id_type=pl.DeviceIdType.MESH,
        )
    pl.semaphore_wait(barrier, parts - 1)

    def send(sources, targets, sends, gots, pick):
        copies = []
        for k in range(1, parts):
            peer = lax.rem(me + k, parts)
            for i in range(count):
                copy = pltpu.make_async_remote_copy(
                    src_ref=pick(sources[i], peer),
                    dst_ref=targets[i].at[k],
                    send_sem=sends.at[i, k],
                    recv_sem=gots.at[i, k],
                    device_id=(peer, shard),
                    device_id_type=pl.DeviceIdType.MESH,
                )
                copy.start()
                copies.append(copy)
        return copies

    first = send(x_refs, recv_one, send_one, got_one, lambda ref, peer: ref.at[peer])
    totals = [x_refs[i][me].astype(jnp.float32) for i in range(count)]
    for n, copy in enumerate(first):
        copy.wait_recv()
        k, i = n // count + 1, n % count
        totals[i] = totals[i] + recv_one[i][k].astype(jnp.float32)
    for i in range(count):
        mine[i][...] = totals[i].astype(mine[i].dtype)
        out_refs[i][me] = mine[i][...]
    second = send(mine, recv_two, send_two, got_two, lambda ref, peer: ref)
    for copy in first:
        copy.wait_send()
    for n, copy in enumerate(second):
        copy.wait_recv()
        k, i = n // count + 1, n % count
        out_refs[i][lax.rem(me + parts - k, parts)] = recv_two[i][k]
    for copy in second:
        copy.wait_send()


def summed_over_dp(arrays):
    parts = lax.axis_size("dp")
    count = len(arrays)
    stacked = [a.reshape((parts, a.shape[0] // parts) + a.shape[1:]) for a in arrays]
    vmem = pl.BlockSpec(memory_space=pltpu.VMEM)
    results = pl.pallas_call(
        partial(dp_sum_kernel, parts, count),
        out_shape=[jax.ShapeDtypeStruct(s.shape, s.dtype) for s in stacked],
        in_specs=[vmem] * count,
        out_specs=[vmem] * count,
        scratch_shapes=[pltpu.VMEM(s.shape, s.dtype) for s in stacked] * 2
        + [pltpu.VMEM(s.shape[1:], s.dtype) for s in stacked]
        + [pltpu.SemaphoreType.DMA((count, parts))] * 4,
        compiler_params=pltpu.CompilerParams(collective_id=0, has_side_effects=True),
    )(*stacked)
    return [r.reshape(a.shape) for r, a in zip(results, arrays)]


def gelu_tanh(inputs):
    inner = 0.7978845608028654 * (inputs + 0.044715 * inputs * inputs * inputs)
    return 0.5 * inputs * (1.0 + jnp.tanh(inner))


def layer_norm(inputs, gain_row, bias_row):
    average = jnp.mean(inputs, axis=-1, keepdims=True)
    centred = inputs - average
    variance = jnp.mean(centred * centred, axis=-1, keepdims=True)
    return centred * lax.rsqrt(variance + eps_norm) * gain_row + bias_row


def allowed_mask(seg_rows):
    length = seg_rows.shape[1]
    places = lax.iota(jnp.int32, length)
    causal = places[:, None] >= places[None, :]
    same_doc = seg_rows[:, :, None] == seg_rows[:, None, :]
    return jnp.logical_and(same_doc, causal[None])[:, None]


def attend_scores(queries, keys_in, seg_rows):
    scaling = queries.shape[-1] ** (-0.5)
    scores = (
        jnp.einsum("rqhe,rkhe->rhqk", queries, keys_in, preferred_element_type=jnp.float32)
        * scaling
    )
    return (scores, allowed_mask(seg_rows), scaling)


def attention_forward(queries, keys_in, values, seg_rows):
    scores, allowed, scaling = attend_scores(queries, keys_in, seg_rows)
    exponent = jnp.where(allowed, jnp.exp(scores), 0.0)
    log_total = jnp.log(jnp.sum(exponent, axis=-1, keepdims=True))
    attn_weights = jnp.where(allowed, jnp.exp(scores - log_total), 0.0).astype(jnp.bfloat16)
    attended = jnp.einsum(
        "rhqk,rkhe->rqhe", attn_weights, values, preferred_element_type=jnp.float32
    )
    return (attended.astype(jnp.bfloat16), log_total)


def attention_backward(queries, keys_in, values, seg_rows, log_total, grad_att):
    scores, allowed, scaling = attend_scores(queries, keys_in, seg_rows)
    weights_full = jnp.where(allowed, jnp.exp(scores - log_total), 0.0)
    weights_half = weights_full.astype(jnp.bfloat16)
    grad_values = jnp.einsum(
        "rhqk,rqhe->rkhe", weights_half, grad_att, preferred_element_type=jnp.float32
    )
    grad_weights = jnp.einsum(
        "rqhe,rkhe->rhqk", grad_att, values, preferred_element_type=jnp.float32
    )
    row_dot = jnp.sum(weights_full * grad_weights, axis=-1, keepdims=True)
    grad_scores = (weights_full * (grad_weights - row_dot) * scaling).astype(jnp.bfloat16)
    grad_queries = jnp.einsum(
        "rhqk,rkhe->rqhe", grad_scores, keys_in, preferred_element_type=jnp.float32
    )
    grad_keys = jnp.einsum(
        "rhqk,rqhe->rkhe", grad_scores, queries, preferred_element_type=jnp.float32
    )
    return (grad_queries, grad_keys, grad_values)


def block_pass(tokens_in, cot_in, seg_rows, qkv_mat, out_mat, fc_mat, proj_mat, vec_rows):
    count_tok = tokens_in.shape[0]
    width = tokens_in.shape[1]
    head_width = width // HEADS
    row_count = count_tok // SEQ
    split_shape = (row_count, SEQ, HEADS, head_width)
    tokens32 = tokens_in.astype(jnp.float32)
    normed_one = layer_norm(tokens32, vec_rows[0], vec_rows[1]).astype(jnp.bfloat16)
    projected = jnp.dot(normed_one, qkv_mat, preferred_element_type=jnp.float32)
    queries = (projected[:, :width] + vec_rows[2]).astype(jnp.bfloat16).reshape(split_shape)
    keys_in = projected[:, width : 2 * width].astype(jnp.bfloat16).reshape(split_shape)
    values = (projected[:, 2 * width :] + vec_rows[3]).astype(jnp.bfloat16).reshape(split_shape)
    attended, log_total = attention_forward(queries, keys_in, values, seg_rows)
    attended = attended.reshape(count_tok, width)
    middle = tokens32 + jnp.dot(attended, out_mat, preferred_element_type=jnp.float32) + vec_rows[4]
    normed_two = layer_norm(middle, vec_rows[5], vec_rows[6]).astype(jnp.bfloat16)
    fc_bias = vec_rows[8:].reshape(-1)
    hidden_pre = jnp.dot(normed_two, fc_mat, preferred_element_type=jnp.float32) + fc_bias
    hidden = gelu_tanh(hidden_pre).astype(jnp.bfloat16)
    block_out = (
        middle + jnp.dot(hidden, proj_mat, preferred_element_type=jnp.float32) + vec_rows[7]
    ).astype(jnp.bfloat16)
    cot32 = cot_in.astype(jnp.float32)
    grad_proj = jnp.dot(hidden.T, cot_in, preferred_element_type=jnp.float32).astype(jnp.bfloat16)
    grad_proj, cot_in, hidden_pre, middle = lax.optimization_barrier(
        (grad_proj, cot_in, hidden_pre, middle)
    )
    grad_hidden = jnp.dot(cot_in, proj_mat.T, preferred_element_type=jnp.float32)
    gelu_back = jax.vjp(gelu_tanh, hidden_pre)[1]
    grad_pre = gelu_back(grad_hidden)[0]
    grad_pre_half = grad_pre.astype(jnp.bfloat16)
    grad_fc = jnp.dot(normed_two.T, grad_pre_half, preferred_element_type=jnp.float32)
    grad_normed_two = jnp.dot(grad_pre_half, fc_mat.T, preferred_element_type=jnp.float32)
    norm_two_back = jax.vjp(layer_norm, middle, vec_rows[5], vec_rows[6])[1]
    grad_mid_norm, grad_gain_two, grad_bias_two = norm_two_back(grad_normed_two)
    grad_middle = cot32 + grad_mid_norm
    grad_middle_half = grad_middle.astype(jnp.bfloat16)
    grad_out = jnp.dot(attended.T, grad_middle_half, preferred_element_type=jnp.float32)
    grad_attended = jnp.dot(grad_middle_half, out_mat.T, preferred_element_type=jnp.float32)
    grad_attended = grad_attended.astype(jnp.bfloat16).reshape(split_shape)
    grad_queries, grad_keys, grad_values = attention_backward(
        queries, keys_in, values, seg_rows, log_total, grad_attended
    )
    flat_queries = grad_queries.reshape(count_tok, width)
    flat_keys = grad_keys.reshape(count_tok, width)
    flat_values = grad_values.reshape(count_tok, width)
    grad_projected = jnp.concatenate([flat_queries, flat_keys, flat_values], axis=1).astype(
        jnp.bfloat16
    )
    grad_qkv = jnp.dot(normed_one.T, grad_projected, preferred_element_type=jnp.float32)
    grad_normed_one = jnp.dot(grad_projected, qkv_mat.T, preferred_element_type=jnp.float32)
    norm_one_back = jax.vjp(layer_norm, tokens32, vec_rows[0], vec_rows[1])[1]
    grad_tok_norm, grad_gain_one, grad_bias_one = norm_one_back(grad_normed_one)
    input_grad = (grad_middle + grad_tok_norm).astype(jnp.bfloat16)
    small_rows = jnp.stack(
        [
            grad_gain_one,
            grad_bias_one,
            jnp.sum(flat_queries, axis=0),
            jnp.sum(flat_values, axis=0),
            jnp.sum(grad_middle, axis=0),
            grad_gain_two,
            grad_bias_two,
            jnp.sum(cot32, axis=0),
        ]
    )
    grad_vec = jnp.concatenate([small_rows, jnp.sum(grad_pre, axis=0).reshape(-1, width)], axis=0)
    return (block_out, input_grad, (grad_qkv, grad_out, grad_fc, grad_proj, grad_vec))


def adam_step(weight, gradient, mean_old, square_old, rate, decay):
    mean_new = beta_first * mean_old + (1.0 - beta_first) * gradient
    square_new = beta_second * square_old + (1.0 - beta_second) * gradient * gradient
    mean_hat = mean_new / (1.0 - beta_first**ADAM_STEP)
    square_hat = square_new / (1.0 - beta_second**ADAM_STEP)
    weight_new = weight - rate * (mean_hat / (jnp.sqrt(square_hat) + eps_adam) + decay * weight)
    return (weight_new, mean_new, square_new)


def local(
    tokens,
    cotangent,
    segments,
    w_qkv,
    w_out,
    w_fc,
    w_proj,
    vectors,
    mean_qkv,
    mean_out,
    mean_fc,
    mean_proj,
    mean_vectors,
    square_qkv,
    square_out,
    square_fc,
    square_proj,
    square_vectors,
):
    dp_size = lax.axis_size("dp")
    zero_size = lax.axis_size("zero")
    replicas = dp_size * zero_size
    vec_cols = jnp.pad(vectors.astype(jnp.bfloat16).T, ((0, 0), (0, LANE - vectors.shape[0])))
    first_mats = (w_qkv.astype(jnp.bfloat16), w_out.astype(jnp.bfloat16), w_fc.astype(jnp.bfloat16), vec_cols)
    first_all = lax.all_gather(jnp.concatenate(first_mats, axis=1), "zero", axis=0, tiled=True)
    first_all, proj_shard = lax.optimization_barrier((first_all, w_proj.astype(jnp.bfloat16)))
    proj_mat = lax.all_gather(proj_shard, "zero", axis=0, tiled=True)
    widths = [m.shape[1] for m in first_mats]
    qkv_mat, out_mat, fc_mat, vec_cols_all = jnp.split(
        first_all, [sum(widths[:k]) for k in range(1, len(widths))], axis=1
    )
    vec_rows = vec_cols_all[:, : vectors.shape[0]].T.astype(jnp.float32)
    block_out, input_grad, local_grads = block_pass(
        tokens, cotangent, segments, qkv_mat, out_mat, fc_mat, proj_mat, vec_rows
    )
    grad_vec_cols = jnp.pad(
        local_grads[4].astype(jnp.bfloat16).T, ((0, 0), (0, LANE - vectors.shape[0]))
    )
    joined = jnp.concatenate(
        (
            local_grads[0].astype(jnp.bfloat16),
            local_grads[1].astype(jnp.bfloat16),
            local_grads[2].astype(jnp.bfloat16),
            grad_vec_cols,
        ),
        axis=1,
    )
    scattered = lax.psum_scatter(joined, "zero", scatter_dimension=0, tiled=True)
    proj_scattered = lax.psum_scatter(
        local_grads[3].astype(jnp.bfloat16), "zero", scatter_dimension=0, tiled=True
    )
    summed_joined, summed_proj = summed_over_dp((scattered, proj_scattered))
    ends = [w_qkv.shape[1], w_qkv.shape[1] + w_out.shape[1], w_qkv.shape[1] + w_out.shape[1] + w_fc.shape[1]]
    g_qkv, g_out, g_fc, g_vec = jnp.split(summed_joined, ends, axis=1)
    summed = (
        g_qkv.astype(jnp.float32),
        g_out.astype(jnp.float32),
        g_fc.astype(jnp.float32),
        summed_proj.astype(jnp.float32),
        lax.dot_general(
            g_vec[:, : vectors.shape[0]],
            jnp.eye(g_vec.shape[0], dtype=jnp.bfloat16),
            (((0,), (0,)), ((), ())),
            preferred_element_type=jnp.float32,
        ),
    )
    grads = jax.tree.map(partial(jnp.multiply, 1.0 / replicas), summed)
    first = adam_step(w_qkv, grads[0], mean_qkv, square_qkv, rate_matrix, decay_matrix)
    second = adam_step(w_out, grads[1], mean_out, square_out, rate_matrix, decay_matrix)
    third = adam_step(w_fc, grads[2], mean_fc, square_fc, rate_matrix, decay_matrix)
    fourth = adam_step(w_proj, grads[3], mean_proj, square_proj, rate_matrix, decay_matrix)
    fifth = adam_step(vectors, grads[4], mean_vectors, square_vectors, rate_vector, 0.0)
    return (
        block_out,
        input_grad,
        grads[0],
        grads[1],
        grads[2],
        grads[3],
        grads[4],
        first[0],
        second[0],
        third[0],
        fourth[0],
        fifth[0],
        first[1],
        second[1],
        third[1],
        fourth[1],
        fifth[1],
        first[2],
        second[2],
        third[2],
        fourth[2],
        fifth[2],
    )


def solution(mesh):
    placed = (
        P(("dp", "zero"), None),
        P(("dp", "zero"), None),
        P(("dp", "zero"), None),
        P("zero", None),
        P("zero", None),
        P("zero", None),
        P("zero", None),
        P(None, "zero"),
        P("zero", None),
        P("zero", None),
        P("zero", None),
        P("zero", None),
        P(None, "zero"),
        P("zero", None),
        P("zero", None),
        P("zero", None),
        P("zero", None),
        P(None, "zero"),
    )
    return jax.shard_map(
        local,
        mesh=mesh,
        in_specs=placed,
        out_specs=(
            P(("dp", "zero"), None),
            P(("dp", "zero"), None),
            P("zero", None),
            P("zero", None),
            P("zero", None),
            P("zero", None),
            P(None, "zero"),
            P("zero", None),
            P("zero", None),
            P("zero", None),
            P("zero", None),
            P(None, "zero"),
            P("zero", None),
            P("zero", None),
            P("zero", None),
            P("zero", None),
            P(None, "zero"),
            P("zero", None),
            P("zero", None),
            P("zero", None),
            P("zero", None),
            P(None, "zero"),
        ),
        check_vma=False,
    )
```

```python
from functools import partial

import jax
import jax.numpy as jnp
from jax import lax
from jax.experimental import pallas as pl
from jax.experimental.pallas import tpu as pltpu
from jax.sharding import PartitionSpec as P

HEADS = 16
SEQ = 128
ADAM_STEP = 3
LANE = 128


eps_norm = 1e-05
beta_first = 0.9
beta_second = 0.999
eps_adam = 1e-08
rate_matrix = 0.02
rate_vector = 0.15
decay_matrix = 0.1


def sent_together(arrays, axis, dim, along):
    widths = [a.shape[along] for a in arrays]
    both = jnp.concatenate(arrays, axis=along)
    result = lax.all_gather(both, axis, axis=dim, tiled=True)
    return tuple(jnp.split(result, [sum(widths[:k]) for k in range(1, len(widths))], axis=along))


def in_one_piece(arrays, axis, dim, along):
    ends, at = ([], 0)
    for a in arrays[:-1]:
        at += a.shape[along]
        ends.append(at)
    both = jnp.concatenate(arrays, axis=along)
    return tuple(
        jnp.split(lax.psum_scatter(both, axis, scatter_dimension=dim, tiled=True), ends, axis=along)
    )


def dp_sum_kernel(parts, count, *refs):
    x_refs, out_refs = refs[:count], refs[count : 2 * count]
    recv_one, recv_two = refs[2 * count : 3 * count], refs[3 * count : 4 * count]
    mine = refs[4 * count : 5 * count]
    send_one, got_one, send_two, got_two = refs[5 * count :]
    me = lax.axis_index("dp")
    shard = lax.axis_index("zero")
    barrier = pltpu.get_barrier_semaphore()
    for k in range(1, parts):
        pl.semaphore_signal(
            barrier, inc=1, device_id=(lax.rem(me + k, parts), shard),
            device_id_type=pl.DeviceIdType.MESH,
        )
    pl.semaphore_wait(barrier, parts - 1)

    def send(sources, targets, sends, gots, pick):
        copies = []
        for k in range(1, parts):
            peer = lax.rem(me + k, parts)
            for i in range(count):
                copy = pltpu.make_async_remote_copy(
                    src_ref=pick(sources[i], peer),
                    dst_ref=targets[i].at[k],
                    send_sem=sends.at[i, k],
                    recv_sem=gots.at[i, k],
                    device_id=(peer, shard),
                    device_id_type=pl.DeviceIdType.MESH,
                )
                copy.start()
                copies.append(copy)
        return copies

    first = send(x_refs, recv_one, send_one, got_one, lambda ref, peer: ref.at[peer])
    totals = [x_refs[i][me].astype(jnp.float32) for i in range(count)]
    for n, copy in enumerate(first):
        copy.wait_recv()
        k, i = n // count + 1, n % count
        totals[i] = totals[i] + recv_one[i][k].astype(jnp.float32)
    for i in range(count):
        mine[i][...] = totals[i].astype(mine[i].dtype)
        out_refs[i][me] = mine[i][...]
    second = send(mine, recv_two, send_two, got_two, lambda ref, peer: ref)
    for copy in first:
        copy.wait_send()
    for n, copy in enumerate(second):
        copy.wait_recv()
        k, i = n // count + 1, n % count
        out_refs[i][lax.rem(me + parts - k, parts)] = recv_two[i][k]
    for copy in second:
        copy.wait_send()


def summed_over_dp(arrays, slot):
    parts = lax.axis_size("dp")
    count = len(arrays)
    stacked = [a.reshape((parts, a.shape[0] // parts) + a.shape[1:]) for a in arrays]
    vmem = pl.BlockSpec(memory_space=pltpu.VMEM)
    results = pl.pallas_call(
        partial(dp_sum_kernel, parts, count),
        out_shape=[jax.ShapeDtypeStruct(s.shape, s.dtype) for s in stacked],
        in_specs=[vmem] * count,
        out_specs=[vmem] * count,
        scratch_shapes=[pltpu.VMEM(s.shape, s.dtype) for s in stacked] * 2
        + [pltpu.VMEM(s.shape[1:], s.dtype) for s in stacked]
        + [pltpu.SemaphoreType.DMA((count, parts))] * 4,
        compiler_params=pltpu.CompilerParams(collective_id=slot, has_side_effects=True),
    )(*stacked)
    return [r.reshape(a.shape) for r, a in zip(results, arrays)]


def gelu_tanh(inputs):
    inner = 0.7978845608028654 * (inputs + 0.044715 * inputs * inputs * inputs)
    return 0.5 * inputs * (1.0 + jnp.tanh(inner))


def layer_norm(inputs, gain_row, bias_row):
    average = jnp.mean(inputs, axis=-1, keepdims=True)
    centred = inputs - average
    variance = jnp.mean(centred * centred, axis=-1, keepdims=True)
    return centred * lax.rsqrt(variance + eps_norm) * gain_row + bias_row


def allowed_mask(seg_rows):
    length = seg_rows.shape[1]
    places = lax.iota(jnp.int32, length)
    causal = places[:, None] >= places[None, :]
    same_doc = seg_rows[:, :, None] == seg_rows[:, None, :]
    return jnp.logical_and(same_doc, causal[None])[:, None]


def attend_scores(queries, keys_in, seg_rows):
    scaling = queries.shape[-1] ** (-0.5)
    scores = (
        jnp.einsum("rqhe,rkhe->rhqk", queries, keys_in, preferred_element_type=jnp.float32)
        * scaling
    )
    return (scores, allowed_mask(seg_rows), scaling)


def attention_forward(queries, keys_in, values, seg_rows):
    scores, allowed, scaling = attend_scores(queries, keys_in, seg_rows)
    exponent = jnp.where(allowed, jnp.exp(scores), 0.0)
    log_total = jnp.log(jnp.sum(exponent, axis=-1, keepdims=True))
    attn_weights = jnp.where(allowed, jnp.exp(scores - log_total), 0.0).astype(jnp.bfloat16)
    attended = jnp.einsum(
        "rhqk,rkhe->rqhe", attn_weights, values, preferred_element_type=jnp.float32
    )
    return (attended.astype(jnp.bfloat16), log_total)


def attention_backward(queries, keys_in, values, seg_rows, log_total, grad_att):
    scores, allowed, scaling = attend_scores(queries, keys_in, seg_rows)
    weights_full = jnp.where(allowed, jnp.exp(scores - log_total), 0.0)
    weights_half = weights_full.astype(jnp.bfloat16)
    grad_values = jnp.einsum(
        "rhqk,rqhe->rkhe", weights_half, grad_att, preferred_element_type=jnp.float32
    )
    grad_weights = jnp.einsum(
        "rqhe,rkhe->rhqk", grad_att, values, preferred_element_type=jnp.float32
    )
    row_dot = jnp.sum(weights_full * grad_weights, axis=-1, keepdims=True)
    grad_scores = (weights_full * (grad_weights - row_dot) * scaling).astype(jnp.bfloat16)
    grad_queries = jnp.einsum(
        "rhqk,rkhe->rqhe", grad_scores, keys_in, preferred_element_type=jnp.float32
    )
    grad_keys = jnp.einsum(
        "rhqk,rqhe->rkhe", grad_scores, queries, preferred_element_type=jnp.float32
    )
    return (grad_queries, grad_keys, grad_values)


def block_pass(tokens_in, cot_in, seg_rows, qkv_mat, out_mat, fc_mat, proj_mat, vec_rows):
    count_tok = tokens_in.shape[0]
    width = tokens_in.shape[1]
    head_width = width // HEADS
    row_count = count_tok // SEQ
    split_shape = (row_count, SEQ, HEADS, head_width)
    tokens32 = tokens_in.astype(jnp.float32)
    normed_one = layer_norm(tokens32, vec_rows[0], vec_rows[1]).astype(jnp.bfloat16)
    projected = jnp.dot(normed_one, qkv_mat, preferred_element_type=jnp.float32)
    queries = (projected[:, :width] + vec_rows[2]).astype(jnp.bfloat16).reshape(split_shape)
    keys_in = projected[:, width : 2 * width].astype(jnp.bfloat16).reshape(split_shape)
    values = (projected[:, 2 * width :] + vec_rows[3]).astype(jnp.bfloat16).reshape(split_shape)
    attended, log_total = attention_forward(queries, keys_in, values, seg_rows)
    attended = attended.reshape(count_tok, width)
    middle = tokens32 + jnp.dot(attended, out_mat, preferred_element_type=jnp.float32) + vec_rows[4]
    normed_two = layer_norm(middle, vec_rows[5], vec_rows[6]).astype(jnp.bfloat16)
    fc_bias = vec_rows[8:].reshape(-1)
    hidden_pre = jnp.dot(normed_two, fc_mat, preferred_element_type=jnp.float32) + fc_bias
    hidden = gelu_tanh(hidden_pre).astype(jnp.bfloat16)
    block_out = (
        middle + jnp.dot(hidden, proj_mat, preferred_element_type=jnp.float32) + vec_rows[7]
    ).astype(jnp.bfloat16)
    cot32 = cot_in.astype(jnp.float32)
    grad_proj = jnp.dot(hidden.T, cot_in, preferred_element_type=jnp.float32).astype(jnp.bfloat16)
    grad_proj, cot_in, hidden_pre, middle = lax.optimization_barrier(
        (grad_proj, cot_in, hidden_pre, middle)
    )
    grad_hidden = jnp.dot(cot_in, proj_mat.T, preferred_element_type=jnp.float32)
    gelu_back = jax.vjp(gelu_tanh, hidden_pre)[1]
    grad_pre = gelu_back(grad_hidden)[0]
    grad_pre_half = grad_pre.astype(jnp.bfloat16)
    grad_fc = jnp.dot(normed_two.T, grad_pre_half, preferred_element_type=jnp.float32)
    grad_normed_two = jnp.dot(grad_pre_half, fc_mat.T, preferred_element_type=jnp.float32)
    norm_two_back = jax.vjp(layer_norm, middle, vec_rows[5], vec_rows[6])[1]
    grad_mid_norm, grad_gain_two, grad_bias_two = norm_two_back(grad_normed_two)
    grad_middle = cot32 + grad_mid_norm
    grad_middle_half = grad_middle.astype(jnp.bfloat16)
    grad_out = jnp.dot(attended.T, grad_middle_half, preferred_element_type=jnp.float32)
    grad_attended = jnp.dot(grad_middle_half, out_mat.T, preferred_element_type=jnp.float32)
    grad_attended = grad_attended.astype(jnp.bfloat16).reshape(split_shape)
    grad_queries, grad_keys, grad_values = attention_backward(
        queries, keys_in, values, seg_rows, log_total, grad_attended
    )
    flat_queries = grad_queries.reshape(count_tok, width)
    flat_keys = grad_keys.reshape(count_tok, width)
    flat_values = grad_values.reshape(count_tok, width)
    grad_projected = jnp.concatenate([flat_queries, flat_keys, flat_values], axis=1).astype(
        jnp.bfloat16
    )
    grad_qkv = jnp.dot(normed_one.T, grad_projected, preferred_element_type=jnp.float32)
    grad_normed_one = jnp.dot(grad_projected, qkv_mat.T, preferred_element_type=jnp.float32)
    norm_one_back = jax.vjp(layer_norm, tokens32, vec_rows[0], vec_rows[1])[1]
    grad_tok_norm, grad_gain_one, grad_bias_one = norm_one_back(grad_normed_one)
    input_grad = (grad_middle + grad_tok_norm).astype(jnp.bfloat16)
    small_rows = jnp.stack(
        [
            grad_gain_one,
            grad_bias_one,
            jnp.sum(flat_queries, axis=0),
            jnp.sum(flat_values, axis=0),
            jnp.sum(grad_middle, axis=0),
            grad_gain_two,
            grad_bias_two,
            jnp.sum(cot32, axis=0),
        ]
    )
    grad_vec = jnp.concatenate([small_rows, jnp.sum(grad_pre, axis=0).reshape(-1, width)], axis=0)
    return (block_out, input_grad, (grad_qkv, grad_out, grad_fc, grad_proj, grad_vec))


def adam_step(weight, gradient, mean_old, square_old, rate, decay):
    mean_new = beta_first * mean_old + (1.0 - beta_first) * gradient
    square_new = beta_second * square_old + (1.0 - beta_second) * gradient * gradient
    mean_hat = mean_new / (1.0 - beta_first**ADAM_STEP)
    square_hat = square_new / (1.0 - beta_second**ADAM_STEP)
    weight_new = weight - rate * (mean_hat / (jnp.sqrt(square_hat) + eps_adam) + decay * weight)
    return (weight_new, mean_new, square_new)


def local(
    tokens,
    cotangent,
    segments,
    w_qkv,
    w_out,
    w_fc,
    w_proj,
    vectors,
    mean_qkv,
    mean_out,
    mean_fc,
    mean_proj,
    mean_vectors,
    square_qkv,
    square_out,
    square_fc,
    square_proj,
    square_vectors,
):
    dp_size = lax.axis_size("dp")
    zero_size = lax.axis_size("zero")
    replicas = dp_size * zero_size
    vec_cols = jnp.pad(vectors.astype(jnp.bfloat16).T, ((0, 0), (0, LANE - vectors.shape[0])))
    first_mats = (w_qkv.astype(jnp.bfloat16), w_out.astype(jnp.bfloat16), w_fc.astype(jnp.bfloat16), vec_cols)
    first_all = lax.all_gather(jnp.concatenate(first_mats, axis=1), "zero", axis=0, tiled=True)
    first_all, proj_shard = lax.optimization_barrier((first_all, w_proj.astype(jnp.bfloat16)))
    proj_mat = lax.all_gather(proj_shard, "zero", axis=0, tiled=True)
    widths = [m.shape[1] for m in first_mats]
    qkv_mat, out_mat, fc_mat, vec_cols_all = jnp.split(
        first_all, [sum(widths[:k]) for k in range(1, len(widths))], axis=1
    )
    vec_rows = vec_cols_all[:, : vectors.shape[0]].T.astype(jnp.float32)
    block_out, input_grad, local_grads = block_pass(
        tokens, cotangent, segments, qkv_mat, out_mat, fc_mat, proj_mat, vec_rows
    )
    grad_vec_cols = jnp.pad(
        local_grads[4].astype(jnp.bfloat16).T, ((0, 0), (0, LANE - vectors.shape[0]))
    )
    joined = jnp.concatenate(
        (
            local_grads[0].astype(jnp.bfloat16),
            local_grads[1].astype(jnp.bfloat16),
            local_grads[2].astype(jnp.bfloat16),
            grad_vec_cols,
        ),
        axis=1,
    )
    scattered = lax.psum_scatter(joined, "zero", scatter_dimension=0, tiled=True)
    proj_scattered = lax.psum_scatter(
        local_grads[3].astype(jnp.bfloat16), "zero", scatter_dimension=0, tiled=True
    )
    (summed_proj,) = summed_over_dp((proj_scattered,), 1)
    (summed_joined,) = summed_over_dp((scattered,), 0)
    ends = [w_qkv.shape[1], w_qkv.shape[1] + w_out.shape[1], w_qkv.shape[1] + w_out.shape[1] + w_fc.shape[1]]
    g_qkv, g_out, g_fc, g_vec = jnp.split(summed_joined, ends, axis=1)
    summed = (
        g_qkv.astype(jnp.float32),
        g_out.astype(jnp.float32),
        g_fc.astype(jnp.float32),
        summed_proj.astype(jnp.float32),
        lax.dot_general(
            g_vec[:, : vectors.shape[0]],
            jnp.eye(g_vec.shape[0], dtype=jnp.bfloat16),
            (((0,), (0,)), ((), ())),
            preferred_element_type=jnp.float32,
        ),
    )
    grads = jax.tree.map(partial(jnp.multiply, 1.0 / replicas), summed)
    first = adam_step(w_qkv, grads[0], mean_qkv, square_qkv, rate_matrix, decay_matrix)
    second = adam_step(w_out, grads[1], mean_out, square_out, rate_matrix, decay_matrix)
    third = adam_step(w_fc, grads[2], mean_fc, square_fc, rate_matrix, decay_matrix)
    fourth = adam_step(w_proj, grads[3], mean_proj, square_proj, rate_matrix, decay_matrix)
    fifth = adam_step(vectors, grads[4], mean_vectors, square_vectors, rate_vector, 0.0)
    return (
        block_out,
        input_grad,
        grads[0],
        grads[1],
        grads[2],
        grads[3],
        grads[4],
        first[0],
        second[0],
        third[0],
        fourth[0],
        fifth[0],
        first[1],
        second[1],
        third[1],
        fourth[1],
        fifth[1],
        first[2],
        second[2],
        third[2],
        fourth[2],
        fifth[2],
    )


def solution(mesh):
    placed = (
        P(("dp", "zero"), None),
        P(("dp", "zero"), None),
        P(("dp", "zero"), None),
        P("zero", None),
        P("zero", None),
        P("zero", None),
        P("zero", None),
        P(None, "zero"),
        P("zero", None),
        P("zero", None),
        P("zero", None),
        P("zero", None),
        P(None, "zero"),
        P("zero", None),
        P("zero", None),
        P("zero", None),
        P("zero", None),
        P(None, "zero"),
    )
    return jax.shard_map(
        local,
        mesh=mesh,
        in_specs=placed,
        out_specs=(
            P(("dp", "zero"), None),
            P(("dp", "zero"), None),
            P("zero", None),
            P("zero", None),
            P("zero", None),
            P("zero", None),
            P(None, "zero"),
            P("zero", None),
            P("zero", None),
            P("zero", None),
            P("zero", None),
            P(None, "zero"),
            P("zero", None),
            P("zero", None),
            P("zero", None),
            P("zero", None),
            P(None, "zero"),
            P("zero", None),
            P("zero", None),
            P("zero", None),
            P("zero", None),
            P(None, "zero"),
        ),
        check_vma=False,
    )
```

```python
from functools import partial

import jax
import jax.numpy as jnp
from jax import lax
from jax.experimental import pallas as pl
from jax.experimental.pallas import tpu as pltpu
from jax.sharding import PartitionSpec as P

HEADS = 16
SEQ = 128
ADAM_STEP = 3
LANE = 128


eps_norm = 1e-05
beta_first = 0.9
beta_second = 0.999
eps_adam = 1e-08
rate_matrix = 0.02
rate_vector = 0.15
decay_matrix = 0.1


def sent_together(arrays, axis, dim, along):
    widths = [a.shape[along] for a in arrays]
    both = jnp.concatenate(arrays, axis=along)
    result = lax.all_gather(both, axis, axis=dim, tiled=True)
    return tuple(jnp.split(result, [sum(widths[:k]) for k in range(1, len(widths))], axis=along))


def in_one_piece(arrays, axis, dim, along):
    ends, at = ([], 0)
    for a in arrays[:-1]:
        at += a.shape[along]
        ends.append(at)
    both = jnp.concatenate(arrays, axis=along)
    return tuple(
        jnp.split(lax.psum_scatter(both, axis, scatter_dimension=dim, tiled=True), ends, axis=along)
    )


def dp_sum_kernel(parts, count, *refs):
    x_refs, out_refs = refs[:count], refs[count : 2 * count]
    recv_one = refs[2 * count : 3 * count]
    mine = refs[3 * count : 4 * count]
    send_one, got_one, send_two, got_two = refs[4 * count :]
    me = lax.axis_index("dp")
    shard = lax.axis_index("zero")
    barrier = pltpu.get_barrier_semaphore()
    for k in range(1, parts):
        pl.semaphore_signal(
            barrier, inc=1, device_id=(lax.rem(me + k, parts), shard),
            device_id_type=pl.DeviceIdType.MESH,
        )
    pl.semaphore_wait(barrier, parts - 1)

    def send(sources, targets, sends, gots, pick):
        copies = []
        for k in range(1, parts):
            peer = lax.rem(me + k, parts)
            for i in range(count):
                copy = pltpu.make_async_remote_copy(
                    src_ref=pick(sources[i], peer),
                    dst_ref=targets[i].at[k],
                    send_sem=sends.at[i, k],
                    recv_sem=gots.at[i, k],
                    device_id=(peer, shard),
                    device_id_type=pl.DeviceIdType.MESH,
                )
                copy.start()
                copies.append(copy)
        return copies

    first = send(x_refs, recv_one, send_one, got_one, lambda ref, peer: ref.at[peer])
    totals = [x_refs[i][me].astype(jnp.float32) for i in range(count)]
    for n, copy in enumerate(first):
        copy.wait_recv()
        k, i = n // count + 1, n % count
        totals[i] = totals[i] + recv_one[i][k].astype(jnp.float32)
    for i in range(count):
        mine[i][...] = totals[i].astype(mine[i].dtype)
        out_refs[i][me] = mine[i][...]
    second = []
    for k in range(1, parts):
        peer = lax.rem(me + k, parts)
        for i in range(count):
            copy = pltpu.make_async_remote_copy(
                src_ref=mine[i],
                dst_ref=out_refs[i].at[me],
                send_sem=send_two.at[i, k],
                recv_sem=got_two.at[i, k],
                device_id=(peer, shard),
                device_id_type=pl.DeviceIdType.MESH,
            )
            copy.start()
            second.append(copy)
    for copy in first:
        copy.wait_send()
    for copy in second:
        copy.wait_recv()
    for copy in second:
        copy.wait_send()


def summed_over_dp(arrays, slot):
    parts = lax.axis_size("dp")
    count = len(arrays)
    stacked = [a.reshape((parts, a.shape[0] // parts) + a.shape[1:]) for a in arrays]
    vmem = pl.BlockSpec(memory_space=pltpu.VMEM)
    results = pl.pallas_call(
        partial(dp_sum_kernel, parts, count),
        out_shape=[jax.ShapeDtypeStruct(s.shape, s.dtype) for s in stacked],
        in_specs=[vmem] * count,
        out_specs=[vmem] * count,
        scratch_shapes=[pltpu.VMEM(s.shape, s.dtype) for s in stacked]
        + [pltpu.VMEM(s.shape[1:], s.dtype) for s in stacked]
        + [pltpu.SemaphoreType.DMA((count, parts))] * 4,
        compiler_params=pltpu.CompilerParams(collective_id=slot, has_side_effects=True),
    )(*stacked)
    return [r.reshape(a.shape) for r, a in zip(results, arrays)]


def gelu_tanh(inputs):
    inner = 0.7978845608028654 * (inputs + 0.044715 * inputs * inputs * inputs)
    return 0.5 * inputs * (1.0 + jnp.tanh(inner))


def layer_norm(inputs, gain_row, bias_row):
    average = jnp.mean(inputs, axis=-1, keepdims=True)
    centred = inputs - average
    variance = jnp.mean(centred * centred, axis=-1, keepdims=True)
    return centred * lax.rsqrt(variance + eps_norm) * gain_row + bias_row


def allowed_mask(seg_rows):
    length = seg_rows.shape[1]
    places = lax.iota(jnp.int32, length)
    causal = places[:, None] >= places[None, :]
    same_doc = seg_rows[:, :, None] == seg_rows[:, None, :]
    return jnp.logical_and(same_doc, causal[None])[:, None]


def attend_scores(queries, keys_in, seg_rows):
    scaling = queries.shape[-1] ** (-0.5)
    scores = (
        jnp.einsum("rqhe,rkhe->rhqk", queries, keys_in, preferred_element_type=jnp.float32)
        * scaling
    )
    return (scores, allowed_mask(seg_rows), scaling)


def attention_forward(queries, keys_in, values, seg_rows):
    scores, allowed, scaling = attend_scores(queries, keys_in, seg_rows)
    exponent = jnp.where(allowed, jnp.exp(scores), 0.0)
    log_total = jnp.log(jnp.sum(exponent, axis=-1, keepdims=True))
    attn_weights = jnp.where(allowed, jnp.exp(scores - log_total), 0.0).astype(jnp.bfloat16)
    attended = jnp.einsum(
        "rhqk,rkhe->rqhe", attn_weights, values, preferred_element_type=jnp.float32
    )
    return (attended.astype(jnp.bfloat16), log_total)


def attention_backward(queries, keys_in, values, seg_rows, log_total, grad_att):
    scores, allowed, scaling = attend_scores(queries, keys_in, seg_rows)
    weights_full = jnp.where(allowed, jnp.exp(scores - log_total), 0.0)
    weights_half = weights_full.astype(jnp.bfloat16)
    grad_values = jnp.einsum(
        "rhqk,rqhe->rkhe", weights_half, grad_att, preferred_element_type=jnp.float32
    )
    grad_weights = jnp.einsum(
        "rqhe,rkhe->rhqk", grad_att, values, preferred_element_type=jnp.float32
    )
    row_dot = jnp.sum(weights_full * grad_weights, axis=-1, keepdims=True)
    grad_scores = (weights_full * (grad_weights - row_dot) * scaling).astype(jnp.bfloat16)
    grad_queries = jnp.einsum(
        "rhqk,rkhe->rqhe", grad_scores, keys_in, preferred_element_type=jnp.float32
    )
    grad_keys = jnp.einsum(
        "rhqk,rqhe->rkhe", grad_scores, queries, preferred_element_type=jnp.float32
    )
    return (grad_queries, grad_keys, grad_values)


def block_pass(tokens_in, cot_in, seg_rows, qkv_mat, out_mat, fc_mat, proj_mat, vec_rows):
    count_tok = tokens_in.shape[0]
    width = tokens_in.shape[1]
    head_width = width // HEADS
    row_count = count_tok // SEQ
    split_shape = (row_count, SEQ, HEADS, head_width)
    tokens32 = tokens_in.astype(jnp.float32)
    normed_one = layer_norm(tokens32, vec_rows[0], vec_rows[1]).astype(jnp.bfloat16)
    projected = jnp.dot(normed_one, qkv_mat, preferred_element_type=jnp.float32)
    queries = (projected[:, :width] + vec_rows[2]).astype(jnp.bfloat16).reshape(split_shape)
    keys_in = projected[:, width : 2 * width].astype(jnp.bfloat16).reshape(split_shape)
    values = (projected[:, 2 * width :] + vec_rows[3]).astype(jnp.bfloat16).reshape(split_shape)
    attended, log_total = attention_forward(queries, keys_in, values, seg_rows)
    attended = attended.reshape(count_tok, width)
    middle = tokens32 + jnp.dot(attended, out_mat, preferred_element_type=jnp.float32) + vec_rows[4]
    normed_two = layer_norm(middle, vec_rows[5], vec_rows[6]).astype(jnp.bfloat16)
    fc_bias = vec_rows[8:].reshape(-1)
    hidden_pre = jnp.dot(normed_two, fc_mat, preferred_element_type=jnp.float32) + fc_bias
    hidden = gelu_tanh(hidden_pre).astype(jnp.bfloat16)
    block_out = (
        middle + jnp.dot(hidden, proj_mat, preferred_element_type=jnp.float32) + vec_rows[7]
    ).astype(jnp.bfloat16)
    cot32 = cot_in.astype(jnp.float32)
    grad_proj = jnp.dot(hidden.T, cot_in, preferred_element_type=jnp.float32).astype(jnp.bfloat16)
    grad_proj, cot_in, hidden_pre, middle = lax.optimization_barrier(
        (grad_proj, cot_in, hidden_pre, middle)
    )
    grad_hidden = jnp.dot(cot_in, proj_mat.T, preferred_element_type=jnp.float32)
    gelu_back = jax.vjp(gelu_tanh, hidden_pre)[1]
    grad_pre = gelu_back(grad_hidden)[0]
    grad_pre_half = grad_pre.astype(jnp.bfloat16)
    grad_fc = jnp.dot(normed_two.T, grad_pre_half, preferred_element_type=jnp.float32)
    grad_normed_two = jnp.dot(grad_pre_half, fc_mat.T, preferred_element_type=jnp.float32)
    norm_two_back = jax.vjp(layer_norm, middle, vec_rows[5], vec_rows[6])[1]
    grad_mid_norm, grad_gain_two, grad_bias_two = norm_two_back(grad_normed_two)
    grad_middle = cot32 + grad_mid_norm
    grad_middle_half = grad_middle.astype(jnp.bfloat16)
    grad_out = jnp.dot(attended.T, grad_middle_half, preferred_element_type=jnp.float32)
    grad_attended = jnp.dot(grad_middle_half, out_mat.T, preferred_element_type=jnp.float32)
    grad_attended = grad_attended.astype(jnp.bfloat16).reshape(split_shape)
    grad_queries, grad_keys, grad_values = attention_backward(
        queries, keys_in, values, seg_rows, log_total, grad_attended
    )
    flat_queries = grad_queries.reshape(count_tok, width)
    flat_keys = grad_keys.reshape(count_tok, width)
    flat_values = grad_values.reshape(count_tok, width)
    grad_projected = jnp.concatenate([flat_queries, flat_keys, flat_values], axis=1).astype(
        jnp.bfloat16
    )
    grad_qkv = jnp.dot(normed_one.T, grad_projected, preferred_element_type=jnp.float32)
    grad_normed_one = jnp.dot(grad_projected, qkv_mat.T, preferred_element_type=jnp.float32)
    norm_one_back = jax.vjp(layer_norm, tokens32, vec_rows[0], vec_rows[1])[1]
    grad_tok_norm, grad_gain_one, grad_bias_one = norm_one_back(grad_normed_one)
    input_grad = (grad_middle + grad_tok_norm).astype(jnp.bfloat16)
    small_rows = jnp.stack(
        [
            grad_gain_one,
            grad_bias_one,
            jnp.sum(flat_queries, axis=0),
            jnp.sum(flat_values, axis=0),
            jnp.sum(grad_middle, axis=0),
            grad_gain_two,
            grad_bias_two,
            jnp.sum(cot32, axis=0),
        ]
    )
    grad_vec = jnp.concatenate([small_rows, jnp.sum(grad_pre, axis=0).reshape(-1, width)], axis=0)
    return (block_out, input_grad, (grad_qkv, grad_out, grad_fc, grad_proj, grad_vec))


def adam_step(weight, gradient, mean_old, square_old, rate, decay):
    mean_new = beta_first * mean_old + (1.0 - beta_first) * gradient
    square_new = beta_second * square_old + (1.0 - beta_second) * gradient * gradient
    mean_hat = mean_new / (1.0 - beta_first**ADAM_STEP)
    square_hat = square_new / (1.0 - beta_second**ADAM_STEP)
    weight_new = weight - rate * (mean_hat / (jnp.sqrt(square_hat) + eps_adam) + decay * weight)
    return (weight_new, mean_new, square_new)


def local(
    tokens,
    cotangent,
    segments,
    w_qkv,
    w_out,
    w_fc,
    w_proj,
    vectors,
    mean_qkv,
    mean_out,
    mean_fc,
    mean_proj,
    mean_vectors,
    square_qkv,
    square_out,
    square_fc,
    square_proj,
    square_vectors,
):
    dp_size = lax.axis_size("dp")
    zero_size = lax.axis_size("zero")
    replicas = dp_size * zero_size
    vec_cols = jnp.pad(vectors.astype(jnp.bfloat16).T, ((0, 0), (0, LANE - vectors.shape[0])))
    first_mats = (w_qkv.astype(jnp.bfloat16), w_out.astype(jnp.bfloat16), w_fc.astype(jnp.bfloat16), vec_cols)
    first_all = lax.all_gather(jnp.concatenate(first_mats, axis=1), "zero", axis=0, tiled=True)
    first_all, proj_shard = lax.optimization_barrier((first_all, w_proj.astype(jnp.bfloat16)))
    proj_mat = lax.all_gather(proj_shard, "zero", axis=0, tiled=True)
    widths = [m.shape[1] for m in first_mats]
    qkv_mat, out_mat, fc_mat, vec_cols_all = jnp.split(
        first_all, [sum(widths[:k]) for k in range(1, len(widths))], axis=1
    )
    vec_rows = vec_cols_all[:, : vectors.shape[0]].T.astype(jnp.float32)
    block_out, input_grad, local_grads = block_pass(
        tokens, cotangent, segments, qkv_mat, out_mat, fc_mat, proj_mat, vec_rows
    )
    grad_vec_cols = jnp.pad(
        local_grads[4].astype(jnp.bfloat16).T, ((0, 0), (0, LANE - vectors.shape[0]))
    )
    joined = jnp.concatenate(
        (
            local_grads[0].astype(jnp.bfloat16),
            local_grads[1].astype(jnp.bfloat16),
            local_grads[2].astype(jnp.bfloat16),
            grad_vec_cols,
        ),
        axis=1,
    )
    scattered = lax.psum_scatter(joined, "zero", scatter_dimension=0, tiled=True)
    proj_scattered = lax.psum_scatter(
        local_grads[3].astype(jnp.bfloat16), "zero", scatter_dimension=0, tiled=True
    )
    (summed_proj,) = summed_over_dp((proj_scattered,), 1)
    (summed_joined,) = summed_over_dp((scattered,), 0)
    ends = [w_qkv.shape[1], w_qkv.shape[1] + w_out.shape[1], w_qkv.shape[1] + w_out.shape[1] + w_fc.shape[1]]
    g_qkv, g_out, g_fc, g_vec = jnp.split(summed_joined, ends, axis=1)
    summed = (
        g_qkv.astype(jnp.float32),
        g_out.astype(jnp.float32),
        g_fc.astype(jnp.float32),
        summed_proj.astype(jnp.float32),
        lax.dot_general(
            g_vec[:, : vectors.shape[0]],
            jnp.eye(g_vec.shape[0], dtype=jnp.bfloat16),
            (((0,), (0,)), ((), ())),
            preferred_element_type=jnp.float32,
        ),
    )
    grads = jax.tree.map(partial(jnp.multiply, 1.0 / replicas), summed)
    first = adam_step(w_qkv, grads[0], mean_qkv, square_qkv, rate_matrix, decay_matrix)
    second = adam_step(w_out, grads[1], mean_out, square_out, rate_matrix, decay_matrix)
    third = adam_step(w_fc, grads[2], mean_fc, square_fc, rate_matrix, decay_matrix)
    fourth = adam_step(w_proj, grads[3], mean_proj, square_proj, rate_matrix, decay_matrix)
    fifth = adam_step(vectors, grads[4], mean_vectors, square_vectors, rate_vector, 0.0)
    return (
        block_out,
        input_grad,
        grads[0],
        grads[1],
        grads[2],
        grads[3],
        grads[4],
        first[0],
        second[0],
        third[0],
        fourth[0],
        fifth[0],
        first[1],
        second[1],
        third[1],
        fourth[1],
        fifth[1],
        first[2],
        second[2],
        third[2],
        fourth[2],
        fifth[2],
    )


def solution(mesh):
    placed = (
        P(("dp", "zero"), None),
        P(("dp", "zero"), None),
        P(("dp", "zero"), None),
        P("zero", None),
        P("zero", None),
        P("zero", None),
        P("zero", None),
        P(None, "zero"),
        P("zero", None),
        P("zero", None),
        P("zero", None),
        P("zero", None),
        P(None, "zero"),
        P("zero", None),
        P("zero", None),
        P("zero", None),
        P("zero", None),
        P(None, "zero"),
    )
    return jax.shard_map(
        local,
        mesh=mesh,
        in_specs=placed,
        out_specs=(
            P(("dp", "zero"), None),
            P(("dp", "zero"), None),
            P("zero", None),
            P("zero", None),
            P("zero", None),
            P("zero", None),
            P(None, "zero"),
            P("zero", None),
            P("zero", None),
            P("zero", None),
            P("zero", None),
            P(None, "zero"),
            P("zero", None),
            P("zero", None),
            P("zero", None),
            P("zero", None),
            P(None, "zero"),
            P("zero", None),
            P("zero", None),
            P("zero", None),
            P("zero", None),
            P(None, "zero"),
        ),
        check_vma=False,
    )
```

```python
from functools import partial

import jax
import jax.numpy as jnp
from jax import lax
from jax.experimental import pallas as pl
from jax.experimental.pallas import tpu as pltpu
from jax.sharding import PartitionSpec as P

HEADS = 16
SEQ = 128
ADAM_STEP = 3
LANE = 128


eps_norm = 1e-05
beta_first = 0.9
beta_second = 0.999
eps_adam = 1e-08
rate_matrix = 0.02
rate_vector = 0.15
decay_matrix = 0.1


def sent_together(arrays, axis, dim, along):
    widths = [a.shape[along] for a in arrays]
    both = jnp.concatenate(arrays, axis=along)
    result = lax.all_gather(both, axis, axis=dim, tiled=True)
    return tuple(jnp.split(result, [sum(widths[:k]) for k in range(1, len(widths))], axis=along))


def in_one_piece(arrays, axis, dim, along):
    ends, at = ([], 0)
    for a in arrays[:-1]:
        at += a.shape[along]
        ends.append(at)
    both = jnp.concatenate(arrays, axis=along)
    return tuple(
        jnp.split(lax.psum_scatter(both, axis, scatter_dimension=dim, tiled=True), ends, axis=along)
    )


def dp_sum_kernel(parts, count, *refs):
    x_refs, out_refs = refs[:count], refs[count : 2 * count]
    recv_one, recv_two = refs[2 * count : 3 * count], refs[3 * count : 4 * count]
    mine = refs[4 * count : 5 * count]
    send_one, got_one, send_two, got_two = refs[5 * count :]
    me = lax.axis_index("dp")
    shard = lax.axis_index("zero")
    barrier = pltpu.get_barrier_semaphore()
    for k in range(1, parts):
        pl.semaphore_signal(
            barrier, inc=1, device_id=(lax.rem(me + k, parts), shard),
            device_id_type=pl.DeviceIdType.MESH,
        )
    pl.semaphore_wait(barrier, parts - 1)

    def send(sources, targets, sends, gots, pick):
        copies = []
        for k in range(1, parts):
            peer = lax.rem(me + k, parts)
            for i in range(count):
                copy = pltpu.make_async_remote_copy(
                    src_ref=pick(sources[i], peer),
                    dst_ref=targets[i].at[k],
                    send_sem=sends.at[i, k],
                    recv_sem=gots.at[i, k],
                    device_id=(peer, shard),
                    device_id_type=pl.DeviceIdType.MESH,
                )
                copy.start()
                copies.append(copy)
        return copies

    first = send(x_refs, recv_one, send_one, got_one, lambda ref, peer: ref.at[peer])
    totals = [x_refs[i][me].astype(jnp.float32) for i in range(count)]
    for n, copy in enumerate(first):
        copy.wait_recv()
        k, i = n // count + 1, n % count
        totals[i] = totals[i] + recv_one[i][k].astype(jnp.float32)
    for i in range(count):
        mine[i][...] = totals[i].astype(mine[i].dtype)
        out_refs[i][me] = mine[i][...]
    second = send(mine, recv_two, send_two, got_two, lambda ref, peer: ref)
    for copy in first:
        copy.wait_send()
    for n, copy in enumerate(second):
        copy.wait_recv()
        k, i = n // count + 1, n % count
        out_refs[i][lax.rem(me + parts - k, parts)] = recv_two[i][k]
    for copy in second:
        copy.wait_send()


def summed_over_dp(arrays, slot):
    parts = lax.axis_size("dp")
    count = len(arrays)
    stacked = [a.reshape((parts, a.shape[0] // parts) + a.shape[1:]) for a in arrays]
    vmem = pl.BlockSpec(memory_space=pltpu.VMEM)
    results = pl.pallas_call(
        partial(dp_sum_kernel, parts, count),
        out_shape=[jax.ShapeDtypeStruct(s.shape, s.dtype) for s in stacked],
        in_specs=[vmem] * count,
        out_specs=[vmem] * count,
        scratch_shapes=[pltpu.VMEM(s.shape, s.dtype) for s in stacked] * 2
        + [pltpu.VMEM(s.shape[1:], s.dtype) for s in stacked]
        + [pltpu.SemaphoreType.DMA((count, parts))] * 4,
        compiler_params=pltpu.CompilerParams(collective_id=slot, has_side_effects=True),
    )(*stacked)
    return [r.reshape(a.shape) for r, a in zip(results, arrays)]


def zero_gather_kernel(parts, x_ref, out_ref, own_sem, send_sem, got_sem):
    me = lax.axis_index("zero")
    row = lax.axis_index("dp")
    barrier = pltpu.get_barrier_semaphore()
    for k in range(1, parts):
        pl.semaphore_signal(
            barrier, inc=1, device_id=(row, lax.rem(me + k, parts)),
            device_id_type=pl.DeviceIdType.MESH,
        )
    pl.semaphore_wait(barrier, parts - 1)
    own = pltpu.make_async_copy(x_ref, out_ref.at[me], own_sem)
    own.start()
    copies = []
    for k in range(1, parts):
        copy = pltpu.make_async_remote_copy(
            src_ref=x_ref,
            dst_ref=out_ref.at[me],
            send_sem=send_sem.at[k],
            recv_sem=got_sem.at[k],
            device_id=(row, lax.rem(me + k, parts)),
            device_id_type=pl.DeviceIdType.MESH,
        )
        copy.start()
        copies.append(copy)
    own.wait()
    for copy in copies:
        copy.wait_recv()
    for copy in copies:
        copy.wait_send()


def gathered_over_zero(shard):
    parts = lax.axis_size("zero")
    anywhere = pl.BlockSpec(memory_space=pl.ANY)
    whole = pl.pallas_call(
        partial(zero_gather_kernel, parts),
        out_shape=jax.ShapeDtypeStruct((parts,) + shard.shape, shard.dtype),
        in_specs=[anywhere],
        out_specs=anywhere,
        scratch_shapes=[
            pltpu.SemaphoreType.DMA(()),
            pltpu.SemaphoreType.DMA((parts,)),
            pltpu.SemaphoreType.DMA((parts,)),
        ],
        compiler_params=pltpu.CompilerParams(collective_id=2, has_side_effects=True),
    )(shard)
    return whole.reshape((parts * shard.shape[0],) + shard.shape[1:])


def gelu_tanh(inputs):
    inner = 0.7978845608028654 * (inputs + 0.044715 * inputs * inputs * inputs)
    return 0.5 * inputs * (1.0 + jnp.tanh(inner))


def layer_norm(inputs, gain_row, bias_row):
    average = jnp.mean(inputs, axis=-1, keepdims=True)
    centred = inputs - average
    variance = jnp.mean(centred * centred, axis=-1, keepdims=True)
    return centred * lax.rsqrt(variance + eps_norm) * gain_row + bias_row


def allowed_mask(seg_rows):
    length = seg_rows.shape[1]
    places = lax.iota(jnp.int32, length)
    causal = places[:, None] >= places[None, :]
    same_doc = seg_rows[:, :, None] == seg_rows[:, None, :]
    return jnp.logical_and(same_doc, causal[None])[:, None]


def attend_scores(queries, keys_in, seg_rows):
    scaling = queries.shape[-1] ** (-0.5)
    scores = (
        jnp.einsum("rqhe,rkhe->rhqk", queries, keys_in, preferred_element_type=jnp.float32)
        * scaling
    )
    return (scores, allowed_mask(seg_rows), scaling)


def attention_forward(queries, keys_in, values, seg_rows):
    scores, allowed, scaling = attend_scores(queries, keys_in, seg_rows)
    exponent = jnp.where(allowed, jnp.exp(scores), 0.0)
    log_total = jnp.log(jnp.sum(exponent, axis=-1, keepdims=True))
    attn_weights = jnp.where(allowed, jnp.exp(scores - log_total), 0.0).astype(jnp.bfloat16)
    attended = jnp.einsum(
        "rhqk,rkhe->rqhe", attn_weights, values, preferred_element_type=jnp.float32
    )
    return (attended.astype(jnp.bfloat16), log_total)


def attention_backward(queries, keys_in, values, seg_rows, log_total, grad_att):
    scores, allowed, scaling = attend_scores(queries, keys_in, seg_rows)
    weights_full = jnp.where(allowed, jnp.exp(scores - log_total), 0.0)
    weights_half = weights_full.astype(jnp.bfloat16)
    grad_values = jnp.einsum(
        "rhqk,rqhe->rkhe", weights_half, grad_att, preferred_element_type=jnp.float32
    )
    grad_weights = jnp.einsum(
        "rqhe,rkhe->rhqk", grad_att, values, preferred_element_type=jnp.float32
    )
    row_dot = jnp.sum(weights_full * grad_weights, axis=-1, keepdims=True)
    grad_scores = (weights_full * (grad_weights - row_dot) * scaling).astype(jnp.bfloat16)
    grad_queries = jnp.einsum(
        "rhqk,rkhe->rqhe", grad_scores, keys_in, preferred_element_type=jnp.float32
    )
    grad_keys = jnp.einsum(
        "rhqk,rqhe->rkhe", grad_scores, queries, preferred_element_type=jnp.float32
    )
    return (grad_queries, grad_keys, grad_values)


def block_pass(tokens_in, cot_in, seg_rows, qkv_mat, out_mat, fc_mat, proj_mat, vec_rows):
    count_tok = tokens_in.shape[0]
    width = tokens_in.shape[1]
    head_width = width // HEADS
    row_count = count_tok // SEQ
    split_shape = (row_count, SEQ, HEADS, head_width)
    tokens32 = tokens_in.astype(jnp.float32)
    normed_one = layer_norm(tokens32, vec_rows[0], vec_rows[1]).astype(jnp.bfloat16)
    projected = jnp.dot(normed_one, qkv_mat, preferred_element_type=jnp.float32)
    queries = (projected[:, :width] + vec_rows[2]).astype(jnp.bfloat16).reshape(split_shape)
    keys_in = projected[:, width : 2 * width].astype(jnp.bfloat16).reshape(split_shape)
    values = (projected[:, 2 * width :] + vec_rows[3]).astype(jnp.bfloat16).reshape(split_shape)
    attended, log_total = attention_forward(queries, keys_in, values, seg_rows)
    attended = attended.reshape(count_tok, width)
    middle = tokens32 + jnp.dot(attended, out_mat, preferred_element_type=jnp.float32) + vec_rows[4]
    normed_two = layer_norm(middle, vec_rows[5], vec_rows[6]).astype(jnp.bfloat16)
    fc_bias = vec_rows[8:].reshape(-1)
    hidden_pre = jnp.dot(normed_two, fc_mat, preferred_element_type=jnp.float32) + fc_bias
    hidden = gelu_tanh(hidden_pre).astype(jnp.bfloat16)
    block_out = (
        middle + jnp.dot(hidden, proj_mat, preferred_element_type=jnp.float32) + vec_rows[7]
    ).astype(jnp.bfloat16)
    cot32 = cot_in.astype(jnp.float32)
    grad_proj = jnp.dot(hidden.T, cot_in, preferred_element_type=jnp.float32).astype(jnp.bfloat16)
    grad_proj, cot_in, hidden_pre, middle = lax.optimization_barrier(
        (grad_proj, cot_in, hidden_pre, middle)
    )
    grad_hidden = jnp.dot(cot_in, proj_mat.T, preferred_element_type=jnp.float32)
    gelu_back = jax.vjp(gelu_tanh, hidden_pre)[1]
    grad_pre = gelu_back(grad_hidden)[0]
    grad_pre_half = grad_pre.astype(jnp.bfloat16)
    grad_fc = jnp.dot(normed_two.T, grad_pre_half, preferred_element_type=jnp.float32)
    grad_normed_two = jnp.dot(grad_pre_half, fc_mat.T, preferred_element_type=jnp.float32)
    norm_two_back = jax.vjp(layer_norm, middle, vec_rows[5], vec_rows[6])[1]
    grad_mid_norm, grad_gain_two, grad_bias_two = norm_two_back(grad_normed_two)
    grad_middle = cot32 + grad_mid_norm
    grad_middle_half = grad_middle.astype(jnp.bfloat16)
    grad_out = jnp.dot(attended.T, grad_middle_half, preferred_element_type=jnp.float32)
    grad_attended = jnp.dot(grad_middle_half, out_mat.T, preferred_element_type=jnp.float32)
    grad_attended = grad_attended.astype(jnp.bfloat16).reshape(split_shape)
    grad_queries, grad_keys, grad_values = attention_backward(
        queries, keys_in, values, seg_rows, log_total, grad_attended
    )
    flat_queries = grad_queries.reshape(count_tok, width)
    flat_keys = grad_keys.reshape(count_tok, width)
    flat_values = grad_values.reshape(count_tok, width)
    grad_projected = jnp.concatenate([flat_queries, flat_keys, flat_values], axis=1).astype(
        jnp.bfloat16
    )
    grad_qkv = jnp.dot(normed_one.T, grad_projected, preferred_element_type=jnp.float32)
    grad_normed_one = jnp.dot(grad_projected, qkv_mat.T, preferred_element_type=jnp.float32)
    norm_one_back = jax.vjp(layer_norm, tokens32, vec_rows[0], vec_rows[1])[1]
    grad_tok_norm, grad_gain_one, grad_bias_one = norm_one_back(grad_normed_one)
    input_grad = (grad_middle + grad_tok_norm).astype(jnp.bfloat16)
    small_rows = jnp.stack(
        [
            grad_gain_one,
            grad_bias_one,
            jnp.sum(flat_queries, axis=0),
            jnp.sum(flat_values, axis=0),
            jnp.sum(grad_middle, axis=0),
            grad_gain_two,
            grad_bias_two,
            jnp.sum(cot32, axis=0),
        ]
    )
    grad_vec = jnp.concatenate([small_rows, jnp.sum(grad_pre, axis=0).reshape(-1, width)], axis=0)
    return (block_out, input_grad, (grad_qkv, grad_out, grad_fc, grad_proj, grad_vec))


def adam_step(weight, gradient, mean_old, square_old, rate, decay):
    mean_new = beta_first * mean_old + (1.0 - beta_first) * gradient
    square_new = beta_second * square_old + (1.0 - beta_second) * gradient * gradient
    mean_hat = mean_new / (1.0 - beta_first**ADAM_STEP)
    square_hat = square_new / (1.0 - beta_second**ADAM_STEP)
    weight_new = weight - rate * (mean_hat / (jnp.sqrt(square_hat) + eps_adam) + decay * weight)
    return (weight_new, mean_new, square_new)


def local(
    tokens,
    cotangent,
    segments,
    w_qkv,
    w_out,
    w_fc,
    w_proj,
    vectors,
    mean_qkv,
    mean_out,
    mean_fc,
    mean_proj,
    mean_vectors,
    square_qkv,
    square_out,
    square_fc,
    square_proj,
    square_vectors,
):
    dp_size = lax.axis_size("dp")
    zero_size = lax.axis_size("zero")
    replicas = dp_size * zero_size
    vec_cols = jnp.pad(vectors.astype(jnp.bfloat16).T, ((0, 0), (0, LANE - vectors.shape[0])))
    first_mats = (w_qkv.astype(jnp.bfloat16), w_out.astype(jnp.bfloat16), w_fc.astype(jnp.bfloat16), vec_cols)
    first_all = lax.all_gather(jnp.concatenate(first_mats, axis=1), "zero", axis=0, tiled=True)
    proj_mat = gathered_over_zero(w_proj.astype(jnp.bfloat16))
    first_all, proj_mat = lax.optimization_barrier((first_all, proj_mat))
    widths = [m.shape[1] for m in first_mats]
    qkv_mat, out_mat, fc_mat, vec_cols_all = jnp.split(
        first_all, [sum(widths[:k]) for k in range(1, len(widths))], axis=1
    )
    vec_rows = vec_cols_all[:, : vectors.shape[0]].T.astype(jnp.float32)
    block_out, input_grad, local_grads = block_pass(
        tokens, cotangent, segments, qkv_mat, out_mat, fc_mat, proj_mat, vec_rows
    )
    grad_vec_cols = jnp.pad(
        local_grads[4].astype(jnp.bfloat16).T, ((0, 0), (0, LANE - vectors.shape[0]))
    )
    joined = jnp.concatenate(
        (
            local_grads[0].astype(jnp.bfloat16),
            local_grads[1].astype(jnp.bfloat16),
            local_grads[2].astype(jnp.bfloat16),
            grad_vec_cols,
        ),
        axis=1,
    )
    scattered = lax.psum_scatter(joined, "zero", scatter_dimension=0, tiled=True)
    proj_scattered = lax.psum_scatter(
        local_grads[3].astype(jnp.bfloat16), "zero", scatter_dimension=0, tiled=True
    )
    (summed_proj,) = summed_over_dp((proj_scattered,), 1)
    (summed_joined,) = summed_over_dp((scattered,), 0)
    ends = [w_qkv.shape[1], w_qkv.shape[1] + w_out.shape[1], w_qkv.shape[1] + w_out.shape[1] + w_fc.shape[1]]
    g_qkv, g_out, g_fc, g_vec = jnp.split(summed_joined, ends, axis=1)
    summed = (
        g_qkv.astype(jnp.float32),
        g_out.astype(jnp.float32),
        g_fc.astype(jnp.float32),
        summed_proj.astype(jnp.float32),
        lax.dot_general(
            g_vec[:, : vectors.shape[0]],
            jnp.eye(g_vec.shape[0], dtype=jnp.bfloat16),
            (((0,), (0,)), ((), ())),
            preferred_element_type=jnp.float32,
        ),
    )
    grads = jax.tree.map(partial(jnp.multiply, 1.0 / replicas), summed)
    first = adam_step(w_qkv, grads[0], mean_qkv, square_qkv, rate_matrix, decay_matrix)
    second = adam_step(w_out, grads[1], mean_out, square_out, rate_matrix, decay_matrix)
    third = adam_step(w_fc, grads[2], mean_fc, square_fc, rate_matrix, decay_matrix)
    fourth = adam_step(w_proj, grads[3], mean_proj, square_proj, rate_matrix, decay_matrix)
    fifth = adam_step(vectors, grads[4], mean_vectors, square_vectors, rate_vector, 0.0)
    return (
        block_out,
        input_grad,
        grads[0],
        grads[1],
        grads[2],
        grads[3],
        grads[4],
        first[0],
        second[0],
        third[0],
        fourth[0],
        fifth[0],
        first[1],
        second[1],
        third[1],
        fourth[1],
        fifth[1],
        first[2],
        second[2],
        third[2],
        fourth[2],
        fifth[2],
    )


def solution(mesh):
    placed = (
        P(("dp", "zero"), None),
        P(("dp", "zero"), None),
        P(("dp", "zero"), None),
        P("zero", None),
        P("zero", None),
        P("zero", None),
        P("zero", None),
        P(None, "zero"),
        P("zero", None),
        P("zero", None),
        P("zero", None),
        P("zero", None),
        P(None, "zero"),
        P("zero", None),
        P("zero", None),
        P("zero", None),
        P("zero", None),
        P(None, "zero"),
    )
    return jax.shard_map(
        local,
        mesh=mesh,
        in_specs=placed,
        out_specs=(
            P(("dp", "zero"), None),
            P(("dp", "zero"), None),
            P("zero", None),
            P("zero", None),
            P("zero", None),
            P("zero", None),
            P(None, "zero"),
            P("zero", None),
            P("zero", None),
            P("zero", None),
            P("zero", None),
            P(None, "zero"),
            P("zero", None),
            P("zero", None),
            P("zero", None),
            P("zero", None),
            P(None, "zero"),
            P("zero", None),
            P("zero", None),
            P("zero", None),
            P("zero", None),
            P(None, "zero"),
        ),
        check_vma=False,
    )
```

```python
from functools import partial

import jax
import jax.numpy as jnp
from jax import lax
from jax.experimental import pallas as pl
from jax.experimental.pallas import tpu as pltpu
from jax.sharding import PartitionSpec as P

HEADS = 16
SEQ = 128
ADAM_STEP = 3
LANE = 128
CHUNKS = 2


eps_norm = 1e-05
beta_first = 0.9
beta_second = 0.999
eps_adam = 1e-08
rate_matrix = 0.02
rate_vector = 0.15
decay_matrix = 0.1


def sent_together(arrays, axis, dim, along):
    widths = [a.shape[along] for a in arrays]
    both = jnp.concatenate(arrays, axis=along)
    result = lax.all_gather(both, axis, axis=dim, tiled=True)
    return tuple(jnp.split(result, [sum(widths[:k]) for k in range(1, len(widths))], axis=along))


def in_one_piece(arrays, axis, dim, along):
    ends, at = ([], 0)
    for a in arrays[:-1]:
        at += a.shape[along]
        ends.append(at)
    both = jnp.concatenate(arrays, axis=along)
    return tuple(
        jnp.split(lax.psum_scatter(both, axis, scatter_dimension=dim, tiled=True), ends, axis=along)
    )


def dp_sum_kernel(parts, count, chunks, *refs):
    x_refs, out_refs = refs[:count], refs[count : 2 * count]
    recv_one = refs[2 * count : 3 * count]
    mine = refs[3 * count : 4 * count]
    send_one, got_one, send_two, got_two = refs[4 * count :]
    me = lax.axis_index("dp")
    shard = lax.axis_index("zero")
    barrier = pltpu.get_barrier_semaphore()
    for k in range(1, parts):
        pl.semaphore_signal(
            barrier, inc=1, device_id=(lax.rem(me + k, parts), shard),
            device_id_type=pl.DeviceIdType.MESH,
        )
    pl.semaphore_wait(barrier, parts - 1)

    def columns(i, c):
        width = x_refs[i].shape[-1]
        cut = (width // LANE // chunks) * LANE
        start = c * cut
        return pl.ds(start, width - start if c == chunks - 1 else cut)

    def remote(src, dst, sends, gots, i, c, k):
        copy = pltpu.make_async_remote_copy(
            src_ref=src,
            dst_ref=dst,
            send_sem=sends.at[i, c, k],
            recv_sem=gots.at[i, c, k],
            device_id=(lax.rem(me + k, parts), shard),
            device_id_type=pl.DeviceIdType.MESH,
        )
        copy.start()
        return copy

    first = {}
    for c in range(chunks):
        for k in range(1, parts):
            peer = lax.rem(me + k, parts)
            for i in range(count):
                cols = columns(i, c)
                first[i, c, k] = remote(
                    x_refs[i].at[peer, :, cols], recv_one[i].at[k, :, cols],
                    send_one, got_one, i, c, k,
                )
    second = []
    for c in range(chunks):
        for i in range(count):
            cols = columns(i, c)
            total = x_refs[i][me, :, cols].astype(jnp.float32)
            for k in range(1, parts):
                first[i, c, k].wait_recv()
                total = total + recv_one[i][k, :, cols].astype(jnp.float32)
            mine[i][:, cols] = total.astype(mine[i].dtype)
            out_refs[i][me, :, cols] = mine[i][:, cols]
            for k in range(1, parts):
                second.append(
                    remote(
                        mine[i].at[:, cols], out_refs[i].at[me, :, cols],
                        send_two, got_two, i, c, k,
                    )
                )
    for copy in first.values():
        copy.wait_send()
    for copy in second:
        copy.wait_recv()
    for copy in second:
        copy.wait_send()


def summed_over_dp(arrays, slot):
    parts = lax.axis_size("dp")
    count = len(arrays)
    stacked = [a.reshape((parts, a.shape[0] // parts) + a.shape[1:]) for a in arrays]
    vmem = pl.BlockSpec(memory_space=pltpu.VMEM)
    results = pl.pallas_call(
        partial(dp_sum_kernel, parts, count, CHUNKS),
        out_shape=[jax.ShapeDtypeStruct(s.shape, s.dtype) for s in stacked],
        in_specs=[vmem] * count,
        out_specs=[vmem] * count,
        scratch_shapes=[pltpu.VMEM(s.shape, s.dtype) for s in stacked]
        + [pltpu.VMEM(s.shape[1:], s.dtype) for s in stacked]
        + [pltpu.SemaphoreType.DMA((count, CHUNKS, parts))] * 4,
        compiler_params=pltpu.CompilerParams(collective_id=slot, has_side_effects=True),
    )(*stacked)
    return [r.reshape(a.shape) for r, a in zip(results, arrays)]


def gelu_tanh(inputs):
    inner = 0.7978845608028654 * (inputs + 0.044715 * inputs * inputs * inputs)
    return 0.5 * inputs * (1.0 + jnp.tanh(inner))


def layer_norm(inputs, gain_row, bias_row):
    average = jnp.mean(inputs, axis=-1, keepdims=True)
    centred = inputs - average
    variance = jnp.mean(centred * centred, axis=-1, keepdims=True)
    return centred * lax.rsqrt(variance + eps_norm) * gain_row + bias_row


def allowed_mask(seg_rows):
    length = seg_rows.shape[1]
    places = lax.iota(jnp.int32, length)
    causal = places[:, None] >= places[None, :]
    same_doc = seg_rows[:, :, None] == seg_rows[:, None, :]
    return jnp.logical_and(same_doc, causal[None])[:, None]


def attend_scores(queries, keys_in, seg_rows):
    scaling = queries.shape[-1] ** (-0.5)
    scores = (
        jnp.einsum("rqhe,rkhe->rhqk", queries, keys_in, preferred_element_type=jnp.float32)
        * scaling
    )
    return (scores, allowed_mask(seg_rows), scaling)


def attention_forward(queries, keys_in, values, seg_rows):
    scores, allowed, scaling = attend_scores(queries, keys_in, seg_rows)
    exponent = jnp.where(allowed, jnp.exp(scores), 0.0)
    log_total = jnp.log(jnp.sum(exponent, axis=-1, keepdims=True))
    attn_weights = jnp.where(allowed, jnp.exp(scores - log_total), 0.0).astype(jnp.bfloat16)
    attended = jnp.einsum(
        "rhqk,rkhe->rqhe", attn_weights, values, preferred_element_type=jnp.float32
    )
    return (attended.astype(jnp.bfloat16), log_total)


def attention_backward(queries, keys_in, values, seg_rows, log_total, grad_att):
    scores, allowed, scaling = attend_scores(queries, keys_in, seg_rows)
    weights_full = jnp.where(allowed, jnp.exp(scores - log_total), 0.0)
    weights_half = weights_full.astype(jnp.bfloat16)
    grad_values = jnp.einsum(
        "rhqk,rqhe->rkhe", weights_half, grad_att, preferred_element_type=jnp.float32
    )
    grad_weights = jnp.einsum(
        "rqhe,rkhe->rhqk", grad_att, values, preferred_element_type=jnp.float32
    )
    row_dot = jnp.sum(weights_full * grad_weights, axis=-1, keepdims=True)
    grad_scores = (weights_full * (grad_weights - row_dot) * scaling).astype(jnp.bfloat16)
    grad_queries = jnp.einsum(
        "rhqk,rkhe->rqhe", grad_scores, keys_in, preferred_element_type=jnp.float32
    )
    grad_keys = jnp.einsum(
        "rhqk,rqhe->rkhe", grad_scores, queries, preferred_element_type=jnp.float32
    )
    return (grad_queries, grad_keys, grad_values)


def block_pass(tokens_in, cot_in, seg_rows, qkv_mat, out_mat, fc_mat, proj_mat, vec_rows):
    count_tok = tokens_in.shape[0]
    width = tokens_in.shape[1]
    head_width = width // HEADS
    row_count = count_tok // SEQ
    split_shape = (row_count, SEQ, HEADS, head_width)
    tokens32 = tokens_in.astype(jnp.float32)
    normed_one = layer_norm(tokens32, vec_rows[0], vec_rows[1]).astype(jnp.bfloat16)
    projected = jnp.dot(normed_one, qkv_mat, preferred_element_type=jnp.float32)
    queries = (projected[:, :width] + vec_rows[2]).astype(jnp.bfloat16).reshape(split_shape)
    keys_in = projected[:, width : 2 * width].astype(jnp.bfloat16).reshape(split_shape)
    values = (projected[:, 2 * width :] + vec_rows[3]).astype(jnp.bfloat16).reshape(split_shape)
    attended, log_total = attention_forward(queries, keys_in, values, seg_rows)
    attended = attended.reshape(count_tok, width)
    middle = tokens32 + jnp.dot(attended, out_mat, preferred_element_type=jnp.float32) + vec_rows[4]
    normed_two = layer_norm(middle, vec_rows[5], vec_rows[6]).astype(jnp.bfloat16)
    fc_bias = vec_rows[8:].reshape(-1)
    hidden_pre = jnp.dot(normed_two, fc_mat, preferred_element_type=jnp.float32) + fc_bias
    hidden = gelu_tanh(hidden_pre).astype(jnp.bfloat16)
    block_out = (
        middle + jnp.dot(hidden, proj_mat, preferred_element_type=jnp.float32) + vec_rows[7]
    ).astype(jnp.bfloat16)
    cot32 = cot_in.astype(jnp.float32)
    grad_proj = jnp.dot(hidden.T, cot_in, preferred_element_type=jnp.float32).astype(jnp.bfloat16)
    grad_proj, cot_in, hidden_pre, middle = lax.optimization_barrier(
        (grad_proj, cot_in, hidden_pre, middle)
    )
    grad_hidden = jnp.dot(cot_in, proj_mat.T, preferred_element_type=jnp.float32)
    gelu_back = jax.vjp(gelu_tanh, hidden_pre)[1]
    grad_pre = gelu_back(grad_hidden)[0]
    grad_pre_half = grad_pre.astype(jnp.bfloat16)
    grad_fc = jnp.dot(normed_two.T, grad_pre_half, preferred_element_type=jnp.float32)
    grad_normed_two = jnp.dot(grad_pre_half, fc_mat.T, preferred_element_type=jnp.float32)
    norm_two_back = jax.vjp(layer_norm, middle, vec_rows[5], vec_rows[6])[1]
    grad_mid_norm, grad_gain_two, grad_bias_two = norm_two_back(grad_normed_two)
    grad_middle = cot32 + grad_mid_norm
    grad_middle_half = grad_middle.astype(jnp.bfloat16)
    grad_out = jnp.dot(attended.T, grad_middle_half, preferred_element_type=jnp.float32)
    grad_attended = jnp.dot(grad_middle_half, out_mat.T, preferred_element_type=jnp.float32)
    grad_attended = grad_attended.astype(jnp.bfloat16).reshape(split_shape)
    grad_queries, grad_keys, grad_values = attention_backward(
        queries, keys_in, values, seg_rows, log_total, grad_attended
    )
    flat_queries = grad_queries.reshape(count_tok, width)
    flat_keys = grad_keys.reshape(count_tok, width)
    flat_values = grad_values.reshape(count_tok, width)
    grad_projected = jnp.concatenate([flat_queries, flat_keys, flat_values], axis=1).astype(
        jnp.bfloat16
    )
    grad_qkv = jnp.dot(normed_one.T, grad_projected, preferred_element_type=jnp.float32)
    grad_normed_one = jnp.dot(grad_projected, qkv_mat.T, preferred_element_type=jnp.float32)
    norm_one_back = jax.vjp(layer_norm, tokens32, vec_rows[0], vec_rows[1])[1]
    grad_tok_norm, grad_gain_one, grad_bias_one = norm_one_back(grad_normed_one)
    input_grad = (grad_middle + grad_tok_norm).astype(jnp.bfloat16)
    small_rows = jnp.stack(
        [
            grad_gain_one,
            grad_bias_one,
            jnp.sum(flat_queries, axis=0),
            jnp.sum(flat_values, axis=0),
            jnp.sum(grad_middle, axis=0),
            grad_gain_two,
            grad_bias_two,
            jnp.sum(cot32, axis=0),
        ]
    )
    grad_vec = jnp.concatenate([small_rows, jnp.sum(grad_pre, axis=0).reshape(-1, width)], axis=0)
    return (block_out, input_grad, (grad_qkv, grad_out, grad_fc, grad_proj, grad_vec))


def adam_step(weight, gradient, mean_old, square_old, rate, decay):
    mean_new = beta_first * mean_old + (1.0 - beta_first) * gradient
    square_new = beta_second * square_old + (1.0 - beta_second) * gradient * gradient
    mean_hat = mean_new / (1.0 - beta_first**ADAM_STEP)
    square_hat = square_new / (1.0 - beta_second**ADAM_STEP)
    weight_new = weight - rate * (mean_hat / (jnp.sqrt(square_hat) + eps_adam) + decay * weight)
    return (weight_new, mean_new, square_new)


def local(
    tokens,
    cotangent,
    segments,
    w_qkv,
    w_out,
    w_fc,
    w_proj,
    vectors,
    mean_qkv,
    mean_out,
    mean_fc,
    mean_proj,
    mean_vectors,
    square_qkv,
    square_out,
    square_fc,
    square_proj,
    square_vectors,
):
    dp_size = lax.axis_size("dp")
    zero_size = lax.axis_size("zero")
    replicas = dp_size * zero_size
    vec_cols = jnp.pad(vectors.astype(jnp.bfloat16).T, ((0, 0), (0, LANE - vectors.shape[0])))
    first_mats = (w_qkv.astype(jnp.bfloat16), w_out.astype(jnp.bfloat16), w_fc.astype(jnp.bfloat16), vec_cols)
    first_all = lax.all_gather(jnp.concatenate(first_mats, axis=1), "zero", axis=0, tiled=True)
    first_all, proj_shard = lax.optimization_barrier((first_all, w_proj.astype(jnp.bfloat16)))
    proj_mat = lax.all_gather(proj_shard, "zero", axis=0, tiled=True)
    widths = [m.shape[1] for m in first_mats]
    qkv_mat, out_mat, fc_mat, vec_cols_all = jnp.split(
        first_all, [sum(widths[:k]) for k in range(1, len(widths))], axis=1
    )
    vec_rows = vec_cols_all[:, : vectors.shape[0]].T.astype(jnp.float32)
    block_out, input_grad, local_grads = block_pass(
        tokens, cotangent, segments, qkv_mat, out_mat, fc_mat, proj_mat, vec_rows
    )
    grad_vec_cols = jnp.pad(
        local_grads[4].astype(jnp.bfloat16).T, ((0, 0), (0, LANE - vectors.shape[0]))
    )
    joined = jnp.concatenate(
        (
            local_grads[0].astype(jnp.bfloat16),
            local_grads[1].astype(jnp.bfloat16),
            local_grads[2].astype(jnp.bfloat16),
            grad_vec_cols,
        ),
        axis=1,
    )
    scattered = lax.psum_scatter(joined, "zero", scatter_dimension=0, tiled=True)
    proj_scattered = lax.psum_scatter(
        local_grads[3].astype(jnp.bfloat16), "zero", scatter_dimension=0, tiled=True
    )
    (summed_proj,) = summed_over_dp((proj_scattered,), 1)
    (summed_joined,) = summed_over_dp((scattered,), 0)
    ends = [w_qkv.shape[1], w_qkv.shape[1] + w_out.shape[1], w_qkv.shape[1] + w_out.shape[1] + w_fc.shape[1]]
    g_qkv, g_out, g_fc, g_vec = jnp.split(summed_joined, ends, axis=1)
    summed = (
        g_qkv.astype(jnp.float32),
        g_out.astype(jnp.float32),
        g_fc.astype(jnp.float32),
        summed_proj.astype(jnp.float32),
        lax.dot_general(
            g_vec[:, : vectors.shape[0]],
            jnp.eye(g_vec.shape[0], dtype=jnp.bfloat16),
            (((0,), (0,)), ((), ())),
            preferred_element_type=jnp.float32,
        ),
    )
    grads = jax.tree.map(partial(jnp.multiply, 1.0 / replicas), summed)
    first = adam_step(w_qkv, grads[0], mean_qkv, square_qkv, rate_matrix, decay_matrix)
    second = adam_step(w_out, grads[1], mean_out, square_out, rate_matrix, decay_matrix)
    third = adam_step(w_fc, grads[2], mean_fc, square_fc, rate_matrix, decay_matrix)
    fourth = adam_step(w_proj, grads[3], mean_proj, square_proj, rate_matrix, decay_matrix)
    fifth = adam_step(vectors, grads[4], mean_vectors, square_vectors, rate_vector, 0.0)
    return (
        block_out,
        input_grad,
        grads[0],
        grads[1],
        grads[2],
        grads[3],
        grads[4],
        first[0],
        second[0],
        third[0],
        fourth[0],
        fifth[0],
        first[1],
        second[1],
        third[1],
        fourth[1],
        fifth[1],
        first[2],
        second[2],
        third[2],
        fourth[2],
        fifth[2],
    )


def solution(mesh):
    placed = (
        P(("dp", "zero"), None),
        P(("dp", "zero"), None),
        P(("dp", "zero"), None),
        P("zero", None),
        P("zero", None),
        P("zero", None),
        P("zero", None),
        P(None, "zero"),
        P("zero", None),
        P("zero", None),
        P("zero", None),
        P("zero", None),
        P(None, "zero"),
        P("zero", None),
        P("zero", None),
        P("zero", None),
        P("zero", None),
        P(None, "zero"),
    )
    return jax.shard_map(
        local,
        mesh=mesh,
        in_specs=placed,
        out_specs=(
            P(("dp", "zero"), None),
            P(("dp", "zero"), None),
            P("zero", None),
            P("zero", None),
            P("zero", None),
            P("zero", None),
            P(None, "zero"),
            P("zero", None),
            P("zero", None),
            P("zero", None),
            P("zero", None),
            P(None, "zero"),
            P("zero", None),
            P("zero", None),
            P("zero", None),
            P("zero", None),
            P(None, "zero"),
            P("zero", None),
            P("zero", None),
            P("zero", None),
            P("zero", None),
            P(None, "zero"),
        ),
        check_vma=False,
    )
```

```python
from functools import partial

import jax
import jax.numpy as jnp
from jax import lax
from jax.experimental import pallas as pl
from jax.experimental.pallas import tpu as pltpu
from jax.sharding import PartitionSpec as P

HEADS = 16
SEQ = 128
ADAM_STEP = 3
LANE = 128
CHUNKS = 4


eps_norm = 1e-05
beta_first = 0.9
beta_second = 0.999
eps_adam = 1e-08
rate_matrix = 0.02
rate_vector = 0.15
decay_matrix = 0.1


def sent_together(arrays, axis, dim, along):
    widths = [a.shape[along] for a in arrays]
    both = jnp.concatenate(arrays, axis=along)
    result = lax.all_gather(both, axis, axis=dim, tiled=True)
    return tuple(jnp.split(result, [sum(widths[:k]) for k in range(1, len(widths))], axis=along))


def in_one_piece(arrays, axis, dim, along):
    ends, at = ([], 0)
    for a in arrays[:-1]:
        at += a.shape[along]
        ends.append(at)
    both = jnp.concatenate(arrays, axis=along)
    return tuple(
        jnp.split(lax.psum_scatter(both, axis, scatter_dimension=dim, tiled=True), ends, axis=along)
    )


def dp_sum_kernel(parts, count, chunks, *refs):
    x_refs, out_refs = refs[:count], refs[count : 2 * count]
    recv_one = refs[2 * count : 3 * count]
    mine = refs[3 * count : 4 * count]
    send_one, got_one, send_two, got_two = refs[4 * count :]
    me = lax.axis_index("dp")
    shard = lax.axis_index("zero")
    barrier = pltpu.get_barrier_semaphore()
    for k in range(1, parts):
        pl.semaphore_signal(
            barrier, inc=1, device_id=(lax.rem(me + k, parts), shard),
            device_id_type=pl.DeviceIdType.MESH,
        )
    pl.semaphore_wait(barrier, parts - 1)

    def columns(i, c):
        width = x_refs[i].shape[-1]
        cut = (width // LANE // chunks) * LANE
        start = c * cut
        return pl.ds(start, width - start if c == chunks - 1 else cut)

    def remote(src, dst, sends, gots, i, c, k):
        copy = pltpu.make_async_remote_copy(
            src_ref=src,
            dst_ref=dst,
            send_sem=sends.at[i, c, k],
            recv_sem=gots.at[i, c, k],
            device_id=(lax.rem(me + k, parts), shard),
            device_id_type=pl.DeviceIdType.MESH,
        )
        copy.start()
        return copy

    first = {}
    for c in range(chunks):
        for k in range(1, parts):
            peer = lax.rem(me + k, parts)
            for i in range(count):
                cols = columns(i, c)
                first[i, c, k] = remote(
                    x_refs[i].at[peer, :, cols], recv_one[i].at[k, :, cols],
                    send_one, got_one, i, c, k,
                )
    second = []
    for c in range(chunks):
        for i in range(count):
            cols = columns(i, c)
            total = x_refs[i][me, :, cols].astype(jnp.float32)
            for k in range(1, parts):
                first[i, c, k].wait_recv()
                total = total + recv_one[i][k, :, cols].astype(jnp.float32)
            mine[i][:, cols] = total.astype(mine[i].dtype)
            out_refs[i][me, :, cols] = mine[i][:, cols]
            for k in range(1, parts):
                second.append(
                    remote(
                        mine[i].at[:, cols], out_refs[i].at[me, :, cols],
                        send_two, got_two, i, c, k,
                    )
                )
    for copy in first.values():
        copy.wait_send()
    for copy in second:
        copy.wait_recv()
    for copy in second:
        copy.wait_send()


def summed_over_dp(arrays, slot):
    parts = lax.axis_size("dp")
    count = len(arrays)
    stacked = [a.reshape((parts, a.shape[0] // parts) + a.shape[1:]) for a in arrays]
    vmem = pl.BlockSpec(memory_space=pltpu.VMEM)
    results = pl.pallas_call(
        partial(dp_sum_kernel, parts, count, CHUNKS),
        out_shape=[jax.ShapeDtypeStruct(s.shape, s.dtype) for s in stacked],
        in_specs=[vmem] * count,
        out_specs=[vmem] * count,
        scratch_shapes=[pltpu.VMEM(s.shape, s.dtype) for s in stacked]
        + [pltpu.VMEM(s.shape[1:], s.dtype) for s in stacked]
        + [pltpu.SemaphoreType.DMA((count, CHUNKS, parts))] * 4,
        compiler_params=pltpu.CompilerParams(collective_id=slot, has_side_effects=True),
    )(*stacked)
    return [r.reshape(a.shape) for r, a in zip(results, arrays)]


def gelu_tanh(inputs):
    inner = 0.7978845608028654 * (inputs + 0.044715 * inputs * inputs * inputs)
    return 0.5 * inputs * (1.0 + jnp.tanh(inner))


def layer_norm(inputs, gain_row, bias_row):
    average = jnp.mean(inputs, axis=-1, keepdims=True)
    centred = inputs - average
    variance = jnp.mean(centred * centred, axis=-1, keepdims=True)
    return centred * lax.rsqrt(variance + eps_norm) * gain_row + bias_row


def allowed_mask(seg_rows):
    length = seg_rows.shape[1]
    places = lax.iota(jnp.int32, length)
    causal = places[:, None] >= places[None, :]
    same_doc = seg_rows[:, :, None] == seg_rows[:, None, :]
    return jnp.logical_and(same_doc, causal[None])[:, None]


def attend_scores(queries, keys_in, seg_rows):
    scaling = queries.shape[-1] ** (-0.5)
    scores = (
        jnp.einsum("rqhe,rkhe->rhqk", queries, keys_in, preferred_element_type=jnp.float32)
        * scaling
    )
    return (scores, allowed_mask(seg_rows), scaling)


def attention_forward(queries, keys_in, values, seg_rows):
    scores, allowed, scaling = attend_scores(queries, keys_in, seg_rows)
    exponent = jnp.where(allowed, jnp.exp(scores), 0.0)
    log_total = jnp.log(jnp.sum(exponent, axis=-1, keepdims=True))
    attn_weights = jnp.where(allowed, jnp.exp(scores - log_total), 0.0).astype(jnp.bfloat16)
    attended = jnp.einsum(
        "rhqk,rkhe->rqhe", attn_weights, values, preferred_element_type=jnp.float32
    )
    return (attended.astype(jnp.bfloat16), log_total)


def attention_backward(queries, keys_in, values, seg_rows, log_total, grad_att):
    scores, allowed, scaling = attend_scores(queries, keys_in, seg_rows)
    weights_full = jnp.where(allowed, jnp.exp(scores - log_total), 0.0)
    weights_half = weights_full.astype(jnp.bfloat16)
    grad_values = jnp.einsum(
        "rhqk,rqhe->rkhe", weights_half, grad_att, preferred_element_type=jnp.float32
    )
    grad_weights = jnp.einsum(
        "rqhe,rkhe->rhqk", grad_att, values, preferred_element_type=jnp.float32
    )
    row_dot = jnp.sum(weights_full * grad_weights, axis=-1, keepdims=True)
    grad_scores = (weights_full * (grad_weights - row_dot) * scaling).astype(jnp.bfloat16)
    grad_queries = jnp.einsum(
        "rhqk,rkhe->rqhe", grad_scores, keys_in, preferred_element_type=jnp.float32
    )
    grad_keys = jnp.einsum(
        "rhqk,rqhe->rkhe", grad_scores, queries, preferred_element_type=jnp.float32
    )
    return (grad_queries, grad_keys, grad_values)


def block_pass(tokens_in, cot_in, seg_rows, qkv_mat, out_mat, fc_mat, proj_mat, vec_rows):
    count_tok = tokens_in.shape[0]
    width = tokens_in.shape[1]
    head_width = width // HEADS
    row_count = count_tok // SEQ
    split_shape = (row_count, SEQ, HEADS, head_width)
    tokens32 = tokens_in.astype(jnp.float32)
    normed_one = layer_norm(tokens32, vec_rows[0], vec_rows[1]).astype(jnp.bfloat16)
    projected = jnp.dot(normed_one, qkv_mat, preferred_element_type=jnp.float32)
    queries = (projected[:, :width] + vec_rows[2]).astype(jnp.bfloat16).reshape(split_shape)
    keys_in = projected[:, width : 2 * width].astype(jnp.bfloat16).reshape(split_shape)
    values = (projected[:, 2 * width :] + vec_rows[3]).astype(jnp.bfloat16).reshape(split_shape)
    attended, log_total = attention_forward(queries, keys_in, values, seg_rows)
    attended = attended.reshape(count_tok, width)
    middle = tokens32 + jnp.dot(attended, out_mat, preferred_element_type=jnp.float32) + vec_rows[4]
    normed_two = layer_norm(middle, vec_rows[5], vec_rows[6]).astype(jnp.bfloat16)
    fc_bias = vec_rows[8:].reshape(-1)
    hidden_pre = jnp.dot(normed_two, fc_mat, preferred_element_type=jnp.float32) + fc_bias
    hidden = gelu_tanh(hidden_pre).astype(jnp.bfloat16)
    block_out = (
        middle + jnp.dot(hidden, proj_mat, preferred_element_type=jnp.float32) + vec_rows[7]
    ).astype(jnp.bfloat16)
    cot32 = cot_in.astype(jnp.float32)
    grad_proj = jnp.dot(hidden.T, cot_in, preferred_element_type=jnp.float32).astype(jnp.bfloat16)
    grad_proj, cot_in, hidden_pre, middle = lax.optimization_barrier(
        (grad_proj, cot_in, hidden_pre, middle)
    )
    grad_hidden = jnp.dot(cot_in, proj_mat.T, preferred_element_type=jnp.float32)
    gelu_back = jax.vjp(gelu_tanh, hidden_pre)[1]
    grad_pre = gelu_back(grad_hidden)[0]
    grad_pre_half = grad_pre.astype(jnp.bfloat16)
    grad_fc = jnp.dot(normed_two.T, grad_pre_half, preferred_element_type=jnp.float32)
    grad_normed_two = jnp.dot(grad_pre_half, fc_mat.T, preferred_element_type=jnp.float32)
    norm_two_back = jax.vjp(layer_norm, middle, vec_rows[5], vec_rows[6])[1]
    grad_mid_norm, grad_gain_two, grad_bias_two = norm_two_back(grad_normed_two)
    grad_middle = cot32 + grad_mid_norm
    grad_middle_half = grad_middle.astype(jnp.bfloat16)
    grad_out = jnp.dot(attended.T, grad_middle_half, preferred_element_type=jnp.float32)
    grad_attended = jnp.dot(grad_middle_half, out_mat.T, preferred_element_type=jnp.float32)
    grad_attended = grad_attended.astype(jnp.bfloat16).reshape(split_shape)
    grad_queries, grad_keys, grad_values = attention_backward(
        queries, keys_in, values, seg_rows, log_total, grad_attended
    )
    flat_queries = grad_queries.reshape(count_tok, width)
    flat_keys = grad_keys.reshape(count_tok, width)
    flat_values = grad_values.reshape(count_tok, width)
    grad_projected = jnp.concatenate([flat_queries, flat_keys, flat_values], axis=1).astype(
        jnp.bfloat16
    )
    grad_qkv = jnp.dot(normed_one.T, grad_projected, preferred_element_type=jnp.float32)
    grad_normed_one = jnp.dot(grad_projected, qkv_mat.T, preferred_element_type=jnp.float32)
    norm_one_back = jax.vjp(layer_norm, tokens32, vec_rows[0], vec_rows[1])[1]
    grad_tok_norm, grad_gain_one, grad_bias_one = norm_one_back(grad_normed_one)
    input_grad = (grad_middle + grad_tok_norm).astype(jnp.bfloat16)
    small_rows = jnp.stack(
        [
            grad_gain_one,
            grad_bias_one,
            jnp.sum(flat_queries, axis=0),
            jnp.sum(flat_values, axis=0),
            jnp.sum(grad_middle, axis=0),
            grad_gain_two,
            grad_bias_two,
            jnp.sum(cot32, axis=0),
        ]
    )
    grad_vec = jnp.concatenate([small_rows, jnp.sum(grad_pre, axis=0).reshape(-1, width)], axis=0)
    return (block_out, input_grad, (grad_qkv, grad_out, grad_fc, grad_proj, grad_vec))


def adam_step(weight, gradient, mean_old, square_old, rate, decay):
    mean_new = beta_first * mean_old + (1.0 - beta_first) * gradient
    square_new = beta_second * square_old + (1.0 - beta_second) * gradient * gradient
    mean_hat = mean_new / (1.0 - beta_first**ADAM_STEP)
    square_hat = square_new / (1.0 - beta_second**ADAM_STEP)
    weight_new = weight - rate * (mean_hat / (jnp.sqrt(square_hat) + eps_adam) + decay * weight)
    return (weight_new, mean_new, square_new)


def local(
    tokens,
    cotangent,
    segments,
    w_qkv,
    w_out,
    w_fc,
    w_proj,
    vectors,
    mean_qkv,
    mean_out,
    mean_fc,
    mean_proj,
    mean_vectors,
    square_qkv,
    square_out,
    square_fc,
    square_proj,
    square_vectors,
):
    dp_size = lax.axis_size("dp")
    zero_size = lax.axis_size("zero")
    replicas = dp_size * zero_size
    vec_cols = jnp.pad(vectors.astype(jnp.bfloat16).T, ((0, 0), (0, LANE - vectors.shape[0])))
    first_mats = (w_qkv.astype(jnp.bfloat16), w_out.astype(jnp.bfloat16), w_fc.astype(jnp.bfloat16), vec_cols)
    first_all = lax.all_gather(jnp.concatenate(first_mats, axis=1), "zero", axis=0, tiled=True)
    first_all, proj_shard = lax.optimization_barrier((first_all, w_proj.astype(jnp.bfloat16)))
    proj_mat = lax.all_gather(proj_shard, "zero", axis=0, tiled=True)
    widths = [m.shape[1] for m in first_mats]
    qkv_mat, out_mat, fc_mat, vec_cols_all = jnp.split(
        first_all, [sum(widths[:k]) for k in range(1, len(widths))], axis=1
    )
    vec_rows = vec_cols_all[:, : vectors.shape[0]].T.astype(jnp.float32)
    block_out, input_grad, local_grads = block_pass(
        tokens, cotangent, segments, qkv_mat, out_mat, fc_mat, proj_mat, vec_rows
    )
    grad_vec_cols = jnp.pad(
        local_grads[4].astype(jnp.bfloat16).T, ((0, 0), (0, LANE - vectors.shape[0]))
    )
    joined = jnp.concatenate(
        (
            local_grads[0].astype(jnp.bfloat16),
            local_grads[1].astype(jnp.bfloat16),
            local_grads[2].astype(jnp.bfloat16),
            grad_vec_cols,
        ),
        axis=1,
    )
    scattered = lax.psum_scatter(joined, "zero", scatter_dimension=0, tiled=True)
    proj_scattered = lax.psum_scatter(
        local_grads[3].astype(jnp.bfloat16), "zero", scatter_dimension=0, tiled=True
    )
    (summed_proj,) = summed_over_dp((proj_scattered,), 1)
    (summed_joined,) = summed_over_dp((scattered,), 0)
    ends = [w_qkv.shape[1], w_qkv.shape[1] + w_out.shape[1], w_qkv.shape[1] + w_out.shape[1] + w_fc.shape[1]]
    g_qkv, g_out, g_fc, g_vec = jnp.split(summed_joined, ends, axis=1)
    summed = (
        g_qkv.astype(jnp.float32),
        g_out.astype(jnp.float32),
        g_fc.astype(jnp.float32),
        summed_proj.astype(jnp.float32),
        lax.dot_general(
            g_vec[:, : vectors.shape[0]],
            jnp.eye(g_vec.shape[0], dtype=jnp.bfloat16),
            (((0,), (0,)), ((), ())),
            preferred_element_type=jnp.float32,
        ),
    )
    grads = jax.tree.map(partial(jnp.multiply, 1.0 / replicas), summed)
    first = adam_step(w_qkv, grads[0], mean_qkv, square_qkv, rate_matrix, decay_matrix)
    second = adam_step(w_out, grads[1], mean_out, square_out, rate_matrix, decay_matrix)
    third = adam_step(w_fc, grads[2], mean_fc, square_fc, rate_matrix, decay_matrix)
    fourth = adam_step(w_proj, grads[3], mean_proj, square_proj, rate_matrix, decay_matrix)
    fifth = adam_step(vectors, grads[4], mean_vectors, square_vectors, rate_vector, 0.0)
    return (
        block_out,
        input_grad,
        grads[0],
        grads[1],
        grads[2],
        grads[3],
        grads[4],
        first[0],
        second[0],
        third[0],
        fourth[0],
        fifth[0],
        first[1],
        second[1],
        third[1],
        fourth[1],
        fifth[1],
        first[2],
        second[2],
        third[2],
        fourth[2],
        fifth[2],
    )


def solution(mesh):
    placed = (
        P(("dp", "zero"), None),
        P(("dp", "zero"), None),
        P(("dp", "zero"), None),
        P("zero", None),
        P("zero", None),
        P("zero", None),
        P("zero", None),
        P(None, "zero"),
        P("zero", None),
        P("zero", None),
        P("zero", None),
        P("zero", None),
        P(None, "zero"),
        P("zero", None),
        P("zero", None),
        P("zero", None),
        P("zero", None),
        P(None, "zero"),
    )
    return jax.shard_map(
        local,
        mesh=mesh,
        in_specs=placed,
        out_specs=(
            P(("dp", "zero"), None),
            P(("dp", "zero"), None),
            P("zero", None),
            P("zero", None),
            P("zero", None),
            P("zero", None),
            P(None, "zero"),
            P("zero", None),
            P("zero", None),
            P("zero", None),
            P("zero", None),
            P(None, "zero"),
            P("zero", None),
            P("zero", None),
            P("zero", None),
            P("zero", None),
            P(None, "zero"),
            P("zero", None),
            P("zero", None),
            P("zero", None),
            P("zero", None),
            P(None, "zero"),
        ),
        check_vma=False,
    )
```

```python
from functools import partial

import jax
import jax.numpy as jnp
from jax import lax
from jax.experimental import pallas as pl
from jax.experimental.pallas import tpu as pltpu
from jax.sharding import PartitionSpec as P

HEADS = 16
SEQ = 128
ADAM_STEP = 3
LANE = 128
CHUNKS = 3


eps_norm = 1e-05
beta_first = 0.9
beta_second = 0.999
eps_adam = 1e-08
rate_matrix = 0.02
rate_vector = 0.15
decay_matrix = 0.1


def sent_together(arrays, axis, dim, along):
    widths = [a.shape[along] for a in arrays]
    both = jnp.concatenate(arrays, axis=along)
    result = lax.all_gather(both, axis, axis=dim, tiled=True)
    return tuple(jnp.split(result, [sum(widths[:k]) for k in range(1, len(widths))], axis=along))


def in_one_piece(arrays, axis, dim, along):
    ends, at = ([], 0)
    for a in arrays[:-1]:
        at += a.shape[along]
        ends.append(at)
    both = jnp.concatenate(arrays, axis=along)
    return tuple(
        jnp.split(lax.psum_scatter(both, axis, scatter_dimension=dim, tiled=True), ends, axis=along)
    )


def dp_sum_kernel(parts, count, chunks, *refs):
    x_refs, out_refs = refs[:count], refs[count : 2 * count]
    recv_one = refs[2 * count : 3 * count]
    mine = refs[3 * count : 4 * count]
    send_one, got_one, send_two, got_two = refs[4 * count :]
    me = lax.axis_index("dp")
    shard = lax.axis_index("zero")
    barrier = pltpu.get_barrier_semaphore()
    for k in range(1, parts):
        pl.semaphore_signal(
            barrier, inc=1, device_id=(lax.rem(me + k, parts), shard),
            device_id_type=pl.DeviceIdType.MESH,
        )
    pl.semaphore_wait(barrier, parts - 1)

    def columns(i, c):
        width = x_refs[i].shape[-1]
        cut = (width // LANE // chunks) * LANE
        start = c * cut
        return pl.ds(start, width - start if c == chunks - 1 else cut)

    def remote(src, dst, sends, gots, i, c, k):
        copy = pltpu.make_async_remote_copy(
            src_ref=src,
            dst_ref=dst,
            send_sem=sends.at[i, c, k],
            recv_sem=gots.at[i, c, k],
            device_id=(lax.rem(me + k, parts), shard),
            device_id_type=pl.DeviceIdType.MESH,
        )
        copy.start()
        return copy

    first = {}
    for c in range(chunks):
        for k in range(1, parts):
            peer = lax.rem(me + k, parts)
            for i in range(count):
                cols = columns(i, c)
                first[i, c, k] = remote(
                    x_refs[i].at[peer, :, cols], recv_one[i].at[k, :, cols],
                    send_one, got_one, i, c, k,
                )
    second = []
    for c in range(chunks):
        for i in range(count):
            cols = columns(i, c)
            total = x_refs[i][me, :, cols].astype(jnp.float32)
            for k in range(1, parts):
                first[i, c, k].wait_recv()
                total = total + recv_one[i][k, :, cols].astype(jnp.float32)
            mine[i][:, cols] = total.astype(mine[i].dtype)
            out_refs[i][me, :, cols] = mine[i][:, cols]
            for k in range(1, parts):
                second.append(
                    remote(
                        mine[i].at[:, cols], out_refs[i].at[me, :, cols],
                        send_two, got_two, i, c, k,
                    )
                )
    for copy in first.values():
        copy.wait_send()
    for copy in second:
        copy.wait_recv()
    for copy in second:
        copy.wait_send()


def summed_over_dp(arrays, slot):
    parts = lax.axis_size("dp")
    count = len(arrays)
    stacked = [a.reshape((parts, a.shape[0] // parts) + a.shape[1:]) for a in arrays]
    vmem = pl.BlockSpec(memory_space=pltpu.VMEM)
    results = pl.pallas_call(
        partial(dp_sum_kernel, parts, count, CHUNKS),
        out_shape=[jax.ShapeDtypeStruct(s.shape, s.dtype) for s in stacked],
        in_specs=[vmem] * count,
        out_specs=[vmem] * count,
        scratch_shapes=[pltpu.VMEM(s.shape, s.dtype) for s in stacked]
        + [pltpu.VMEM(s.shape[1:], s.dtype) for s in stacked]
        + [pltpu.SemaphoreType.DMA((count, CHUNKS, parts))] * 4,
        compiler_params=pltpu.CompilerParams(collective_id=slot, has_side_effects=True),
    )(*stacked)
    return [r.reshape(a.shape) for r, a in zip(results, arrays)]


def gelu_tanh(inputs):
    inner = 0.7978845608028654 * (inputs + 0.044715 * inputs * inputs * inputs)
    return 0.5 * inputs * (1.0 + jnp.tanh(inner))


def layer_norm(inputs, gain_row, bias_row):
    average = jnp.mean(inputs, axis=-1, keepdims=True)
    centred = inputs - average
    variance = jnp.mean(centred * centred, axis=-1, keepdims=True)
    return centred * lax.rsqrt(variance + eps_norm) * gain_row + bias_row


def allowed_mask(seg_rows):
    length = seg_rows.shape[1]
    places = lax.iota(jnp.int32, length)
    causal = places[:, None] >= places[None, :]
    same_doc = seg_rows[:, :, None] == seg_rows[:, None, :]
    return jnp.logical_and(same_doc, causal[None])[:, None]


def attend_scores(queries, keys_in, seg_rows):
    scaling = queries.shape[-1] ** (-0.5)
    scores = (
        jnp.einsum("rqhe,rkhe->rhqk", queries, keys_in, preferred_element_type=jnp.float32)
        * scaling
    )
    return (scores, allowed_mask(seg_rows), scaling)


def attention_forward(queries, keys_in, values, seg_rows):
    scores, allowed, scaling = attend_scores(queries, keys_in, seg_rows)
    exponent = jnp.where(allowed, jnp.exp(scores), 0.0)
    log_total = jnp.log(jnp.sum(exponent, axis=-1, keepdims=True))
    attn_weights = jnp.where(allowed, jnp.exp(scores - log_total), 0.0).astype(jnp.bfloat16)
    attended = jnp.einsum(
        "rhqk,rkhe->rqhe", attn_weights, values, preferred_element_type=jnp.float32
    )
    return (attended.astype(jnp.bfloat16), log_total)


def attention_backward(queries, keys_in, values, seg_rows, log_total, grad_att):
    scores, allowed, scaling = attend_scores(queries, keys_in, seg_rows)
    weights_full = jnp.where(allowed, jnp.exp(scores - log_total), 0.0)
    weights_half = weights_full.astype(jnp.bfloat16)
    grad_values = jnp.einsum(
        "rhqk,rqhe->rkhe", weights_half, grad_att, preferred_element_type=jnp.float32
    )
    grad_weights = jnp.einsum(
        "rqhe,rkhe->rhqk", grad_att, values, preferred_element_type=jnp.float32
    )
    row_dot = jnp.sum(weights_full * grad_weights, axis=-1, keepdims=True)
    grad_scores = (weights_full * (grad_weights - row_dot) * scaling).astype(jnp.bfloat16)
    grad_queries = jnp.einsum(
        "rhqk,rkhe->rqhe", grad_scores, keys_in, preferred_element_type=jnp.float32
    )
    grad_keys = jnp.einsum(
        "rhqk,rqhe->rkhe", grad_scores, queries, preferred_element_type=jnp.float32
    )
    return (grad_queries, grad_keys, grad_values)


def block_pass(tokens_in, cot_in, seg_rows, qkv_mat, out_mat, fc_mat, proj_mat, vec_rows):
    count_tok = tokens_in.shape[0]
    width = tokens_in.shape[1]
    head_width = width // HEADS
    row_count = count_tok // SEQ
    split_shape = (row_count, SEQ, HEADS, head_width)
    tokens32 = tokens_in.astype(jnp.float32)
    normed_one = layer_norm(tokens32, vec_rows[0], vec_rows[1]).astype(jnp.bfloat16)
    projected = jnp.dot(normed_one, qkv_mat, preferred_element_type=jnp.float32)
    queries = (projected[:, :width] + vec_rows[2]).astype(jnp.bfloat16).reshape(split_shape)
    keys_in = projected[:, width : 2 * width].astype(jnp.bfloat16).reshape(split_shape)
    values = (projected[:, 2 * width :] + vec_rows[3]).astype(jnp.bfloat16).reshape(split_shape)
    attended, log_total = attention_forward(queries, keys_in, values, seg_rows)
    attended = attended.reshape(count_tok, width)
    middle = tokens32 + jnp.dot(attended, out_mat, preferred_element_type=jnp.float32) + vec_rows[4]
    normed_two = layer_norm(middle, vec_rows[5], vec_rows[6]).astype(jnp.bfloat16)
    fc_bias = vec_rows[8:].reshape(-1)
    hidden_pre = jnp.dot(normed_two, fc_mat, preferred_element_type=jnp.float32) + fc_bias
    hidden = gelu_tanh(hidden_pre).astype(jnp.bfloat16)
    block_out = (
        middle + jnp.dot(hidden, proj_mat, preferred_element_type=jnp.float32) + vec_rows[7]
    ).astype(jnp.bfloat16)
    cot32 = cot_in.astype(jnp.float32)
    grad_proj = jnp.dot(hidden.T, cot_in, preferred_element_type=jnp.float32).astype(jnp.bfloat16)
    grad_proj, cot_in, hidden_pre, middle = lax.optimization_barrier(
        (grad_proj, cot_in, hidden_pre, middle)
    )
    grad_hidden = jnp.dot(cot_in, proj_mat.T, preferred_element_type=jnp.float32)
    gelu_back = jax.vjp(gelu_tanh, hidden_pre)[1]
    grad_pre = gelu_back(grad_hidden)[0]
    grad_pre_half = grad_pre.astype(jnp.bfloat16)
    grad_fc = jnp.dot(normed_two.T, grad_pre_half, preferred_element_type=jnp.float32)
    grad_normed_two = jnp.dot(grad_pre_half, fc_mat.T, preferred_element_type=jnp.float32)
    norm_two_back = jax.vjp(layer_norm, middle, vec_rows[5], vec_rows[6])[1]
    grad_mid_norm, grad_gain_two, grad_bias_two = norm_two_back(grad_normed_two)
    grad_middle = cot32 + grad_mid_norm
    grad_middle_half = grad_middle.astype(jnp.bfloat16)
    grad_out = jnp.dot(attended.T, grad_middle_half, preferred_element_type=jnp.float32)
    grad_attended = jnp.dot(grad_middle_half, out_mat.T, preferred_element_type=jnp.float32)
    grad_attended = grad_attended.astype(jnp.bfloat16).reshape(split_shape)
    grad_queries, grad_keys, grad_values = attention_backward(
        queries, keys_in, values, seg_rows, log_total, grad_attended
    )
    flat_queries = grad_queries.reshape(count_tok, width)
    flat_keys = grad_keys.reshape(count_tok, width)
    flat_values = grad_values.reshape(count_tok, width)
    grad_projected = jnp.concatenate([flat_queries, flat_keys, flat_values], axis=1).astype(
        jnp.bfloat16
    )
    grad_qkv = jnp.dot(normed_one.T, grad_projected, preferred_element_type=jnp.float32)
    grad_normed_one = jnp.dot(grad_projected, qkv_mat.T, preferred_element_type=jnp.float32)
    norm_one_back = jax.vjp(layer_norm, tokens32, vec_rows[0], vec_rows[1])[1]
    grad_tok_norm, grad_gain_one, grad_bias_one = norm_one_back(grad_normed_one)
    input_grad = (grad_middle + grad_tok_norm).astype(jnp.bfloat16)
    small_rows = jnp.stack(
        [
            grad_gain_one,
            grad_bias_one,
            jnp.sum(flat_queries, axis=0),
            jnp.sum(flat_values, axis=0),
            jnp.sum(grad_middle, axis=0),
            grad_gain_two,
            grad_bias_two,
            jnp.sum(cot32, axis=0),
        ]
    )
    grad_vec = jnp.concatenate([small_rows, jnp.sum(grad_pre, axis=0).reshape(-1, width)], axis=0)
    return (block_out, input_grad, (grad_qkv, grad_out, grad_fc, grad_proj, grad_vec))


def adam_step(weight, gradient, mean_old, square_old, rate, decay):
    mean_new = beta_first * mean_old + (1.0 - beta_first) * gradient
    square_new = beta_second * square_old + (1.0 - beta_second) * gradient * gradient
    mean_hat = mean_new / (1.0 - beta_first**ADAM_STEP)
    square_hat = square_new / (1.0 - beta_second**ADAM_STEP)
    weight_new = weight - rate * (mean_hat / (jnp.sqrt(square_hat) + eps_adam) + decay * weight)
    return (weight_new, mean_new, square_new)


def local(
    tokens,
    cotangent,
    segments,
    w_qkv,
    w_out,
    w_fc,
    w_proj,
    vectors,
    mean_qkv,
    mean_out,
    mean_fc,
    mean_proj,
    mean_vectors,
    square_qkv,
    square_out,
    square_fc,
    square_proj,
    square_vectors,
):
    dp_size = lax.axis_size("dp")
    zero_size = lax.axis_size("zero")
    replicas = dp_size * zero_size
    vec_cols = jnp.pad(vectors.astype(jnp.bfloat16).T, ((0, 0), (0, LANE - vectors.shape[0])))
    first_mats = (w_qkv.astype(jnp.bfloat16), w_out.astype(jnp.bfloat16), w_fc.astype(jnp.bfloat16), vec_cols)
    first_all = lax.all_gather(jnp.concatenate(first_mats, axis=1), "zero", axis=0, tiled=True)
    first_all, proj_shard = lax.optimization_barrier((first_all, w_proj.astype(jnp.bfloat16)))
    proj_mat = lax.all_gather(proj_shard, "zero", axis=0, tiled=True)
    widths = [m.shape[1] for m in first_mats]
    qkv_mat, out_mat, fc_mat, vec_cols_all = jnp.split(
        first_all, [sum(widths[:k]) for k in range(1, len(widths))], axis=1
    )
    vec_rows = vec_cols_all[:, : vectors.shape[0]].T.astype(jnp.float32)
    block_out, input_grad, local_grads = block_pass(
        tokens, cotangent, segments, qkv_mat, out_mat, fc_mat, proj_mat, vec_rows
    )
    grad_vec_cols = jnp.pad(
        local_grads[4].astype(jnp.bfloat16).T, ((0, 0), (0, LANE - vectors.shape[0]))
    )
    joined = jnp.concatenate(
        (
            local_grads[0].astype(jnp.bfloat16),
            local_grads[1].astype(jnp.bfloat16),
            local_grads[2].astype(jnp.bfloat16),
            grad_vec_cols,
        ),
        axis=1,
    )
    scattered = lax.psum_scatter(joined, "zero", scatter_dimension=0, tiled=True)
    proj_scattered = lax.psum_scatter(
        local_grads[3].astype(jnp.bfloat16), "zero", scatter_dimension=0, tiled=True
    )
    (summed_proj,) = summed_over_dp((proj_scattered,), 1)
    (summed_joined,) = summed_over_dp((scattered,), 0)
    ends = [w_qkv.shape[1], w_qkv.shape[1] + w_out.shape[1], w_qkv.shape[1] + w_out.shape[1] + w_fc.shape[1]]
    g_qkv, g_out, g_fc, g_vec = jnp.split(summed_joined, ends, axis=1)
    summed = (
        g_qkv.astype(jnp.float32),
        g_out.astype(jnp.float32),
        g_fc.astype(jnp.float32),
        summed_proj.astype(jnp.float32),
        lax.dot_general(
            g_vec[:, : vectors.shape[0]],
            jnp.eye(g_vec.shape[0], dtype=jnp.bfloat16),
            (((0,), (0,)), ((), ())),
            preferred_element_type=jnp.float32,
        ),
    )
    grads = jax.tree.map(partial(jnp.multiply, 1.0 / replicas), summed)
    first = adam_step(w_qkv, grads[0], mean_qkv, square_qkv, rate_matrix, decay_matrix)
    second = adam_step(w_out, grads[1], mean_out, square_out, rate_matrix, decay_matrix)
    third = adam_step(w_fc, grads[2], mean_fc, square_fc, rate_matrix, decay_matrix)
    fourth = adam_step(w_proj, grads[3], mean_proj, square_proj, rate_matrix, decay_matrix)
    fifth = adam_step(vectors, grads[4], mean_vectors, square_vectors, rate_vector, 0.0)
    return (
        block_out,
        input_grad,
        grads[0],
        grads[1],
        grads[2],
        grads[3],
        grads[4],
        first[0],
        second[0],
        third[0],
        fourth[0],
        fifth[0],
        first[1],
        second[1],
        third[1],
        fourth[1],
        fifth[1],
        first[2],
        second[2],
        third[2],
        fourth[2],
        fifth[2],
    )


def solution(mesh):
    placed = (
        P(("dp", "zero"), None),
        P(("dp", "zero"), None),
        P(("dp", "zero"), None),
        P("zero", None),
        P("zero", None),
        P("zero", None),
        P("zero", None),
        P(None, "zero"),
        P("zero", None),
        P("zero", None),
        P("zero", None),
        P("zero", None),
        P(None, "zero"),
        P("zero", None),
        P("zero", None),
        P("zero", None),
        P("zero", None),
        P(None, "zero"),
    )
    return jax.shard_map(
        local,
        mesh=mesh,
        in_specs=placed,
        out_specs=(
            P(("dp", "zero"), None),
            P(("dp", "zero"), None),
            P("zero", None),
            P("zero", None),
            P("zero", None),
            P("zero", None),
            P(None, "zero"),
            P("zero", None),
            P("zero", None),
            P("zero", None),
            P("zero", None),
            P(None, "zero"),
            P("zero", None),
            P("zero", None),
            P("zero", None),
            P("zero", None),
            P(None, "zero"),
            P("zero", None),
            P("zero", None),
            P("zero", None),
            P("zero", None),
            P(None, "zero"),
        ),
        check_vma=False,
    )
```
